32 devices in a mesh: dp: 8 (over z, y), mp: 4 (over x, core).
Axes of the slice: x: 2, y: 2, z: 4, core: 2. Of those that a mesh axis runs over, the one named last changes fastest.
Arguments:
- tokens: bfloat16 [16, 1024, 1024], P(None, ('dp', 'mp')), may hold values from -6 to 6
- encoder: bfloat16 [16, 1024, 1024], P(None, ('dp', 'mp')), may hold values from -6 to 6
- cotangent: bfloat16 [16, 1024, 1024], P(None, ('dp', 'mp')), may hold values from -6 to 6
- lengths: int32 [16], replicated, may hold values from 1 to 1024, 8192 in all
- deal: int32 [16], replicated, may hold values from 0 to 15, each once
- attn_in: float32 [6, 1024, 1024], P(None, 'dp', 'mp'), may hold values from -0.16 to 0.16
- attn_out: float32 [2, 1024, 1024], P(None, 'mp', 'dp'), may hold values from -0.75 to 0.75
- ff_in: float32 [2, 1024, 2816], P(None, 'dp', 'mp'), may hold values from -0.1875 to 0.1875
- ff_out: float32 [2816, 1024], P('mp', 'dp'), may hold values from -0.109375 to 0.109375
- gains: float32 [3, 1024], P(None, 'dp'), may hold values from 0.5 to 1.5
- mom_attn_in: float32 [6, 1024, 1024], P(None, 'dp', 'mp'), may hold values from -6 to 6
- mom_attn_out: float32 [2, 1024, 1024], P(None, 'mp', 'dp'), may hold values from -6 to 6
- mom_ff_in: float32 [2, 1024, 2816], P(None, 'dp', 'mp'), may hold values from -6 to 6
- mom_ff_out: float32 [2816, 1024], P('mp', 'dp'), may hold values from -6 to 6
- mom_gains: float32 [3, 1024], P(None, 'dp'), may hold values from -6 to 6
- avg_attn_in: float32 [6, 1024, 1024], P(None, 'dp', 'mp'), may hold values from -0.1875 to 0.1875
- avg_attn_out: float32 [2, 1024, 1024], P(None, 'mp', 'dp'), may hold values from -0.75 to 0.75
- avg_ff_in: float32 [2, 1024, 2816], P(None, 'dp', 'mp'), may hold values from -0.1875 to 0.1875
- avg_ff_out: float32 [2816, 1024], P('mp', 'dp'), may hold values from -0.109375 to 0.109375
- avg_gains: float32 [3, 1024], P(None, 'dp'), may hold values from 0.5 to 1.5
Outputs:
- block_output: float32 [16, 1024, 1024], P(None, ('dp', 'mp'))
- grad_tokens: float32 [16, 1024, 1024], P(None, ('dp', 'mp'))
- grad_encoder: float32 [16, 1024, 1024], P(None, ('dp', 'mp'))
- grad_attn_in: float32 [6, 1024, 1024], P(None, 'dp', 'mp')
- moment_attn_in: float32 [6, 1024, 1024], P(None, 'dp', 'mp')
- average_attn_in: float32 [6, 1024, 1024], P(None, 'dp', 'mp')
- master_attn_in: float32 [6, 1024, 1024], P(None, 'dp', 'mp')
- grad_attn_out: float32 [2, 1024, 1024], P(None, 'mp', 'dp')
- moment_attn_out: float32 [2, 1024, 1024], P(None, 'mp', 'dp')
- average_attn_out: float32 [2, 1024, 1024], P(None, 'mp', 'dp')
- master_attn_out: float32 [2, 1024, 1024], P(None, 'mp', 'dp')
- grad_ff_in: float32 [2, 1024, 2816], P(None, 'dp', 'mp')
- moment_ff_in: float32 [2, 1024, 2816], P(None, 'dp', 'mp')
- average_ff_in: float32 [2, 1024, 2816], P(None, 'dp', 'mp')
- master_ff_in: float32 [2, 1024, 2816], P(None, 'dp', 'mp')
- grad_ff_out: float32 [2816, 1024], P('mp', 'dp')
- moment_ff_out: float32 [2816, 1024], P('mp', 'dp')
- average_ff_out: float32 [2816, 1024], P('mp', 'dp')
- master_ff_out: float32 [2816, 1024], P('mp', 'dp')
- grad_gains: float32 [3, 1024], P(None, 'dp')
- moment_gains: float32 [3, 1024], P(None, 'dp')
- average_gains: float32 [3, 1024], P(None, 'dp')
- master_gains: float32 [3, 1024], P(None, 'dp')
- head_maxima: float32 [16], P('mp')
- clip_factors: float32 [16], P('mp')
The draws below stay inside these ranges and needn't reach their ends.
Inputs may be any that keep to these rules, and one draw needn't show every extreme that they name: lengths[j] counts the real tokens of slot j; positions from lengths[j] on are padding. deal holds each slot once; slot j is micro-batch j % 2 of data index j // 2.
All inputs are finite; a program needn't handle non-finite values.
Results may differ from the reference program's by a relative error of at most 0.025.
The reference program's roundings to bfloat16 on the way count: a program that leaves them out, or rounds other values in their place, can miss the bound.
Values may be sent and summed in bfloat16 or wider, within the bound.
No kernel may reach another device: no remote copies, remote signals or barrier semaphores. Data moves between devices by JAX's collectives and lax.ppermute only.
A program may use at most 256 MiB of HBM per device.

```python
import math
import jax
import jax.numpy as jnp
import numpy as np
from jax import lax

D = 1024
HEADS = 16
DK = 64
FF = 2816
INNER = 1024
L = 1024
ENC = 1024
NSEQ = 16


entry_bound = 0.16


def draw_attn_in(key, part):
    key_scale, key_value = jax.random.split(key)
    head_scale = jnp.exp(jax.random.uniform(key_scale, (HEADS,), jnp.float32, 0.0, 1.0986123))
    base_value = jnp.clip(jax.random.normal(key_value, (6, D, INNER), jnp.float32), -5.0, 5.0)
    column_scale = jnp.repeat(head_scale, DK) * float(D * DK) ** (-0.5)
    query_rows = jnp.arange(6) % 3 == 0
    entry_scale = jnp.where(query_rows[:, None, None], column_scale[None, None, :], float(D) ** (-0.5))
    return jnp.clip(base_value * entry_scale, -entry_bound, entry_bound)


def steps_of(key, dims, cuts, low, top_value):
    factor_of, own = 1.0, jax.random.fold_in(key, 6)
    for dim, shards_of in cuts:
        steps = jnp.exp(jax.random.uniform(jax.random.fold_in(own, dim), (shards_of,), jnp.float32, low / len(cuts), top_value / len(cuts)))
        factor_of = factor_of * jnp.repeat(steps, dims[dim] // shards_of).reshape([-1 if axis == dim else 1 for axis in range(len(dims))])
    return factor_of


def profile(count, total, bound, skew):
    portions = [(1 << 20) // math.isqrt(rank ** skew) + 1 for rank in range(2, count + 1)]
    spare, given = total - bound - (count - 1), [1] * (count - 1)
    while spare > 0:
        candidates = [i for i in range(count - 1) if given[i] < bound]
        whole, left = sum([portions[i] for i in candidates]), spare
        for i in candidates:
            addition = min(bound - given[i], max(1, left * portions[i] // whole), spare)
            given[i] = given[i] + addition
            spare = spare - addition
    return np.array([bound] + given)


def ragged(stream_key, number_of, total, reach, lean):
    if number_of == 2:
        one = jax.random.randint(stream_key, (), max(1, total - reach), min(reach, total - 1) + 1)
        return jnp.stack([one, total - one])
    sizes = jnp.asarray(profile(number_of, total, reach, lean), jnp.int32)
    couples = (number_of - 1) // 2
    giver, taker = sizes[1:1 + 2 * couples:2], sizes[2:2 + 2 * couples:2]
    margin = jnp.minimum(giver - 1, reach - taker)
    shifted = jax.random.randint(jax.random.fold_in(stream_key, 1), (couples,), 0, 1 << 20) % (margin + 1)
    sizes = sizes.at[1:1 + 2 * couples:2].set(giver - shifted).at[2:2 + 2 * couples:2].set(taker + shifted)
    return sizes[jax.random.permutation(jax.random.fold_in(stream_key, 2), number_of)]


def normal_values(key, dims, deviation, limit, shards=(), kind=jnp.bfloat16):
    level = steps_of(key, dims, shards, -0.22, 0.18) if shards else 1.0
    drawn = jax.random.normal(key, dims, jnp.float32) * deviation * level
    return jnp.minimum(jnp.maximum(drawn, -limit), limit).astype(kind)


def setup_inputs(seed: int = 0) -> dict:
    arg_keys = jax.random.split(jax.random.key(seed), 21)
    tokens = normal_values(arg_keys[0], (NSEQ, L, D), 1.0, 6.0, ((1, 32),))
    encoder = normal_values(arg_keys[1], (NSEQ, ENC, D), 1.0, 6.0, ((1, 32),))
    cotangent = normal_values(arg_keys[2], (NSEQ, L, D), 1.0, 6.0, ((1, 32),))
    lengths = ragged(arg_keys[3], NSEQ, NSEQ * L // 2, L, 1).astype(jnp.int32)
    deal = jax.random.permutation(arg_keys[4], NSEQ).astype(jnp.int32)
    attn_in = draw_attn_in(jax.random.fold_in(arg_keys[20], 71), 0)
    attn_out = normal_values(arg_keys[6], (2, INNER, D), (INNER // 16) ** -0.5, 0.75, ((1, 4), (2, 8)), jnp.float32)
    ff_in = normal_values(arg_keys[7], (2, D, FF), D ** -0.5, 0.1875, ((1, 8), (2, 4)), jnp.float32)
    ff_out = normal_values(arg_keys[8], (FF, D), FF ** -0.5, 0.109375, ((0, 4), (1, 8)), jnp.float32)
    gains = jnp.clip(1.0 + 0.1 * jax.random.normal(arg_keys[9], (3, D), jnp.float32), 0.5, 1.5)
    mom_attn_in = normal_values(arg_keys[10], (6, D, INNER), 0.5, 6.0, ((1, 8), (2, 4)), jnp.float32)
    mom_attn_out = normal_values(arg_keys[11], (2, INNER, D), 0.5, 6.0, ((1, 4), (2, 8)), jnp.float32)
    mom_ff_in = normal_values(arg_keys[12], (2, D, FF), 0.5, 6.0, ((1, 8), (2, 4)), jnp.float32)
    mom_ff_out = normal_values(arg_keys[13], (FF, D), 0.5, 6.0, ((0, 4), (1, 8)), jnp.float32)
    mom_gains = normal_values(arg_keys[14], (3, D), 1.0, 6.0, ((1, 8),), jnp.float32)
    avg_attn_in = normal_values(arg_keys[15], (6, D, INNER), D ** -0.5, 0.1875, ((1, 8), (2, 4)), jnp.float32)
    avg_attn_out = normal_values(arg_keys[16], (2, INNER, D), (INNER // 16) ** -0.5, 0.75, ((1, 4), (2, 8)), jnp.float32)
    avg_ff_in = normal_values(arg_keys[17], (2, D, FF), D ** -0.5, 0.1875, ((1, 8), (2, 4)), jnp.float32)
    avg_ff_out = normal_values(arg_keys[18], (FF, D), FF ** -0.5, 0.109375, ((0, 4), (1, 8)), jnp.float32)
    avg_gains = jnp.clip(0.5 + 1.0 * jax.random.uniform(arg_keys[19], (3, D), jnp.float32) ** steps_of(arg_keys[19], (3, D), ((1, 8),), -0.2, 0.2), 0.5, 1.5)
    return dict(tokens=tokens, encoder=encoder, cotangent=cotangent, lengths=lengths, deal=deal, attn_in=attn_in, attn_out=attn_out, ff_in=ff_in, ff_out=ff_out, gains=gains, mom_attn_in=mom_attn_in, mom_attn_out=mom_attn_out, mom_ff_in=mom_ff_in, mom_ff_out=mom_ff_out, mom_gains=mom_gains, avg_attn_in=avg_attn_in, avg_attn_out=avg_attn_out, avg_ff_in=avg_ff_in, avg_ff_out=avg_ff_out, avg_gains=avg_gains)


@jax.custom_vjp
def low(v):
    return lax.optimization_barrier(v.astype(jnp.bfloat16)).astype(jnp.float32)

@jax.custom_vjp
def low_back(v):
    return v

def low_keep(v):
    return (low(v), None)

def low_pass(kept, grad):
    return (grad,)

def back_keep(v):
    return (v, None)

def back_low(kept, grad):
    return (low(grad),)
low.defvjp(low_keep, low_pass)
low_back.defvjp(back_keep, back_low)
epsilon = 1e-06
clip_limit = 10.0
momentum_rate = 0.9
learn_rate = 0.01
average_rate = 0.5
neg_large = -1e+30
highest = lax.Precision.HIGHEST

def rms_norm(hidden, gain_vec):
    row_scale = lax.rsqrt(lax.optimization_barrier(jnp.mean(hidden * hidden, axis=-1, keepdims=True)) + epsilon)
    return hidden * row_scale * gain_vec

def softmax_rows(scores, allowed):
    masked = jnp.where(allowed, scores, neg_large)
    row_top = lax.optimization_barrier(jnp.max(masked, axis=-1, keepdims=True))
    expo_rows = jnp.exp(masked - row_top)
    return (expo_rows / lax.optimization_barrier(jnp.sum(expo_rows, axis=-1, keepdims=True)), row_top)

def attention(query_rows, key_rows, value_rows, allowed):
    query_h = query_rows.reshape(query_rows.shape[0], HEADS, DK)
    keys_h = key_rows.reshape(key_rows.shape[0], HEADS, DK)
    values_h = value_rows.reshape(value_rows.shape[0], HEADS, DK)
    scores = low_back(jnp.einsum('qhe,khe->hqk', query_h, keys_h, precision=highest))
    soft_rows, row_top = softmax_rows(scores, allowed)
    mixed = jnp.einsum('hqk,khe->qhe', low(soft_rows), values_h, precision=highest)
    return (low_back(low(mixed.reshape(query_rows.shape[0], INNER))), row_top)

def block_layer(tok_rows, enc_rows, attn_in, attn_out, ff_in, ff_out, gains, length):
    positions = jnp.arange(L)
    valid_rows = positions < length
    allowed = positions[None, :] <= positions[:, None]
    w_in = low(attn_in)
    w_out = low(attn_out)
    f_in = low(ff_in)
    f_out = low(ff_out)
    gain_low = low(gains)
    norm_one = low(rms_norm(tok_rows, gain_low[0]))
    proj_qkv = low_back(low(jnp.einsum('ld,cde->cle', norm_one, w_in[0:3], precision=highest)))
    self_mixed, self_top = attention(proj_qkv[0], proj_qkv[1], proj_qkv[2], allowed)
    head_top = lax.optimization_barrier(jnp.max(jnp.where(valid_rows[None, :, None], self_top, neg_large), axis=(1, 2)))
    hidden_one = tok_rows + low_back(jnp.dot(self_mixed, w_out[0], precision=highest))
    norm_two = low(rms_norm(hidden_one, gain_low[1]))
    cross_q = low_back(low(jnp.dot(norm_two, w_in[3], precision=highest)))
    cross_kv = low_back(low(jnp.einsum('ed,cdf->cef', enc_rows, w_in[4:6], precision=highest)))
    cross_mixed, cross_top = attention(cross_q, cross_kv[0], cross_kv[1], True)
    hidden_two = hidden_one + low_back(jnp.dot(cross_mixed, w_out[1], precision=highest))
    norm_three = low(rms_norm(hidden_two, gain_low[2]))
    gate_up = low_back(jnp.einsum('ld,cdf->clf', norm_three, f_in, precision=highest))
    inner_act = low(jax.nn.gelu(gate_up[0], approximate=True) * gate_up[1])
    result = hidden_two + low_back(jnp.dot(inner_act, f_out, precision=highest))
    return (result * valid_rows[:, None].astype(jnp.float32), head_top)

def apply_update(weight, grad_sum, moment, average, factor, grad_scale):
    grad_now = grad_sum * grad_scale
    moment_new = momentum_rate * moment + grad_now
    master_new = (weight - learn_rate * (grad_now + momentum_rate * moment_new)) * factor
    average_new = average_rate * average + (1.0 - average_rate) * master_new
    return (grad_now, moment_new, average_new, master_new)

def reference(tokens, encoder, cotangent, lengths, deal, attn_in, attn_out, ff_in, ff_out, gains, mom_attn_in, mom_attn_out, mom_ff_in, mom_ff_out, mom_gains, avg_attn_in, avg_attn_out, avg_ff_in, avg_ff_out, avg_gains):
    seq_lengths = jnp.take(lengths, deal, axis=0)

    def sequence_step(step_carry, step_items):
        totals, head_max = step_carry
        tok_rows, enc_rows, cot_rows, length = step_items

        def closed(tok_in, enc_in, weight_a, weight_b, weight_c, weight_d, weight_e):
            return block_layer(tok_in, enc_in, weight_a, weight_b, weight_c, weight_d, weight_e, length)
        result, back_fn, head_top = jax.vjp(closed, tok_rows.astype(jnp.float32), enc_rows.astype(jnp.float32), attn_in, attn_out, ff_in, ff_out, gains, has_aux=True)
        grads = back_fn(cot_rows.astype(jnp.float32))
        new_totals = (totals[0] + grads[2], totals[1] + grads[3], totals[2] + grads[4], totals[3] + grads[5], totals[4] + grads[6])
        return ((new_totals, jnp.maximum(head_max, head_top)), (result, grads[0], grads[1]))
    start = ((jnp.zeros_like(attn_in), jnp.zeros_like(attn_out), jnp.zeros_like(ff_in), jnp.zeros_like(ff_out), jnp.zeros_like(gains)), jnp.full((HEADS,), neg_large, jnp.float32))
    (totals, head_max), (block_output, grad_tokens, grad_encoder) = lax.scan(sequence_step, start, (tokens, encoder, cotangent, seq_lengths))
    grad_scale = float(NSEQ * L) ** (-0.5)
    clip_factors = clip_limit / jnp.maximum(head_max, clip_limit)
    column = jnp.repeat(jnp.sqrt(clip_factors), DK)
    factor = jnp.where((jnp.arange(6) < 2)[:, None, None], column[None, None, :], 1.0)
    up_a = apply_update(attn_in, totals[0], mom_attn_in, avg_attn_in, factor, grad_scale)
    up_b = apply_update(attn_out, totals[1], mom_attn_out, avg_attn_out, 1.0, grad_scale)
    up_c = apply_update(ff_in, totals[2], mom_ff_in, avg_ff_in, 1.0, grad_scale)
    up_d = apply_update(ff_out, totals[3], mom_ff_out, avg_ff_out, 1.0, grad_scale)
    up_e = apply_update(gains, totals[4], mom_gains, avg_gains, 1.0, grad_scale)
    return (block_output, grad_tokens, grad_encoder, up_a[0], up_a[1], up_a[2], up_a[3], up_b[0], up_b[1], up_b[2], up_b[3], up_c[0], up_c[1], up_c[2], up_c[3], up_d[0], up_d[1], up_d[2], up_d[3], up_e[0], up_e[1], up_e[2], up_e[3], head_max, clip_factors)
```

```python
import jax
import jax.numpy as jnp
from jax import lax
from jax.sharding import Mesh, PartitionSpec as P

D = 1024
DK = 64

epsilon = 1e-06
clip_limit = 10.0
momentum_rate = 0.9
learn_rate = 0.01
average_rate = 0.5
neg_large = -1e30
bf16 = jnp.bfloat16
f32 = jnp.float32
swap = ((0, 1), (1, 0))
chips = ("dp", "mx")


def rms_norm(hidden, gain_vec):
    row_scale = lax.rsqrt(jnp.mean(hidden * hidden, axis=-1, keepdims=True) + epsilon)
    return hidden * row_scale * gain_vec


def gelu_product(gate_part, up_part):
    return jax.nn.gelu(gate_part, approximate=True) * up_part


def nn(left, right):
    return lax.dot_general(left, right, (((1,), (0,)), ((), ())), preferred_element_type=f32)


def nt(left, right):
    return lax.dot_general(left, right, (((1,), (1,)), ((), ())), preferred_element_type=f32)


def tn(left, right):
    return lax.dot_general(left, right, (((0,), (0,)), ((), ())), preferred_element_type=f32)


def both_cores(own):
    return jnp.concatenate([own, lax.ppermute(own, "mc", swap)], axis=0)


def sum_cores(parts):
    own, other = parts
    return own + lax.ppermute(other, "mc", swap)


def split_heads(values):
    return values.reshape(values.shape[0], values.shape[1] // DK, DK)


def attend(query, keys, values, allowed):
    query_h, keys_h, values_h = split_heads(query), split_heads(keys), split_heads(values)
    scores = jnp.einsum("qhe,khe->hqk", query_h, keys_h, preferred_element_type=f32)
    masked = jnp.where(allowed, scores, neg_large)
    row_top = jnp.max(masked, axis=-1, keepdims=True)
    expo_rows = jnp.exp(masked - row_top)
    row_total = jnp.sum(expo_rows, axis=-1, keepdims=True)
    soft_rows = expo_rows / row_total
    mixed = jnp.einsum("hqk,khe->qhe", soft_rows.astype(bf16), values_h, preferred_element_type=f32)
    return (mixed.reshape(query.shape).astype(bf16), row_top + jnp.log(row_total), row_top)


def attend_back(query, keys, values, allowed, log_total, grad_mixed):
    query_h, keys_h, values_h = split_heads(query), split_heads(keys), split_heads(values)
    grad_h = split_heads(grad_mixed)
    scores = jnp.einsum("qhe,khe->hqk", query_h, keys_h, preferred_element_type=f32)
    soft_rows = jnp.exp(jnp.where(allowed, scores, neg_large) - log_total)
    grad_soft = jnp.einsum("qhe,khe->hqk", grad_h, values_h, preferred_element_type=f32)
    grad_values = jnp.einsum("hqk,qhe->khe", soft_rows.astype(bf16), grad_h, preferred_element_type=f32)
    row_dot = jnp.sum(grad_soft * soft_rows, axis=-1, keepdims=True)
    grad_scores = (soft_rows * (grad_soft - row_dot)).astype(bf16)
    grad_query = jnp.einsum("hqk,khe->qhe", grad_scores, keys_h, preferred_element_type=f32)
    grad_keys = jnp.einsum("hqk,qhe->khe", grad_scores, query_h, preferred_element_type=f32)
    return tuple(t.reshape(t.shape[0], -1).astype(bf16) for t in (grad_query, grad_keys, grad_values))


def norm_back(hidden, gain_vec, grad):
    row_scale = lax.rsqrt(jnp.mean(hidden * hidden, axis=-1, keepdims=True) + epsilon)
    z = hidden * row_scale
    grad_z = grad * gain_vec
    grad_hidden = row_scale * (grad_z - z * jnp.mean(grad_z * z, axis=-1, keepdims=True))
    return grad_hidden, jnp.sum(grad * z, axis=0)


def apply_update(weight, grad_sum, moment, average, factor, grad_scale):
    grad_now = grad_sum * grad_scale
    moment_new = momentum_rate * moment + grad_now
    master_new = (weight - learn_rate * (grad_now + momentum_rate * moment_new)) * factor
    average_new = average_rate * average + (1.0 - average_rate) * master_new
    return (grad_now, moment_new, average_new, master_new)


def flat_columns(block):
    return jnp.swapaxes(block, 0, 1).reshape(block.shape[1], -1)


def gather_chunk(local):
    own = lax.all_gather(local, "dp", axis=0, tiled=True)
    return own, lax.ppermute(own, "mx", swap)


def reduce_chunk(own, other):
    arrived = lax.ppermute(other.astype(bf16), "mx", swap)
    total = (own + arrived.astype(f32)).astype(bf16)
    return lax.psum_scatter(total, "dp", scatter_dimension=0, tiled=True).astype(f32)


def on_device(
    tokens,
    encoder,
    cotangent,
    lengths,
    deal,
    attn_in,
    attn_out,
    ff_in,
    ff_out,
    gains,
    mom_attn_in,
    mom_attn_out,
    mom_ff_in,
    mom_ff_out,
    mom_gains,
    avg_attn_in,
    avg_attn_out,
    avg_ff_in,
    avg_ff_out,
    avg_gains,
):
    seq_count, block_rows = tokens.shape[0], tokens.shape[1]
    core = lax.axis_index("mc")
    chip = lax.axis_index("dp") * lax.axis_size("mx") + lax.axis_index("mx")
    own_rows = block_rows * seq_count
    slot_len = 2 * own_rows
    heads_cols = attn_in.shape[2]
    hidden = ff_in.shape[2]
    model_rows = attn_in.shape[1]

    def to_chips(values):
        moved = lax.all_to_all(values, chips, split_axis=0, concat_axis=1, tiled=True)
        return moved.reshape(own_rows, D)

    def from_chips(rows):
        return lax.all_to_all(
            rows.reshape(1, own_rows, D), chips, split_axis=1, concat_axis=0, tiled=True
        ).astype(f32)

    seq_len = lengths[deal[chip]]
    row_ids = jnp.arange(own_rows, dtype=jnp.int32)
    lane = row_ids % block_rows
    pos_own = (row_ids // block_rows * 2 + core) * block_rows + lane
    pos_other = (row_ids // block_rows * 2 + 1 - core) * block_rows + lane
    pos = jnp.concatenate([pos_own, pos_other])
    allowed = pos[None, :] <= pos[:, None]
    valid_own = (pos_own < seq_len).astype(f32)[:, None]
    valid_all = pos < seq_len

    pad = jnp.zeros((model_rows, 125), bf16)
    chunk_a = jnp.concatenate(
        [flat_columns(attn_in[0:3].astype(bf16)), gains.astype(bf16).T, pad], axis=1
    )
    out_t = jnp.swapaxes(attn_out.astype(bf16), 1, 2)
    chunk_b = jnp.concatenate([out_t[0], flat_columns(attn_in[3:6].astype(bf16)), out_t[1]], axis=1)
    chunk_c = flat_columns(ff_in.astype(bf16))
    chunk_d = ff_out.astype(bf16).T

    tok_own = to_chips(tokens)
    got_a = gather_chunk(chunk_a)
    enc_own = to_chips(encoder)
    got_b = gather_chunk(chunk_b)
    cot_own = to_chips(cotangent)
    got_c = gather_chunk(chunk_c)
    got_d = gather_chunk(chunk_d)
    gain_f = got_a[0][:, 3 * heads_cols : 3 * heads_cols + 3].astype(f32).T

    hc = heads_cols
    w_qkv = [g[:, : 3 * hc] for g in got_a]
    w_ot = [g[:, :hc] for g in got_b]
    w_cq = [g[:, hc : 2 * hc] for g in got_b]
    w_ckv = [g[:, 2 * hc : 4 * hc] for g in got_b]
    w_cot = [g[:, 4 * hc :] for g in got_b]
    w_gu = got_c
    w_dt = got_d

    halves = lambda v: (v[:own_rows], v[own_rows:])
    x_rows = tok_own.astype(f32)
    norm_one = both_cores(rms_norm(x_rows, gain_f[0]).astype(bf16))
    qkv = [nn(norm_one, w).astype(bf16) for w in w_qkv]
    qkv = [(t[:, :hc], t[:, hc : 2 * hc], t[:, 2 * hc :]) for t in qkv]
    self_out = [attend(q, k, v, allowed) for q, k, v in qkv]
    head_top = jnp.stack(
        [jnp.max(jnp.where(valid_all[None, :, None], o[2], neg_large), axis=(1, 2)) for o in self_out]
    )
    branch = nt(self_out[0][0], w_ot[0]) + nt(self_out[1][0], w_ot[1])
    hidden_one = x_rows + sum_cores(halves(branch))
    norm_two = both_cores(rms_norm(hidden_one, gain_f[1]).astype(bf16))
    enc_all = both_cores(enc_own)
    cross_q = [nn(norm_two, w).astype(bf16) for w in w_cq]
    cross_kv = [nn(enc_all, w).astype(bf16) for w in w_ckv]
    cross_kv = [(t[:, :hc], t[:, hc:]) for t in cross_kv]
    cross_out = [attend(q, k, v, True) for q, (k, v) in zip(cross_q, cross_kv)]
    branch = nt(cross_out[0][0], w_cot[0]) + nt(cross_out[1][0], w_cot[1])
    hidden_two = hidden_one + sum_cores(halves(branch))
    norm_three = both_cores(rms_norm(hidden_two, gain_f[2]).astype(bf16))
    gate_up = [nn(norm_three, w) for w in w_gu]
    gate_up = [(t[:, :hidden], t[:, hidden:]) for t in gate_up]
    inner = [gelu_product(g, u).astype(bf16) for g, u in gate_up]
    branch = nt(inner[0], w_dt[0]) + nt(inner[1], w_dt[1])
    out_rows = (hidden_two + sum_cores(halves(branch))) * valid_own
    block_output = from_chips(out_rows.astype(bf16))

    grad_out = cot_own.astype(f32) * valid_own
    grad_out_all = both_cores(grad_out.astype(bf16))
    g_dt = [tn(grad_out_all, f) for f in inner]
    red_d = reduce_chunk(*g_dt)
    grad_gu = []
    for (g, u), w in zip(gate_up, w_dt):
        _, back = jax.vjp(gelu_product, g, u)
        dg, du = back(nn(grad_out_all, w))
        grad_gu.append(jnp.concatenate([dg.astype(bf16), du.astype(bf16)], axis=1))
    g_gu = [tn(norm_three, t) for t in grad_gu]
    red_c = reduce_chunk(*g_gu)
    grad_norm = sum_cores(halves(nt(grad_gu[0], w_gu[0]) + nt(grad_gu[1], w_gu[1])))
    grad_h, gain_three = norm_back(hidden_two, gain_f[2], grad_norm)
    grad_hidden_two = grad_out + grad_h
    grad_co = both_cores(grad_hidden_two.astype(bf16))
    g_cot = [tn(grad_co, o[0]) for o in cross_out]
    grad_ca = [nn(grad_co, w).astype(bf16) for w in w_cot]
    cross_back = [
        attend_back(q, k, v, True, o[1], d)
        for q, (k, v), o, d in zip(cross_q, cross_kv, cross_out, grad_ca)
    ]
    g_cq = [tn(norm_two, b[0]) for b in cross_back]
    d_ckv = [jnp.concatenate([b[1], b[2]], axis=1) for b in cross_back]
    g_ckv = [tn(enc_all, t) for t in d_ckv]
    red_b = reduce_chunk(*[jnp.concatenate(t, axis=1) for t in zip(g_cq, g_ckv, g_cot)])
    grad_norm = sum_cores(halves(nt(cross_back[0][0], w_cq[0]) + nt(cross_back[1][0], w_cq[1])))
    grad_enc = sum_cores(halves(nt(d_ckv[0], w_ckv[0]) + nt(d_ckv[1], w_ckv[1])))
    grad_encoder = from_chips(grad_enc.astype(bf16))
    grad_h, gain_two = norm_back(hidden_one, gain_f[1], grad_norm)
    grad_hidden_one = grad_hidden_two + grad_h
    grad_o = both_cores(grad_hidden_one.astype(bf16))
    g_ot = [tn(grad_o, o[0]) for o in self_out]
    grad_a = [nn(grad_o, w).astype(bf16) for w in w_ot]
    self_back = [
        jnp.concatenate(attend_back(q, k, v, allowed, o[1], d), axis=1)
        for (q, k, v), o, d in zip(qkv, self_out, grad_a)
    ]
    g_qkv = [tn(norm_one, t) for t in self_back]
    red_a = reduce_chunk(*[jnp.concatenate(t, axis=1) for t in zip(g_qkv, g_ot)])
    grad_norm = sum_cores(halves(nt(self_back[0], w_qkv[0]) + nt(self_back[1], w_qkv[1])))
    grad_h, gain_one = norm_back(x_rows, gain_f[0], grad_norm)
    grad_tokens = from_chips((grad_hidden_one + grad_h).astype(bf16))

    gain_total = lax.psum(jnp.stack([gain_one, gain_two, gain_three]), ("mx", "mc"))
    red_gain = lax.psum_scatter(gain_total, "dp", scatter_dimension=1, tiled=True)
    mx = lax.axis_index("mx")
    local_heads = hc // DK
    head_rows = jnp.where(mx == 0, head_top, head_top[::-1])
    head_peak = lax.dynamic_index_in_dim(lax.pmax(head_rows, chips), mx, 0, keepdims=False)

    unflat = lambda t, n: jnp.swapaxes(t.reshape(model_rows, n, -1), 0, 1)
    red_in = jnp.concatenate([unflat(red_a[:, : 3 * hc], 3), unflat(red_b[:, : 3 * hc], 3)])
    red_out = jnp.stack([red_a[:, 3 * hc :].T, red_b[:, 3 * hc :].T])
    clip_factors = clip_limit / jnp.maximum(head_peak, clip_limit)
    column = jnp.repeat(jnp.sqrt(clip_factors), DK)
    factor = jnp.where((jnp.arange(6) < 2)[:, None, None], column[None, None, :], 1.0)
    grad_scale = float(seq_count * slot_len) ** (-0.5)
    up_a = apply_update(attn_in, red_in, mom_attn_in, avg_attn_in, factor, grad_scale)
    up_b = apply_update(attn_out, red_out, mom_attn_out, avg_attn_out, 1.0, grad_scale)
    up_c = apply_update(ff_in, unflat(red_c, 2), mom_ff_in, avg_ff_in, 1.0, grad_scale)
    up_d = apply_update(ff_out, red_d.T, mom_ff_out, avg_ff_out, 1.0, grad_scale)
    up_e = apply_update(gains, red_gain, mom_gains, avg_gains, 1.0, grad_scale)
    return (
        block_output,
        grad_tokens,
        grad_encoder,
        *up_a,
        *up_b,
        *up_c,
        *up_d,
        *up_e,
        head_peak,
        clip_factors,
    )


def solution(mesh):
    dp, mp = mesh.shape["dp"], mesh.shape["mp"]
    fine = Mesh(mesh.devices.reshape(dp, mp // 2, 2), ("dp", "mx", "mc"))
    mp_axes = ("mx", "mc")
    rows = P(None, ("dp", "mx", "mc"), None)
    wide = P(None, "dp", mp_axes)
    tall = P(None, mp_axes, "dp")
    down = P(mp_axes, "dp")
    gain = P(None, "dp")
    state = (wide, tall, wide, down, gain)
    in_specs = (rows, rows, rows, P(), P(), *state, *state, *state)
    out_specs = (
        rows,
        rows,
        rows,
        *[wide] * 4,
        *[tall] * 4,
        *[wide] * 4,
        *[down] * 4,
        *[gain] * 4,
        P(mp_axes),
        P(mp_axes),
    )
    return jax.shard_map(
        on_device, mesh=fine, in_specs=in_specs, out_specs=out_specs, check_vma=False
    )
```

```python
import functools

import jax
import jax.numpy as jnp
from jax import lax
from jax.experimental import pallas as pl
from jax.experimental.layout import Layout, with_layout_constraint
from jax.experimental.pallas import tpu as pltpu
from jax.sharding import Mesh, PartitionSpec as P

D = 1024
DK = 64

epsilon = 1e-06
clip_limit = 10.0
momentum_rate = 0.9
learn_rate = 0.01
average_rate = 0.5
neg_large = -1e30
tanh_rate = 0.7978845608
tanh_cube = 0.044715
bf16 = jnp.bfloat16
f32 = jnp.float32
swap = ((0, 1), (1, 0))
chips = ("dz", "dy", "mx")


def dot(left, right, dims):
    return lax.dot_general(left, right, (dims, ((), ())), preferred_element_type=f32)


def head_lanes(block, head):
    lanes = lax.broadcasted_iota(jnp.int32, block.shape, 1)
    return jnp.where((lanes >= DK) == (head == 1), block, jnp.zeros_like(block))


def key_spans(rows, keys, start, size, causal):
    half = rows // 2
    reach = start % half + size
    return [(0, reach), (half, half + reach)] if causal and reach < half else [(0, keys)]


def total(parts):
    return functools.reduce(jnp.add, parts)


def attend_kernel(causal, size, q_ref, k_ref, v_ref, pq_ref, pk_ref, len_ref, o_ref, lse_ref, top_ref):
    rows, keys = q_ref.shape[0], k_ref.shape[0]
    tops = []
    for head in range(2):
        k, v = head_lanes(k_ref[...], head), head_lanes(v_ref[...], head)
        top = jnp.full((1, 1), neg_large, f32)
        for start in range(0, rows, size):
            r = slice(start, start + size)
            spans = key_spans(rows, keys, start, size, causal)
            q = q_ref[r, :]
            s = [dot(q, k[a:b], ((1,), (1,))) for a, b in spans]
            if causal:
                s = [jnp.where(pk_ref[:, a:b] <= pq_ref[r, :], t, neg_large) for t, (a, b) in zip(s, spans)]
            m = functools.reduce(jnp.maximum, [jnp.max(t, axis=1, keepdims=True) for t in s])
            if causal:
                real = jnp.where(pq_ref[r, :] < len_ref[0], m, neg_large)
                top = jnp.maximum(top, jnp.max(real, axis=0, keepdims=True))
            e = [jnp.exp(t - m) for t in s]
            mass = total([jnp.sum(t, axis=1, keepdims=True) for t in e])
            scale = 1.0 / mass
            mix = total([dot((t * scale).astype(bf16), v[a:b], ((1,), (0,))) for t, (a, b) in zip(e, spans)])
            if head == 0:
                o_ref[r, :] = mix.astype(bf16)
            else:
                o_ref[r, :] = (o_ref[r, :].astype(f32) + mix).astype(bf16)
            lse_ref[0, r, head : head + 1] = m + jnp.log(mass)
        tops.append(top)
    lanes = lax.broadcasted_iota(jnp.int32, (8, 128), 1)
    top_ref[0] = jnp.where(lanes == 0, tops[0], tops[1])


def attend_back_kernel(
    causal, size, q_ref, k_ref, v_ref, pq_ref, pk_ref, lse_ref, do_ref, dq_ref, dk_ref, dv_ref, dk_acc, dv_acc
):
    rows, keys = q_ref.shape[0], k_ref.shape[0]
    dk_acc[...] = jnp.zeros_like(dk_acc)
    dv_acc[...] = jnp.zeros_like(dv_acc)
    for head in range(2):
        k, v = head_lanes(k_ref[...], head), head_lanes(v_ref[...], head)
        own = slice(DK * head, DK * head + DK)
        for start in range(0, rows, size):
            r = slice(start, start + size)
            spans = key_spans(rows, keys, start, size, causal)
            q, do, lse = q_ref[r, :], do_ref[r, :], lse_ref[0, r, head : head + 1]
            soft, grad = [], []
            for a, b in spans:
                s = dot(q, k[a:b], ((1,), (1,)))
                if causal:
                    s = jnp.where(pk_ref[:, a:b] <= pq_ref[r, :], s, neg_large)
                soft.append(jnp.exp(s - lse))
                grad.append(dot(do, v[a:b], ((1,), (1,))))
            row_dot = total([jnp.sum(p * t, axis=1, keepdims=True) for p, t in zip(soft, grad)])
            q_t, do_t = q.T[own], do.T[own]
            parts = []
            for (a, b), p, t in zip(spans, soft, grad):
                ds = (p * (t - row_dot)).astype(bf16)
                parts.append(dot(ds, k[a:b], ((1,), (0,))))
                dv_acc[own, a:b] += dot(do_t, p.astype(bf16), ((1,), (0,)))
                dk_acc[own, a:b] += dot(q_t, ds, ((1,), (0,)))
            dq = total(parts)
            if head == 0:
                dq_ref[r, :] = dq.astype(bf16)
            else:
                dq_ref[r, :] = (dq_ref[r, :].astype(f32) + dq).astype(bf16)
    dk_ref[...] = dk_acc[...].T.astype(bf16)
    dv_ref[...] = dv_acc[...].T.astype(bf16)


def attend_cost(rows, keys, pairs, dots):
    return cost(0, 0)


def lane_pairs(count, first):
    return pl.BlockSpec((count, 2 * DK), lambda p: (0, first + p))


def attend(q, k, v, pos_col, pos_row, length, causal, size):
    rows, keys, pairs = q[0].shape[0], k[0].shape[0], q[2]
    mixed, lse, top = pl.pallas_call(
        functools.partial(attend_kernel, causal, size),
        grid=(pairs,),
        in_specs=[
            lane_pairs(rows, q[1]),
            lane_pairs(keys, k[1]),
            lane_pairs(keys, v[1]),
            pl.BlockSpec((rows, 1), lambda p: (0, 0)),
            pl.BlockSpec((1, keys), lambda p: (0, 0)),
            pl.BlockSpec(memory_space=pltpu.SMEM),
        ],
        out_specs=[
            lane_pairs(rows, 0),
            pl.BlockSpec((1, rows, 2), lambda p: (p, 0, 0)),
            pl.BlockSpec((1, 8, 128), lambda p: (p, 0, 0)),
        ],
        out_shape=[
            jax.ShapeDtypeStruct((rows, pairs * 2 * DK), bf16),
            jax.ShapeDtypeStruct((pairs, rows, 2), f32),
            jax.ShapeDtypeStruct((pairs, 8, 128), f32),
        ],
        cost_estimate=attend_cost(rows, keys, pairs, 2),
        name="attend",
    )(q[0], k[0], v[0], pos_col, pos_row, length)
    return mixed, lse, top[:, 0, :2].reshape(-1)


def attend_back(q, k, v, pos_col, pos_row, lse, grad, causal, size):
    rows, keys, pairs = q[0].shape[0], k[0].shape[0], q[2]
    return pl.pallas_call(
        functools.partial(attend_back_kernel, causal, size),
        grid=(pairs,),
        in_specs=[
            lane_pairs(rows, q[1]),
            lane_pairs(keys, k[1]),
            lane_pairs(keys, v[1]),
            pl.BlockSpec((rows, 1), lambda p: (0, 0)),
            pl.BlockSpec((1, keys), lambda p: (0, 0)),
            pl.BlockSpec((1, rows, 2), lambda p: (p, 0, 0)),
            lane_pairs(rows, 0),
        ],
        out_specs=[lane_pairs(rows, 0), lane_pairs(keys, 0), lane_pairs(keys, 0)],
        out_shape=[jax.ShapeDtypeStruct((n, pairs * 2 * DK), bf16) for n in (rows, keys, keys)],
        scratch_shapes=[pltpu.VMEM((2 * DK, keys), f32)] * 2,
        cost_estimate=attend_cost(rows, keys, pairs, 5),
        name="attend_back",
    )(q[0], k[0], v[0], pos_col, pos_row, lse, grad)


def apply_update(weight, grad_sum, moment, average, factor, grad_scale):
    grad_now = grad_sum * grad_scale
    moment_new = momentum_rate * moment + grad_now
    master_new = (weight - learn_rate * (grad_now + momentum_rate * moment_new)) * factor
    average_new = average_rate * average + (1.0 - average_rate) * master_new
    return (grad_now, moment_new, average_new, master_new)


def flat_columns(block):
    return jnp.swapaxes(block, 0, 1).reshape(block.shape[1], -1)


def row_major(values):
    return with_layout_constraint(values, Layout(major_to_minor=tuple(range(values.ndim))))


spec = pl.BlockSpec


def cost(flops, moved):
    return pl.CostEstimate(flops=1, bytes_accessed=1, transcendentals=0)


def reorder(parts, block, dy, to_own, keep=None):
    arrays = halves(parts)
    rows, width = arrays[0].shape[0], D
    steps = width // block // 2
    extra = [] if keep is None else [keep]
    if block % 128:
        value = total([(jnp.concatenate(p, axis=1) if isinstance(p, (list, tuple)) else p).astype(f32) for p in parts])
        value = value * (1.0 if keep is None else keep)
        axis = 2 if to_own else 1
        value = value.reshape((rows, steps, 2, block) if to_own else (rows, 2, steps, block))
        low, high = (lax.index_in_dim(value, n, axis, keepdims=False) for n in range(2))
        pair = jnp.where(dy == 0, low, high), jnp.where(dy == 0, high, low)
        return jnp.stack(pair, axis=3 - axis).reshape(rows, width).astype(bf16)

    def source(j, flag):
        if to_own:
            return j % steps * 2 + (j // steps + flag) % 2
        return j // 2 + (j % 2 + flag) % 2 * steps

    def kernel(flag_ref, *refs):
        out = refs[-1]
        whole = len(arrays) == 1
        value = refs[0] if whole else read_total(parts, refs[: len(arrays)])
        for j in range(2 * steps):
            spans = [slice(source(j, flag) * block, (source(j, flag) + 1) * block) for flag in range(2)]
            picked = jnp.where(flag_ref[0] == 0, value[:, spans[0]], value[:, spans[1]])
            if extra:
                picked = picked.astype(f32) * refs[len(arrays)][...]
            out[:, j * block : (j + 1) * block] = picked.astype(bf16)

    return pl.pallas_call(
        kernel,
        grid=(4,),
        in_specs=[
            spec(memory_space=pltpu.SMEM),
            *[by_rows(p, rows // 4) for p in [*arrays, *extra]],
        ],
        out_specs=spec((rows // 4, width), lambda i: (i, 0)),
        out_shape=jax.ShapeDtypeStruct((rows, width), bf16),
        cost_estimate=cost(0, rows * width * 4),
        name="reorder",
    )(dy[None], *arrays, *extra)


def weight_specs(weights):
    specs, arrays = [], []
    for own, other, width, place in weights:
        specs += [spec((own.shape[0], width), lambda i, place=place: (0, place))] * 2
        arrays += [own, other]
    return specs, arrays


def project(rows, weights, mode="plain", scales=()):
    own, other = rows
    half, size = own.shape[0], own.shape[0] // 2
    specs, arrays = weight_specs(weights)
    widths = [w[2] for w in weights]
    count = len(weights)
    out_widths = {"plain": widths, "gelu": widths[:1] * 3, "scale": [w for w in widths for _ in range(2)]}[mode]

    def kernel(own_ref, other_ref, *refs):
        here = pl.program_id(0) < 2
        x = jnp.where(here, own_ref[...], other_ref[...])
        split = x.shape[1] // 2
        made = []
        for j in range(count):
            low, high = refs[2 * j], refs[2 * j + 1]
            made.append(
                dot(x[:, :split], low[...], ((1,), (0,))) + dot(x[:, split:], high[...], ((1,), (0,)))
            )
        outs = refs[2 * count + len(scales) :]
        if mode == "plain":
            for out, value in zip(outs, made):
                out[...] = value.astype(bf16)
        elif mode == "gelu":
            gate, up = made
            square = gate * gate
            bend = jnp.tanh(tanh_rate * gate * (1.0 + tanh_cube * square))
            rise = 0.5 * (1.0 + bend)
            value = gate * rise
            slope = rise + 0.5 * gate * (1.0 - bend * bend) * tanh_rate * (1.0 + 3.0 * tanh_cube * square)
            outs[0][...] = (value * up).astype(bf16)
            outs[1][...] = (slope * up).astype(bf16)
            outs[2][...] = value.astype(bf16)
        else:
            for j, out in enumerate(outs):
                out[...] = (made[j // 2] * refs[2 * count + j][...].astype(f32)).astype(bf16)

    by_rows = lambda width: spec((size, width), lambda i: (i, 0))
    width_all = own.shape[1]
    return pl.pallas_call(
        kernel,
        grid=(4,),
        in_specs=[
            spec((size, width_all), lambda i: (jnp.minimum(i, 1), 0)),
            spec((size, width_all), lambda i: (jnp.maximum(i - 2, 0), 0)),
            *specs,
            *[by_rows(t.shape[1]) for t in scales],
        ],
        out_specs=[by_rows(w) for w in out_widths],
        out_shape=[jax.ShapeDtypeStruct((2 * half, w), bf16) for w in out_widths],
        cost_estimate=cost(4 * half * width_all * sum(widths), half * width_all * 4 + width_all * sum(widths) * 2),
        name="project_" + mode,
    )(own, other, *arrays, *scales)


def combine(values, weights, which):
    specs, arrays = weight_specs(weights)
    half = values[0].shape[0] // 2
    size = half // 2
    count = len(values)
    depth = weights[0][0].shape[0]

    def kernel(*refs):
        for side in range(2):
            parts = [
                dot(refs[j][...], refs[count + 2 * j + side][...], ((1,), (1,))) for j in range(count)
            ]
            refs[side - 2][...] = total(parts)

    return pl.pallas_call(
        kernel,
        grid=(2,),
        in_specs=[spec((size, v.shape[1]), lambda i: (2 * which + i, 0)) for v in values] + specs,
        out_specs=[spec((size, depth), lambda i: (i, 0))] * 2,
        out_shape=[jax.ShapeDtypeStruct((half, depth), f32)] * 2,
        cost_estimate=cost(0, 0),
        name="combine",
    )(*values, *arrays)


def weight_grad(items, part, arrived=()):
    sources = []
    for rows, _ in items:
        if not any(rows is t for t in sources):
            sources.append(rows)
    half, width = sources[0][0].shape
    size = width // 2
    steps, base = (2, 0) if part is None else (1, part)
    spans, last = [], 0
    for _, value in items:
        spans.append((last, last + value.shape[1]))
        last = spans[-1][1]
    first = len(sources) * 2

    def kernel(*refs):
        out = refs[-1]
        for (rows, _), value, (a, b) in zip(items, refs[first:], spans):
            place = [rows is t for t in sources].index(True)
            own, other = refs[2 * place], refs[2 * place + 1]
            made = dot(own[...], value[:half], ((0,), (0,))) + dot(other[...], value[half:], ((0,), (0,)))
            for (array, _, start), came in zip(arrived, refs[first + len(items) :]):
                if start <= a < start + array.shape[1]:
                    made = made + came[:, a - start : b - start].astype(f32)
            out[:, a:b] = made.astype(bf16)

    columns = spec((half, size), lambda i: (0, base + i))
    return pl.pallas_call(
        kernel,
        grid=(steps,),
        in_specs=[columns] * first
        + [spec(v.shape, lambda i: (0, 0)) for _, v in items]
        + [spec((size, a.shape[1]), lambda i, place=place: (place + i, 0)) for a, place, _ in arrived],
        out_specs=spec((size, last), lambda i: (i, 0)),
        out_shape=jax.ShapeDtypeStruct((steps * size, last), bf16),
        cost_estimate=cost(4 * half * steps * size * last, half * width * 4 + half * 4 * last),
        name="weight_grad",
    )(*[t for pair in sources for t in pair], *[v for _, v in items], *[a for a, _, _ in arrived])


def halves(parts):
    return [t for p in parts for t in (p if isinstance(p, (list, tuple)) else [p])]


def read_total(parts, refs):
    refs, read = list(refs), []
    for p in parts:
        if isinstance(p, (list, tuple)):
            read.append(jnp.concatenate([refs.pop(0)[...] for _ in p], axis=1))
        else:
            read.append(refs.pop(0)[...])
    return total([r.astype(f32) for r in read])


def by_rows(array, size=256):
    if array.shape[0] == 1:
        return spec(array.shape, lambda i: (0, 0))
    return spec((size, array.shape[1]), lambda i: (i, 0))


def add_norm(parts, gain_row):
    arrays = halves(parts)
    rows, width = arrays[0].shape[0], D

    def kernel(gain_ref, *refs):
        hidden = read_total(parts, refs[: len(arrays)])
        scale = lax.rsqrt(jnp.mean(hidden * hidden, axis=-1, keepdims=True) + epsilon)
        refs[-1][...] = (hidden * scale * gain_ref[...]).astype(bf16)
        if len(parts) > 1:
            refs[-2][...] = hidden

    kinds = [f32, bf16] if len(parts) > 1 else [bf16]
    shapes = [jax.ShapeDtypeStruct((rows, width), k) for k in kinds]
    return pl.pallas_call(
        kernel,
        grid=(rows // 256,),
        in_specs=[by_rows(gain_row), *[by_rows(p) for p in arrays]],
        out_specs=[by_rows(t) for t in shapes],
        out_shape=shapes,
        cost_estimate=cost(rows * width * 8, rows * width * 14),
        name="add_norm",
    )(gain_row, *arrays)


def norm_back(hidden, gain_row, grads, base):
    rows, width = hidden.shape
    arrays = halves(grads)

    def kernel(gain_ref, hidden_ref, base_ref, *refs):
        grad = read_total(grads, refs[: len(arrays)])
        out, low, gain_grad = refs[len(arrays) :]
        hidden = hidden_ref[...].astype(f32)
        scale = lax.rsqrt(jnp.mean(hidden * hidden, axis=-1, keepdims=True) + epsilon)
        z = hidden * scale
        grad_z = grad * gain_ref[...]
        grad_hidden = scale * (grad_z - z * jnp.mean(grad_z * z, axis=-1, keepdims=True))
        value = base_ref[...].astype(f32) + grad_hidden
        out[...] = value
        low[...] = value.astype(bf16)

        @pl.when(pl.program_id(0) == 0)
        def _():
            gain_grad[...] = jnp.zeros_like(gain_grad)

        gain_grad[...] += jnp.sum(grad * z, axis=0, keepdims=True)

    shapes = [jax.ShapeDtypeStruct((rows, width), f32), jax.ShapeDtypeStruct((rows, width), bf16)]
    return pl.pallas_call(
        kernel,
        grid=(rows // 256,),
        in_specs=[by_rows(gain_row), by_rows(hidden), by_rows(base), *[by_rows(g) for g in arrays]],
        out_specs=[*[by_rows(t) for t in shapes], spec((1, width), lambda i: (0, 0))],
        out_shape=[*shapes, jax.ShapeDtypeStruct((1, width), f32)],
        cost_estimate=cost(rows * width * 16, rows * width * 22),
        name="norm_back",
    )(gain_row, hidden, base, *arrays)


def after(value, *others):
    return lax.optimization_barrier((value, *others))[0]


def swap_cores(values):
    return lax.ppermute(values, "mc", swap)


def swap_x(values):
    return row_major(lax.ppermute(row_major(values), "mx", swap))


def swap_y(values):
    return row_major(lax.ppermute(row_major(values), "dy", swap))


def gather_part(local):
    return row_major(lax.all_gather(row_major(local), "dz", axis=0, tiled=True))


def spread(part, x_last):
    if x_last:
        high = swap_y(part)
        return (part, high), (swap_x(part), swap_x(high))
    beside = swap_x(part)
    return (part, swap_y(part)), (beside, swap_y(beside))


class Group:
    def __init__(self, x_items, y_items):
        self.own = [(r, v) for r, v, _ in (*x_items, *y_items)]
        self.own_x, self.own_y = self.own[: len(x_items)], self.own[len(x_items) :]
        self.other_x, self.other_y = ([(r, v) for r, _, v in items] for items in (x_items, y_items))

    def first(self):
        self.sent = [weight_grad(self.other_x, None), weight_grad([*self.own_y, *self.other_y], 1)]
        self.from_x, self.from_y = swap_x(self.sent[0]), swap_y(self.sent[1])
        return self.sent

    def second(self, *deps):
        self.from_x, self.from_y = after(self.from_x, *deps), after(self.from_y, *deps)
        wide_y = self.from_y.shape[1] // 2
        self.sent = [
            weight_grad(self.own_x, 1, [(self.from_x, 1, 0)]),
            weight_grad(self.other_y, 0, [(self.from_y, 0, -wide_y)]),
        ]
        self.late_y, self.late_x = swap_y(self.sent[0]), swap_x(self.sent[1])
        return self.sent

    def third(self, *deps, behind=()):
        wide_x = self.from_x.shape[1]
        late_y, late_x = after(self.late_y, *deps), after(self.late_x, *deps)
        summed = weight_grad(
            self.own, 0, [(self.from_x, 0, 0), (late_y, 0, 0), (self.from_y, 0, wide_x), (late_x, 0, wide_x)]
        )
        self.sent = [summed]
        summed = after(summed, *behind) if behind else summed
        summed = lax.psum_scatter(row_major(summed), "dz", scatter_dimension=0, tiled=True)
        self.result = summed.astype(f32)
        return self.sent


def on_device(
    tokens,
    encoder,
    cotangent,
    lengths,
    deal,
    attn_in,
    attn_out,
    ff_in,
    ff_out,
    gains,
    mom_attn_in,
    mom_attn_out,
    mom_ff_in,
    mom_ff_out,
    mom_gains,
    avg_attn_in,
    avg_attn_out,
    avg_ff_in,
    avg_ff_out,
    avg_gains,
):
    seq_count, block_rows = tokens.shape[0], tokens.shape[1]
    core = lax.axis_index("mc")
    dy = lax.axis_index("dy")
    chip = lax.axis_index(chips)
    own_rows = block_rows * seq_count
    slot_len = 2 * own_rows
    heads_cols = attn_in.shape[2]
    hidden = ff_in.shape[2]
    model_rows = attn_in.shape[1]

    def exchange(values):
        return lax.all_to_all(values, chips, split_axis=0, concat_axis=0, tiled=True)

    def to_chips(values):
        return exchange(values).reshape(own_rows, D)

    def from_chips(rows):
        return exchange(rows.reshape(seq_count, block_rows, D))

    seq_len = lengths[deal[chip]]
    row_ids = jnp.arange(own_rows, dtype=jnp.int32)
    lane = row_ids % block_rows
    pos_own = (row_ids // block_rows * 2 + core) * block_rows + lane
    pos_other = (row_ids // block_rows * 2 + 1 - core) * block_rows + lane
    pos = jnp.concatenate([pos_own, pos_other])
    places = (pos[:, None], pos[None, :])
    length = seq_len[None]
    valid_own = (pos_own < seq_len).astype(f32)[:, None]

    hc = heads_cols
    pairs = hc // (2 * DK)
    spare = -hidden % 256
    deep = hidden + spare
    widen = lambda t: jnp.pad(t.astype(bf16), ((0, 0), (0, spare)))
    out_t = jnp.swapaxes(attn_out.astype(bf16), 1, 2)
    low_in = attn_in.astype(bf16)
    pad = jnp.zeros((model_rows, 125), bf16)
    chunk_a = jnp.concatenate([*low_in[0:3], out_t[0], gains.astype(bf16).T, pad], axis=1)
    chunk_b = jnp.concatenate([*low_in[3:6], out_t[1]], axis=1)
    chunk_c = jnp.concatenate([widen(ff_in[0]), widen(ff_in[1]), widen(ff_out.T)], axis=1)

    tok_own = to_chips(tokens)
    part_a, part_b, part_c = (gather_part(t) for t in (chunk_a, chunk_b, chunk_c))
    got_a = spread(part_a, True)
    enc_own = to_chips(after(encoder, part_c))
    got_b = spread(part_b, False)
    cot_own = to_chips(cotangent)

    gain_f = jnp.concatenate([g[:, 4 * hc : 4 * hc + 3] for g in got_a[0]]).astype(f32).T
    gain_rows = [gain_f[n : n + 1] for n in range(3)]
    w_qkv = [(*g, 3 * hc, 0) for g in got_a]
    w_q, w_k, w_v, w_ot = ([(*g, hc, n) for g in got_a] for n in range(4))
    w_cq, w_ck, w_cv, w_cot = ([(*g, hc, n) for g in got_b] for n in range(4))

    def both(own):
        return own, swap_cores(own)

    def over_cores(values, weights):
        away = [swap_cores(t) for t in combine(values, weights, 1)]
        return combine(values, weights, 0), away

    x_own = reorder([after(tok_own, chunk_b, chunk_c)], model_rows, dy, True)
    norm_one = both(add_norm([x_own], gain_rows[0])[0])
    norm_one = after(norm_one[0], part_b), norm_one[1]
    qkv = [project(norm_one, [w_qkv[0]])[0]]
    qkv += project((after(norm_one[0], got_b[0][1], got_b[1][0]), norm_one[1]), [w_qkv[1]])
    self_qkv = [[(t, n * pairs, pairs) for n in range(3)] for t in qkv]
    got_c = spread(after(part_c, qkv[1]), True)
    w_g, w_u, w_dt = ([(*g, deep, n) for g in got_c] for n in range(3))
    self_qkv[1][0] = (after(qkv[1], got_b[1][1]), *self_qkv[1][0][1:])
    self_out = [attend(*t, *places, length, True, 256) for t in self_qkv]
    self_mixed = [self_out[0][0], after(self_out[1][0], part_c)]
    hidden_one, norm_two = add_norm([x_own, *over_cores(self_mixed, w_ot)], gain_rows[1])
    norm_two = both(norm_two)
    e_own = reorder([enc_own], model_rows, dy, True)
    enc_rows = both(e_own)
    cross_kv = project(enc_rows, [*w_ck, *w_cv])
    cross_q = project(norm_two, w_cq)
    cross_qkv = [
        [(t, 0, pairs) for t in (cross_q[n], cross_kv[n], cross_kv[2 + n])] for n in range(2)
    ]
    cross_qkv[1][0] = (after(cross_q[1], cross_q[0], got_c[0][1], got_c[1][0]), 0, pairs)
    cross_out = [attend(*t, *places, length, False, 512) for t in cross_qkv]
    cross_mixed = [o[0] for o in cross_out]
    hidden_two, norm_three = add_norm(
        [hidden_one, *over_cores(cross_mixed, w_cot)], gain_rows[2]
    )
    norm_three = both(norm_three)
    dy_own = reorder([cot_own], model_rows, dy, True, valid_own)
    grad_out = both(dy_own)
    inner, slope, value = zip(*[project(norm_three, list(w), "gelu") for w in zip(w_g, w_u)])

    scales = [t for pair in zip(slope, value) for t in pair]
    grad_gu = project(grad_out, w_dt, "scale", scales)
    grad_gate, grad_up = grad_gu[::2], grad_gu[1::2]
    group_c = Group([(norm_three, *grad_gate), (grad_out, *inner)], [(norm_three, *grad_up)])
    sent = group_c.first()
    parts = over_cores([after(grad_gate[0], *sent), grad_gate[1], *grad_up], [*w_g, *w_u])
    grad_two, low_two, gain_three = norm_back(hidden_two, gain_rows[2], parts, dy_own)
    grad_co = both(low_two)
    out_parts = over_cores([after(inner[0], low_two), inner[1]], w_dt)
    grad_ca = project((after(grad_co[0], out_parts[0][0]), grad_co[1]), w_cot)
    out_block = reorder([after(hidden_two, *grad_ca), *out_parts], model_rows, dy, False, valid_own)
    block_output = from_chips(out_block)
    cross_qkv[0][0] = (after(cross_q[0], out_block), 0, pairs)
    cross_back = [
        attend_back(*t, *places, o[1], d, False, 512) for t, o, d in zip(cross_qkv, cross_out, grad_ca)
    ]
    grad_cq, grad_ck, grad_cv = zip(*cross_back)
    group_b = Group(
        [(norm_two, *grad_cq), (grad_co, *[o[0] for o in cross_out])],
        [(enc_rows, *grad_ck), (enc_rows, *grad_cv)],
    )
    parts = over_cores(grad_cq, w_cq)
    sent = group_b.first()
    parts_enc = over_cores([after(grad_ck[0], *sent), grad_ck[1], *grad_cv], [*w_ck, *w_cv])
    grad_one, low_one, gain_two = norm_back(
        hidden_one, gain_rows[1], [parts[0], [after(parts[1][0], parts_enc[0][0]), parts[1][1]]], grad_two
    )
    grad_o = both(low_one)
    out_enc = reorder([parts_enc[0], [after(parts_enc[1][0], low_one), parts_enc[1][1]]], model_rows, dy, False)
    grad_encoder = from_chips(out_enc)
    sent = group_c.second(out_enc)
    grad_a = project((after(grad_o[0], *sent, block_output), grad_o[1]), w_ot)
    self_back = [attend_back(*self_qkv[0], *places, self_out[0][1], grad_a[0], True, 256)]
    sent = group_c.third(*self_back[0])
    self_back.append(attend_back(*self_qkv[1], *places, self_out[1][1], after(grad_a[1], *sent), True, 256))
    sent = group_b.second(*self_back[1])
    grad_q, grad_k, grad_v = zip(*self_back)
    group_a = Group(
        [(norm_one, *grad_q), (grad_o, *[o[0] for o in self_out])],
        [(norm_one, *grad_k), (norm_one, *grad_v)],
    )
    sent = group_a.first()
    parts = over_cores(
        [after(grad_q[0], *sent, *group_b.sent, grad_encoder), grad_q[1], *grad_k, *grad_v], [*w_q, *w_k, *w_v]
    )
    sent = group_b.third(*parts[0], behind=[group_c.result])
    _, low_tok, gain_one = norm_back(
        x_own, gain_rows[0], [[after(parts[0][0], *sent), parts[0][1]], parts[1]], grad_one
    )
    group_a.second(low_tok)
    out_tok = reorder([after(low_tok, *group_a.sent)], model_rows, dy, False)
    grad_tokens = from_chips(out_tok)
    group_a.third(out_tok, behind=[group_b.result])
    sum_a, sum_b, sum_c = group_a.result, group_b.result, group_c.result

    dp_count = seq_count // 2
    gain_part = jnp.concatenate([gain_one, gain_two, gain_three])
    gain_part = gain_part + swap_cores(gain_part)
    low, high = (gain_part[:, n * D // 2 : (n + 1) * D // 2].reshape(3, dp_count // 2, model_rows) for n in range(2))
    gain_part = jnp.stack([jnp.where(dy == 0, low, high), jnp.where(dy == 0, high, low)], axis=2)
    gain_part = jnp.swapaxes(gain_part.reshape(3, dp_count, model_rows), 0, 1)
    mx = lax.axis_index("mx")
    tops = [jnp.where(mx == n, self_out[0][2], self_out[1][2]) for n in range(2)]
    tops = jnp.broadcast_to(jnp.stack(tops)[None], (dp_count, 2, hc // DK))
    small = jnp.concatenate(
        [jnp.repeat(gain_part, 2, axis=0).reshape(dp_count * 2, -1), tops.reshape(dp_count * 2, -1)], axis=1
    )
    small = exchange(small)
    red_gain = jnp.sum(small[:, : 3 * model_rows], axis=0).reshape(3, model_rows)
    head_peak = jnp.max(small[:, 3 * model_rows :], axis=0)

    cut = lambda t, n: t[:, n * hc : (n + 1) * hc]
    red_in = jnp.stack([cut(t, n) for t in (sum_a, sum_b) for n in (0, 2, 3)])
    red_out = jnp.stack([cut(sum_a, 1).T, cut(sum_b, 1).T])
    red_ff = jnp.stack([sum_c[:, n * deep : n * deep + hidden] for n in (0, 2)])
    red_out = with_layout_constraint(red_out, Layout(major_to_minor=(0, 1, 2)))
    red_ff = with_layout_constraint(red_ff, Layout(major_to_minor=(0, 2, 1)))
    red_down = with_layout_constraint(sum_c[:, deep : deep + hidden].T, Layout(major_to_minor=(0, 1)))
    clip_factors = clip_limit / jnp.maximum(head_peak, clip_limit)
    column = jnp.repeat(jnp.sqrt(clip_factors), DK)
    factor = jnp.where((jnp.arange(6) < 2)[:, None, None], column[None, None, :], 1.0)
    grad_scale = float(seq_count * slot_len) ** (-0.5)
    up_a = apply_update(attn_in, red_in, mom_attn_in, avg_attn_in, factor, grad_scale)
    up_b = apply_update(attn_out, red_out, mom_attn_out, avg_attn_out, 1.0, grad_scale)
    up_c = apply_update(ff_in, red_ff, mom_ff_in, avg_ff_in, 1.0, grad_scale)
    up_d = apply_update(ff_out, red_down, mom_ff_out, avg_ff_out, 1.0, grad_scale)
    up_e = apply_update(gains, red_gain, mom_gains, avg_gains, 1.0, grad_scale)
    return (
        block_output.astype(f32),
        grad_tokens.astype(f32),
        grad_encoder.astype(f32),
        *up_a,
        *up_b,
        *up_c,
        *up_d,
        *up_e,
        head_peak,
        clip_factors,
    )


def solution(mesh):
    dp, mp = mesh.shape["dp"], mesh.shape["mp"]
    fine = Mesh(mesh.devices.reshape(dp // 2, 2, mp // 2, 2), ("dz", "dy", "mx", "mc"))
    dp_axes, mp_axes = ("dz", "dy"), ("mx", "mc")
    rows = P(None, (*dp_axes, *mp_axes), None)
    wide = P(None, dp_axes, mp_axes)
    tall = P(None, mp_axes, dp_axes)
    down = P(mp_axes, dp_axes)
    gain = P(None, dp_axes)
    state = (wide, tall, wide, down, gain)
    in_specs = (rows, rows, rows, P(), P(), *state, *state, *state)
    out_specs = (
        rows,
        rows,
        rows,
        *[wide] * 4,
        *[tall] * 4,
        *[wide] * 4,
        *[down] * 4,
        *[gain] * 4,
        P(mp_axes),
        P(mp_axes),
    )
    return jax.shard_map(
        on_device, mesh=fine, in_specs=in_specs, out_specs=out_specs, check_vma=False
    )
```

```python
import functools

import jax
import jax.numpy as jnp
from jax import lax
from jax.experimental import pallas as pl
from jax.experimental.layout import Layout, with_layout_constraint
from jax.experimental.pallas import tpu as pltpu
from jax.sharding import Mesh, PartitionSpec as P

D = 1024
DK = 64

epsilon = 1e-06
clip_limit = 10.0
momentum_rate = 0.9
learn_rate = 0.01
average_rate = 0.5
neg_large = -1e30
vmem_room = 24 << 20
tanh_rate = 0.7978845608
tanh_cube = 0.044715
bf16 = jnp.bfloat16
f32 = jnp.float32
swap = ((0, 1), (1, 0))
chips = ("dz", "dy", "mx")


def dot(left, right, dims):
    return lax.dot_general(left, right, (dims, ((), ())), preferred_element_type=f32)


def head_lanes(block, head):
    lanes = lax.broadcasted_iota(jnp.int32, block.shape, 1)
    return jnp.where((lanes >= DK) == (head == 1), block, jnp.zeros_like(block))


def key_spans(rows, keys, start, size, causal):
    half = rows // 2
    reach = start % half + size
    return [(0, reach), (half, half + reach)] if causal and reach < half else [(0, keys)]


def total(parts):
    return functools.reduce(jnp.add, parts)


def attend_kernel(causal, size, q_ref, k_ref, v_ref, pq_ref, pk_ref, len_ref, o_ref, lse_ref, top_ref):
    rows, keys = q_ref.shape[0], k_ref.shape[0]
    tops = []
    for head in range(2):
        k, v = head_lanes(k_ref[...], head), head_lanes(v_ref[...], head)
        top = jnp.full((1, 1), neg_large, f32)
        for start in range(0, rows, size):
            r = slice(start, start + size)
            spans = key_spans(rows, keys, start, size, causal)
            q = q_ref[r, :]
            s = [dot(q, k[a:b], ((1,), (1,))) for a, b in spans]
            if causal:
                s = [jnp.where(pk_ref[:, a:b] <= pq_ref[r, :], t, neg_large) for t, (a, b) in zip(s, spans)]
            m = functools.reduce(jnp.maximum, [jnp.max(t, axis=1, keepdims=True) for t in s])
            if causal:
                real = jnp.where(pq_ref[r, :] < len_ref[0], m, neg_large)
                top = jnp.maximum(top, jnp.max(real, axis=0, keepdims=True))
            e = [jnp.exp(t - m) for t in s]
            mass = total([jnp.sum(t, axis=1, keepdims=True) for t in e])
            scale = 1.0 / mass
            mix = total([dot((t * scale).astype(bf16), v[a:b], ((1,), (0,))) for t, (a, b) in zip(e, spans)])
            if head == 0:
                o_ref[r, :] = mix.astype(bf16)
            else:
                o_ref[r, :] = (o_ref[r, :].astype(f32) + mix).astype(bf16)
            lse_ref[0, r, head : head + 1] = m + jnp.log(mass)
        tops.append(top)
    lanes = lax.broadcasted_iota(jnp.int32, (8, 128), 1)
    top_ref[0] = jnp.where(lanes == 0, tops[0], tops[1])


def attend_back_kernel(
    causal, size, q_ref, k_ref, v_ref, pq_ref, pk_ref, lse_ref, do_ref, dq_ref, dk_ref, dv_ref, dk_acc, dv_acc
):
    rows, keys = q_ref.shape[0], k_ref.shape[0]
    dk_acc[...] = jnp.zeros_like(dk_acc)
    dv_acc[...] = jnp.zeros_like(dv_acc)
    for head in range(2):
        k, v = head_lanes(k_ref[...], head), head_lanes(v_ref[...], head)
        own = slice(DK * head, DK * head + DK)
        for start in range(0, rows, size):
            r = slice(start, start + size)
            spans = key_spans(rows, keys, start, size, causal)
            q, do, lse = q_ref[r, :], do_ref[r, :], lse_ref[0, r, head : head + 1]
            soft, grad = [], []
            for a, b in spans:
                s = dot(q, k[a:b], ((1,), (1,)))
                if causal:
                    s = jnp.where(pk_ref[:, a:b] <= pq_ref[r, :], s, neg_large)
                soft.append(jnp.exp(s - lse))
                grad.append(dot(do, v[a:b], ((1,), (1,))))
            row_dot = total([jnp.sum(p * t, axis=1, keepdims=True) for p, t in zip(soft, grad)])
            q_t, do_t = q.T[own], do.T[own]
            parts = []
            for (a, b), p, t in zip(spans, soft, grad):
                ds = (p * (t - row_dot)).astype(bf16)
                parts.append(dot(ds, k[a:b], ((1,), (0,))))
                dv_acc[own, a:b] += dot(do_t, p.astype(bf16), ((1,), (0,)))
                dk_acc[own, a:b] += dot(q_t, ds, ((1,), (0,)))
            dq = total(parts)
            if head == 0:
                dq_ref[r, :] = dq.astype(bf16)
            else:
                dq_ref[r, :] = (dq_ref[r, :].astype(f32) + dq).astype(bf16)
    dk_ref[...] = dk_acc[...].T.astype(bf16)
    dv_ref[...] = dv_acc[...].T.astype(bf16)


def attend_cost(rows, keys, pairs, dots):
    return cost(0, 0)


def lane_pairs(count, first):
    return pl.BlockSpec((count, 2 * DK), lambda p: (0, first + p))


def attend(q, k, v, pos_col, pos_row, length, causal, size):
    rows, keys, pairs = q[0].shape[0], k[0].shape[0], q[2]
    mixed, lse, top = pl.pallas_call(
        functools.partial(attend_kernel, causal, size),
        grid=(pairs,),
        in_specs=[
            lane_pairs(rows, q[1]),
            lane_pairs(keys, k[1]),
            lane_pairs(keys, v[1]),
            pl.BlockSpec((rows, 1), lambda p: (0, 0)),
            pl.BlockSpec((1, keys), lambda p: (0, 0)),
            pl.BlockSpec(memory_space=pltpu.SMEM),
        ],
        out_specs=[
            lane_pairs(rows, 0),
            pl.BlockSpec((1, rows, 2), lambda p: (p, 0, 0)),
            pl.BlockSpec((1, 8, 128), lambda p: (p, 0, 0)),
        ],
        out_shape=[
            jax.ShapeDtypeStruct((rows, pairs * 2 * DK), bf16),
            jax.ShapeDtypeStruct((pairs, rows, 2), f32),
            jax.ShapeDtypeStruct((pairs, 8, 128), f32),
        ],
        compiler_params=pltpu.CompilerParams(vmem_limit_bytes=vmem_room),
        cost_estimate=attend_cost(rows, keys, pairs, 2),
        name="attend",
    )(q[0], k[0], v[0], pos_col, pos_row, length)
    return mixed, lse, top[:, 0, :2].reshape(-1)


def attend_back(q, k, v, pos_col, pos_row, lse, grad, causal, size):
    rows, keys, pairs = q[0].shape[0], k[0].shape[0], q[2]
    return pl.pallas_call(
        functools.partial(attend_back_kernel, causal, size),
        grid=(pairs,),
        in_specs=[
            lane_pairs(rows, q[1]),
            lane_pairs(keys, k[1]),
            lane_pairs(keys, v[1]),
            pl.BlockSpec((rows, 1), lambda p: (0, 0)),
            pl.BlockSpec((1, keys), lambda p: (0, 0)),
            pl.BlockSpec((1, rows, 2), lambda p: (p, 0, 0)),
            lane_pairs(rows, 0),
        ],
        out_specs=[lane_pairs(rows, 0), lane_pairs(keys, 0), lane_pairs(keys, 0)],
        out_shape=[jax.ShapeDtypeStruct((n, pairs * 2 * DK), bf16) for n in (rows, keys, keys)],
        scratch_shapes=[pltpu.VMEM((2 * DK, keys), f32)] * 2,
        compiler_params=pltpu.CompilerParams(vmem_limit_bytes=vmem_room),
        cost_estimate=attend_cost(rows, keys, pairs, 5),
        name="attend_back",
    )(q[0], k[0], v[0], pos_col, pos_row, lse, grad)


def apply_update(weight, grad_sum, moment, average, factor, grad_scale):
    grad_now = grad_sum * grad_scale
    moment_new = momentum_rate * moment + grad_now
    master_new = (weight - learn_rate * (grad_now + momentum_rate * moment_new)) * factor
    average_new = average_rate * average + (1.0 - average_rate) * master_new
    return (grad_now, moment_new, average_new, master_new)


def flat_columns(block):
    return jnp.swapaxes(block, 0, 1).reshape(block.shape[1], -1)


def row_major(values):
    return with_layout_constraint(values, Layout(major_to_minor=tuple(range(values.ndim))))


spec = pl.BlockSpec


def cost(flops, moved):
    return pl.CostEstimate(flops=1, bytes_accessed=1, transcendentals=0)


def reorder(parts, block, dy, to_own, keep=None):
    arrays = halves(parts)
    rows, width = arrays[0].shape[0], D
    steps = width // block // 2
    extra = [] if keep is None else [keep]
    if block % 128:
        value = total([(jnp.concatenate(p, axis=1) if isinstance(p, (list, tuple)) else p).astype(f32) for p in parts])
        value = value * (1.0 if keep is None else keep)
        axis = 2 if to_own else 1
        value = value.reshape((rows, steps, 2, block) if to_own else (rows, 2, steps, block))
        low, high = (lax.index_in_dim(value, n, axis, keepdims=False) for n in range(2))
        pair = jnp.where(dy == 0, low, high), jnp.where(dy == 0, high, low)
        return jnp.stack(pair, axis=3 - axis).reshape(rows, width).astype(bf16)

    def source(j, flag):
        if to_own:
            return j % steps * 2 + (j // steps + flag) % 2
        return j // 2 + (j % 2 + flag) % 2 * steps

    def kernel(flag_ref, *refs):
        out = refs[-1]
        whole = len(arrays) == 1
        value = refs[0] if whole else read_total(parts, refs[: len(arrays)])
        for j in range(2 * steps):
            spans = [slice(source(j, flag) * block, (source(j, flag) + 1) * block) for flag in range(2)]
            picked = jnp.where(flag_ref[0] == 0, value[:, spans[0]], value[:, spans[1]])
            if extra:
                picked = picked.astype(f32) * refs[len(arrays)][...]
            out[:, j * block : (j + 1) * block] = picked.astype(bf16)

    return pl.pallas_call(
        kernel,
        grid=(4,),
        in_specs=[
            spec(memory_space=pltpu.SMEM),
            *[by_rows(p, rows // 4) for p in [*arrays, *extra]],
        ],
        out_specs=spec((rows // 4, width), lambda i: (i, 0)),
        out_shape=jax.ShapeDtypeStruct((rows, width), bf16),
        compiler_params=pltpu.CompilerParams(vmem_limit_bytes=vmem_room),
        cost_estimate=cost(0, rows * width * 4),
        name="reorder",
    )(dy[None], *arrays, *extra)


def weight_specs(weights):
    specs, arrays = [], []
    for own, other, width, *places in weights:
        for array, place in zip((own, other), (places[0], places[-1])):
            specs.append(spec((array.shape[0], width), lambda i, place=place: (0, place)))
            arrays.append(array)
    return specs, arrays


def project(rows, weights, mode="plain", scales=()):
    own, other = rows
    half, size = own.shape[0], own.shape[0] // 2
    specs, arrays = weight_specs(weights)
    widths = [w[2] for w in weights]
    count = len(weights)
    out_widths = {"plain": widths, "gelu": widths[:1] * 3, "scale": [w for w in widths for _ in range(2)]}[mode]

    def kernel(own_ref, other_ref, *refs):
        here = pl.program_id(0) < 2
        x = jnp.where(here, own_ref[...], other_ref[...])
        split = x.shape[1] // 2
        made = []
        for j in range(count):
            low, high = refs[2 * j], refs[2 * j + 1]
            made.append(
                dot(x[:, :split], low[...], ((1,), (0,))) + dot(x[:, split:], high[...], ((1,), (0,)))
            )
        outs = refs[2 * count + len(scales) :]
        if mode == "plain":
            for out, value in zip(outs, made):
                out[...] = value.astype(bf16)
        elif mode == "gelu":
            gate, up = made
            square = gate * gate
            bend = jnp.tanh(tanh_rate * gate * (1.0 + tanh_cube * square))
            rise = 0.5 * (1.0 + bend)
            value = gate * rise
            slope = rise + 0.5 * gate * (1.0 - bend * bend) * tanh_rate * (1.0 + 3.0 * tanh_cube * square)
            outs[0][...] = (value * up).astype(bf16)
            outs[1][...] = (slope * up).astype(bf16)
            outs[2][...] = value.astype(bf16)
        else:
            for j, out in enumerate(outs):
                out[...] = (made[j // 2] * refs[2 * count + j][...].astype(f32)).astype(bf16)

    by_rows = lambda width: spec((size, width), lambda i: (i, 0))
    width_all = own.shape[1]
    return pl.pallas_call(
        kernel,
        grid=(4,),
        in_specs=[
            spec((size, width_all), lambda i: (jnp.minimum(i, 1), 0)),
            spec((size, width_all), lambda i: (jnp.maximum(i - 2, 0), 0)),
            *specs,
            *[by_rows(t.shape[1]) for t in scales],
        ],
        out_specs=[by_rows(w) for w in out_widths],
        out_shape=[jax.ShapeDtypeStruct((2 * half, w), bf16) for w in out_widths],
        compiler_params=pltpu.CompilerParams(vmem_limit_bytes=vmem_room),
        cost_estimate=cost(4 * half * width_all * sum(widths), half * width_all * 4 + width_all * sum(widths) * 2),
        name="project_" + mode,
    )(own, other, *arrays, *scales)


def combine(values, weights, which):
    specs, arrays = weight_specs(weights)
    half = values[0].shape[0] // 2
    size = half // 2
    count = len(values)
    depth = weights[0][0].shape[0]

    def kernel(*refs):
        for side in range(2):
            parts = [
                dot(refs[j][...], refs[count + 2 * j + side][...], ((1,), (1,))) for j in range(count)
            ]
            refs[side - 2][...] = total(parts)

    return pl.pallas_call(
        kernel,
        grid=(2,),
        in_specs=[spec((size, v.shape[1]), lambda i: (2 * which + i, 0)) for v in values] + specs,
        out_specs=[spec((size, depth), lambda i: (i, 0))] * 2,
        out_shape=[jax.ShapeDtypeStruct((half, depth), f32)] * 2,
        compiler_params=pltpu.CompilerParams(vmem_limit_bytes=vmem_room),
        cost_estimate=cost(0, 0),
        name="combine",
    )(*values, *arrays)


def weight_grad(items, part, arrived=()):
    sources = []
    for rows, _ in items:
        if not any(rows is t for t in sources):
            sources.append(rows)
    half, width = sources[0][0].shape
    size = width // 2
    steps, base = (2, 0) if part is None else (1, part)
    spans, last = [], 0
    for _, value in items:
        spans.append((last, last + value.shape[1]))
        last = spans[-1][1]
    first = len(sources) * 2

    def kernel(*refs):
        out = refs[-1]
        for (rows, _), value, (a, b) in zip(items, refs[first:], spans):
            place = [rows is t for t in sources].index(True)
            own, other = refs[2 * place], refs[2 * place + 1]
            made = dot(own[...], value[:half], ((0,), (0,))) + dot(other[...], value[half:], ((0,), (0,)))
            for (array, _, start), came in zip(arrived, refs[first + len(items) :]):
                if start <= a < start + array.shape[1]:
                    made = made + came[:, a - start : b - start].astype(f32)
            out[:, a:b] = made.astype(bf16)

    columns = spec((half, size), lambda i: (0, base + i))
    return pl.pallas_call(
        kernel,
        grid=(steps,),
        in_specs=[columns] * first
        + [spec(v.shape, lambda i: (0, 0)) for _, v in items]
        + [spec((size, a.shape[1]), lambda i, place=place: (place + i, 0)) for a, place, _ in arrived],
        out_specs=spec((size, last), lambda i: (i, 0)),
        out_shape=jax.ShapeDtypeStruct((steps * size, last), bf16),
        compiler_params=pltpu.CompilerParams(vmem_limit_bytes=vmem_room),
        cost_estimate=cost(4 * half * steps * size * last, half * width * 4 + half * 4 * last),
        name="weight_grad",
    )(*[t for pair in sources for t in pair], *[v for _, v in items], *[a for a, _, _ in arrived])


def halves(parts):
    return [t for p in parts for t in (p if isinstance(p, (list, tuple)) else [p])]


def read_total(parts, refs):
    refs, read = list(refs), []
    for p in parts:
        if isinstance(p, (list, tuple)):
            read.append(jnp.concatenate([refs.pop(0)[...] for _ in p], axis=1))
        else:
            read.append(refs.pop(0)[...])
    return total([r.astype(f32) for r in read])


def by_rows(array, size=256):
    if array.shape[0] == 1:
        return spec(array.shape, lambda i: (0, 0))
    return spec((size, array.shape[1]), lambda i: (i, 0))


def add_norm(parts, gain_row):
    arrays = halves(parts)
    rows, width = arrays[0].shape[0], D

    def kernel(gain_ref, *refs):
        hidden = read_total(parts, refs[: len(arrays)])
        scale = lax.rsqrt(jnp.mean(hidden * hidden, axis=-1, keepdims=True) + epsilon)
        refs[-1][...] = (hidden * scale * gain_ref[...]).astype(bf16)
        if len(parts) > 1:
            refs[-2][...] = hidden

    kinds = [f32, bf16] if len(parts) > 1 else [bf16]
    shapes = [jax.ShapeDtypeStruct((rows, width), k) for k in kinds]
    return pl.pallas_call(
        kernel,
        grid=(rows // 256,),
        in_specs=[by_rows(gain_row), *[by_rows(p) for p in arrays]],
        out_specs=[by_rows(t) for t in shapes],
        out_shape=shapes,
        compiler_params=pltpu.CompilerParams(vmem_limit_bytes=vmem_room),
        cost_estimate=cost(rows * width * 8, rows * width * 14),
        name="add_norm",
    )(gain_row, *arrays)


def norm_back(hidden, gain_row, grads, base):
    rows, width = hidden.shape
    arrays = halves(grads)

    def kernel(gain_ref, hidden_ref, base_ref, *refs):
        grad = read_total(grads, refs[: len(arrays)])
        out, low, gain_grad = refs[len(arrays) :]
        hidden = hidden_ref[...].astype(f32)
        scale = lax.rsqrt(jnp.mean(hidden * hidden, axis=-1, keepdims=True) + epsilon)
        z = hidden * scale
        grad_z = grad * gain_ref[...]
        grad_hidden = scale * (grad_z - z * jnp.mean(grad_z * z, axis=-1, keepdims=True))
        value = base_ref[...].astype(f32) + grad_hidden
        out[...] = value
        low[...] = value.astype(bf16)

        @pl.when(pl.program_id(0) == 0)
        def _():
            gain_grad[...] = jnp.zeros_like(gain_grad)

        gain_grad[...] += jnp.sum(grad * z, axis=0, keepdims=True)

    shapes = [jax.ShapeDtypeStruct((rows, width), f32), jax.ShapeDtypeStruct((rows, width), bf16)]
    return pl.pallas_call(
        kernel,
        grid=(rows // 256,),
        in_specs=[by_rows(gain_row), by_rows(hidden), by_rows(base), *[by_rows(g) for g in arrays]],
        out_specs=[*[by_rows(t) for t in shapes], spec((1, width), lambda i: (0, 0))],
        out_shape=[*shapes, jax.ShapeDtypeStruct((1, width), f32)],
        compiler_params=pltpu.CompilerParams(vmem_limit_bytes=vmem_room),
        cost_estimate=cost(rows * width * 16, rows * width * 22),
        name="norm_back",
    )(gain_row, hidden, base, *arrays)


def after(value, *others):
    return lax.optimization_barrier((value, *others))[0]


def swap_cores(values):
    return lax.ppermute(values, "mc", swap)


def swap_x(values):
    return row_major(lax.ppermute(row_major(values), "mx", swap))


def swap_y(values):
    return row_major(lax.ppermute(row_major(values), "dy", swap))


def gather_part(local):
    return row_major(lax.all_gather(row_major(local), "dz", axis=0, tiled=True))


def spread(part, x_last):
    if x_last:
        high = swap_y(part)
        return (part, high), (swap_x(part), swap_x(high))
    beside = swap_x(part)
    return (part, swap_y(part)), (beside, swap_y(beside))


def pieces(value, count):
    made = []
    for _ in range(count):
        made.append(value.astype(bf16))
        value = value - made[-1].astype(f32)
    return made


class Group:
    def __init__(self, x_items, y_items):
        self.own = [(r, v) for r, v, _ in (*x_items, *y_items)]
        self.own_x, self.own_y = self.own[: len(x_items)], self.own[len(x_items) :]
        self.other_x, self.other_y = ([(r, v) for r, _, v in items] for items in (x_items, y_items))

    def first(self):
        self.sent = [weight_grad(self.other_x, None), weight_grad([*self.own_y, *self.other_y], 1)]
        self.from_x, self.from_y = swap_x(self.sent[0]), swap_y(self.sent[1])
        return self.sent

    def second(self, *deps):
        self.from_x, self.from_y = after(self.from_x, *deps), after(self.from_y, *deps)
        wide_y = self.from_y.shape[1] // 2
        self.sent = [
            weight_grad(self.own_x, 1, [(self.from_x, 1, 0)]),
            weight_grad(self.other_y, 0, [(self.from_y, 0, -wide_y)]),
        ]
        self.late_y, self.late_x = swap_y(self.sent[0]), swap_x(self.sent[1])
        return self.sent

    def third(self, *deps, behind=()):
        wide_x = self.from_x.shape[1]
        late_y, late_x = after(self.late_y, *deps), after(self.late_x, *deps)
        summed = weight_grad(
            self.own, 0, [(self.from_x, 0, 0), (late_y, 0, 0), (self.from_y, 0, wide_x), (late_x, 0, wide_x)]
        )
        self.sent = [summed]
        summed = after(summed, *behind) if behind else summed
        summed = lax.psum_scatter(row_major(summed), "dz", scatter_dimension=0, tiled=True)
        self.result = summed.astype(f32)
        return self.sent


def on_device(
    tokens,
    encoder,
    cotangent,
    lengths,
    deal,
    attn_in,
    attn_out,
    ff_in,
    ff_out,
    gains,
    mom_attn_in,
    mom_attn_out,
    mom_ff_in,
    mom_ff_out,
    mom_gains,
    avg_attn_in,
    avg_attn_out,
    avg_ff_in,
    avg_ff_out,
    avg_gains,
):
    seq_count, block_rows = tokens.shape[0], tokens.shape[1]
    core = lax.axis_index("mc")
    dy = lax.axis_index("dy")
    chip = lax.axis_index(chips)
    own_rows = block_rows * seq_count
    slot_len = 2 * own_rows
    heads_cols = attn_in.shape[2]
    hidden = ff_in.shape[2]
    model_rows = attn_in.shape[1]

    def exchange(values):
        return lax.all_to_all(values, chips, split_axis=0, concat_axis=0, tiled=True)

    def to_chips(values):
        return exchange(values).reshape(own_rows, D)

    def from_chips(rows):
        return exchange(rows.reshape(seq_count, block_rows, D))

    seq_len = lengths[deal[chip]]
    row_ids = jnp.arange(own_rows, dtype=jnp.int32)
    lane = row_ids % block_rows
    pos_own = (row_ids // block_rows * 2 + core) * block_rows + lane
    pos_other = (row_ids // block_rows * 2 + 1 - core) * block_rows + lane
    pos = jnp.concatenate([pos_own, pos_other])
    places = (pos[:, None], pos[None, :])
    length = seq_len[None]
    valid_own = (pos_own < seq_len).astype(f32)[:, None]

    hc = heads_cols
    pairs = hc // (2 * DK)
    spare = -hidden % 256
    deep = hidden + spare
    widen = lambda t: jnp.pad(t.astype(bf16), ((0, 0), (0, spare)))
    out_t = jnp.swapaxes(attn_out.astype(bf16), 1, 2)
    low_in = attn_in.astype(bf16)
    pad = jnp.zeros((model_rows, 125), bf16)
    chunk_a = jnp.concatenate([*low_in[0:3], out_t[0], gains.astype(bf16).T, pad], axis=1)
    chunk_b = jnp.concatenate([*low_in[3:6], out_t[1]], axis=1)
    chunk_c = jnp.concatenate([widen(ff_in[0]), widen(ff_in[1]), widen(ff_out.T)], axis=1)

    part_a, part_b, part_c = (gather_part(t) for t in (chunk_a, chunk_b, chunk_c))
    got_a = spread(part_a, True)
    tok_own = to_chips(after(tokens, part_a))
    cot_own = to_chips(cotangent)

    gain_f = jnp.concatenate([g[:, 4 * hc : 4 * hc + 3] for g in got_a[0]]).astype(f32).T
    gain_rows = [gain_f[n : n + 1] for n in range(3)]
    w_qkv = [(*g, 3 * hc, 0) for g in got_a]
    w_q, w_k, w_v, w_ot = ([(*g, hc, n) for g in got_a] for n in range(4))

    def both(own):
        return own, swap_cores(own)

    def over_cores(values, weights):
        away = [swap_cores(t) for t in combine(values, weights, 1)]
        return combine(values, weights, 0), away

    x_own = reorder([after(tok_own, chunk_b, chunk_c)], model_rows, dy, True)
    norm_one = both(add_norm([x_own], gain_rows[0])[0])
    norm_one = after(norm_one[0], part_b), norm_one[1]
    qkv = [project(norm_one, [w_qkv[0]])[0]]
    self_qkv = [[(qkv[0], n * pairs, pairs) for n in range(3)]]
    self_out = [attend(*self_qkv[0], *places, length, True, 256)]
    qkv += project((after(norm_one[0], self_out[0][0]), norm_one[1]), [w_qkv[1]])
    self_qkv += [[(qkv[1], n * pairs, pairs) for n in range(3)]]
    high_b, beside_b = swap_y(part_b), swap_x(part_b)
    self_out += [attend(*self_qkv[1], *places, length, True, 256)]
    far_b = swap_y(after(beside_b, self_out[1][0], high_b))
    got_b = (part_b, high_b), (beside_b, far_b)
    w_cq, w_ck, w_cv, w_cot = ([(*g, hc, n) for g in got_b] for n in range(4))

    enc_own = to_chips(after(encoder, part_c, self_out[1][0]))
    part_c = after(part_c, self_out[1][0], far_b)
    high_c, beside_c = swap_y(part_c), swap_x(part_c)
    far_gu, far_d = swap_x(high_c[:, : 2 * deep]), swap_y(beside_c[:, 2 * deep :])
    w_g, w_u, w_dt = (
        [(part_c, high_c, deep, n), (beside_c, far, deep, n, place)]
        for n, far, place in ((0, far_gu, 0), (1, far_gu, 1), (2, far_d, 0))
    )

    self_mixed = [o[0] for o in self_out]
    hidden_one, norm_two = add_norm([x_own, *over_cores(self_mixed, w_ot)], gain_rows[1])
    norm_two = both(norm_two)
    e_own = reorder([enc_own], model_rows, dy, True)
    enc_rows = both(e_own)
    cross_kv = project(enc_rows, [*w_ck, *w_cv])
    cross_q = project(norm_two, w_cq)
    cross_qkv = [
        [(t, 0, pairs) for t in (cross_q[n], cross_kv[n], cross_kv[2 + n])] for n in range(2)
    ]
    cross_qkv[0][0] = (after(cross_q[0], cross_q[1], high_c, beside_c), 0, pairs)
    cross_out = [attend(*t, *places, length, False, 512) for t in cross_qkv]
    cross_mixed = [o[0] for o in cross_out]
    hidden_two, norm_three = add_norm(
        [hidden_one, *over_cores(cross_mixed, w_cot)], gain_rows[2]
    )
    norm_three = both(norm_three)
    dy_own = reorder([cot_own], model_rows, dy, True, valid_own)
    grad_out = both(dy_own)
    inner, slope, value = zip(*[project(norm_three, list(w), "gelu") for w in zip(w_g, w_u)])

    scales = [t for pair in zip(slope, value) for t in pair]
    grad_gu = project(grad_out, w_dt, "scale", scales)
    grad_gate, grad_up = grad_gu[::2], grad_gu[1::2]
    group_c = Group([(norm_three, *grad_gate), (grad_out, *inner)], [(norm_three, *grad_up)])
    sent = group_c.first()
    parts = over_cores([after(grad_gate[0], *sent), grad_gate[1], *grad_up], [*w_g, *w_u])
    grad_two, low_two, gain_three = norm_back(hidden_two, gain_rows[2], parts, dy_own)
    grad_co = both(low_two)
    out_parts = over_cores([after(inner[0], low_two), inner[1]], w_dt)
    grad_ca = project((after(grad_co[0], out_parts[0][0]), grad_co[1]), w_cot)
    out_block = reorder([after(hidden_two, *grad_ca), *out_parts], model_rows, dy, False, valid_own)
    block_output = from_chips(out_block)
    cross_back = [attend_back(*cross_qkv[0], *places, cross_out[0][1], after(grad_ca[0], out_block), False, 512)]
    grad_late = after(grad_ca[1], group_c.from_y, *cross_back[0])
    cross_back += [attend_back(*cross_qkv[1], *places, cross_out[1][1], grad_late, False, 512)]
    grad_cq, grad_ck, grad_cv = zip(*cross_back)
    sent = group_c.second(*grad_cq)
    grad_cq = (after(grad_cq[0], *sent), grad_cq[1])
    group_b = Group(
        [(norm_two, *grad_cq), (grad_co, *[o[0] for o in cross_out])],
        [(enc_rows, *grad_ck), (enc_rows, *grad_cv)],
    )
    parts = over_cores(grad_cq, w_cq)
    sent = group_b.first()
    parts_enc = over_cores([after(grad_ck[0], *sent), grad_ck[1], *grad_cv], [*w_ck, *w_cv])
    grad_one, low_one, gain_two = norm_back(
        hidden_one, gain_rows[1], [parts[0], [after(parts[1][0], parts_enc[0][0]), parts[1][1]]], grad_two
    )
    grad_o = both(low_one)
    out_enc = reorder([parts_enc[0], [after(parts_enc[1][0], low_one), parts_enc[1][1]]], model_rows, dy, False)
    grad_encoder = from_chips(out_enc)
    grad_a = project((after(grad_o[0], out_enc, block_output), grad_o[1]), w_ot)
    self_back = [attend_back(*self_qkv[0], *places, self_out[0][1], grad_a[0], True, 256)]
    sent = group_c.third(*self_back[0])
    self_back.append(attend_back(*self_qkv[1], *places, self_out[1][1], after(grad_a[1], *sent), True, 256))
    sent = group_b.second(*self_back[1])
    self_back[1] = [*[after(t, *sent) for t in self_back[1][:2]], self_back[1][2]]
    grad_q, grad_k, grad_v = zip(*self_back)
    group_a = Group(
        [(norm_one, *grad_q), (grad_o, *[o[0] for o in self_out])],
        [(norm_one, *grad_k), (norm_one, *grad_v)],
    )
    sent = group_a.first()
    parts = over_cores(
        [after(grad_q[0], *sent, *group_b.sent, grad_encoder), grad_q[1], *grad_k, *grad_v], [*w_q, *w_k, *w_v]
    )
    sent = group_b.third(*parts[0], behind=[group_c.result])
    _, low_tok, gain_one = norm_back(
        x_own, gain_rows[0], [[after(parts[0][0], *sent), parts[0][1]], parts[1]], grad_one
    )
    group_a.second(low_tok)
    out_tok = reorder([after(low_tok, *group_a.sent)], model_rows, dy, False)
    dp_count = seq_count // 2
    gain_part = jnp.concatenate([gain_one, gain_two, gain_three])
    parts = [gain_part[:, n * D // 2 : (n + 1) * D // 2].reshape(3, dp_count // 2, model_rows) for n in range(2)]
    gain_part = jnp.stack([jnp.where(dy == 0, *parts), jnp.where(dy == 0, *parts[::-1])], axis=2)
    gain_part = jnp.swapaxes(gain_part.reshape(3, dp_count, model_rows), 0, 1).reshape(dp_count, -1)
    mx = lax.axis_index("mx")
    tops = jnp.stack([jnp.where(mx == n, self_out[0][2], self_out[1][2]) for n in range(2)])
    tops = jnp.broadcast_to(tops[None], (dp_count, *tops.shape)).reshape(seq_count, -1)
    small = jnp.concatenate([*pieces(jnp.repeat(gain_part, 2, axis=0), 2), *pieces(tops, 3)], axis=1)
    small = jnp.pad(small, ((0, 0), (0, D - small.shape[1])))[:, None]
    sent = jnp.concatenate([out_tok.reshape(seq_count, block_rows, D), small], axis=1)
    came = exchange(sent)
    grad_tokens, small = came[:, :block_rows], came[:, block_rows].astype(f32)
    group_a.third(out_tok, group_b.result)
    sum_a, sum_b, sum_c = group_a.result, group_b.result, group_c.result

    small = after(small, group_a.result)
    wide = 3 * model_rows
    red_gain = jnp.sum(small[:, :wide] + small[:, wide : 2 * wide], axis=0).reshape(3, model_rows)
    red_gain = red_gain + swap_cores(red_gain)
    tops = small[:, 2 * wide : 2 * wide + 3 * (hc // DK)].reshape(seq_count, 3, -1)
    head_peak = jnp.max(tops[:, 0] + tops[:, 1] + tops[:, 2], axis=0)

    cut = lambda t, n: t[:, n * hc : (n + 1) * hc]
    red_in = jnp.stack([cut(t, n) for t in (sum_a, sum_b) for n in (0, 2, 3)])
    red_out = jnp.stack([cut(sum_a, 1).T, cut(sum_b, 1).T])
    red_ff = jnp.stack([sum_c[:, n * deep : n * deep + hidden] for n in (0, 2)])
    red_in = row_major(red_in)
    red_out = with_layout_constraint(red_out, Layout(major_to_minor=(0, 1, 2)))
    red_ff = with_layout_constraint(red_ff, Layout(major_to_minor=(0, 2, 1)))
    red_down = with_layout_constraint(sum_c[:, deep : deep + hidden].T, Layout(major_to_minor=(0, 1)))
    clip_factors = clip_limit / jnp.maximum(head_peak, clip_limit)
    column = jnp.repeat(jnp.sqrt(clip_factors), DK)
    factor = jnp.where((jnp.arange(6) < 2)[:, None, None], column[None, None, :], 1.0)
    grad_scale = float(seq_count * slot_len) ** (-0.5)
    up_a = apply_update(attn_in, red_in, mom_attn_in, avg_attn_in, factor, grad_scale)
    up_b = apply_update(attn_out, red_out, mom_attn_out, avg_attn_out, 1.0, grad_scale)
    up_c = apply_update(ff_in, red_ff, mom_ff_in, avg_ff_in, 1.0, grad_scale)
    up_d = apply_update(ff_out, red_down, mom_ff_out, avg_ff_out, 1.0, grad_scale)
    up_e = apply_update(gains, red_gain, mom_gains, avg_gains, 1.0, grad_scale)
    return (
        block_output.astype(f32),
        grad_tokens.astype(f32),
        grad_encoder.astype(f32),
        *up_a,
        *up_b,
        *up_c,
        *up_d,
        *up_e,
        head_peak,
        clip_factors,
    )


def solution(mesh):
    dp, mp = mesh.shape["dp"], mesh.shape["mp"]
    fine = Mesh(mesh.devices.reshape(dp // 2, 2, mp // 2, 2), ("dz", "dy", "mx", "mc"))
    dp_axes, mp_axes = ("dz", "dy"), ("mx", "mc")
    rows = P(None, (*dp_axes, *mp_axes), None)
    wide = P(None, dp_axes, mp_axes)
    tall = P(None, mp_axes, dp_axes)
    down = P(mp_axes, dp_axes)
    gain = P(None, dp_axes)
    state = (wide, tall, wide, down, gain)
    in_specs = (rows, rows, rows, P(), P(), *state, *state, *state)
    out_specs = (
        rows,
        rows,
        rows,
        *[wide] * 4,
        *[tall] * 4,
        *[wide] * 4,
        *[down] * 4,
        *[gain] * 4,
        P(mp_axes),
        P(mp_axes),
    )
    return jax.shard_map(
        on_device, mesh=fine, in_specs=in_specs, out_specs=out_specs, check_vma=False
    )
```

```python
import functools

import jax
import jax.numpy as jnp
from jax import lax
from jax.experimental import pallas as pl
from jax.experimental.layout import Layout, with_layout_constraint
from jax.experimental.pallas import tpu as pltpu
from jax.sharding import Mesh, PartitionSpec as P

D = 1024
DK = 64

epsilon = 1e-06
clip_limit = 10.0
momentum_rate = 0.9
learn_rate = 0.01
average_rate = 0.5
neg_large = -1e30
vmem_room = 24 << 20
tanh_rate = 0.7978845608
tanh_cube = 0.044715
bf16 = jnp.bfloat16
f32 = jnp.float32
swap = ((0, 1), (1, 0))
chips = ("dz", "dy", "mx")


def dot(left, right, dims):
    return lax.dot_general(left, right, (dims, ((), ())), preferred_element_type=f32)


def head_lanes(block, head):
    lanes = lax.broadcasted_iota(jnp.int32, block.shape, 1)
    return jnp.where((lanes >= DK) == (head == 1), block, jnp.zeros_like(block))


def key_spans(rows, keys, start, size, causal):
    half = rows // 2
    reach = start % half + size
    return [(0, reach), (half, half + reach)] if causal and reach < half else [(0, keys)]


def total(parts):
    return functools.reduce(jnp.add, parts)


def attend_kernel(causal, size, q_ref, k_ref, v_ref, pq_ref, pk_ref, len_ref, o_ref, lse_ref, top_ref):
    rows, keys = q_ref.shape[0], k_ref.shape[0]
    tops = []
    for head in range(2):
        k, v = head_lanes(k_ref[...], head), head_lanes(v_ref[...], head)
        top = jnp.full((1, 1), neg_large, f32)
        for start in range(0, rows, size):
            r = slice(start, start + size)
            spans = key_spans(rows, keys, start, size, causal)
            q = q_ref[r, :]
            s = [dot(q, k[a:b], ((1,), (1,))) for a, b in spans]
            if causal:
                s = [jnp.where(pk_ref[:, a:b] <= pq_ref[r, :], t, neg_large) for t, (a, b) in zip(s, spans)]
            m = functools.reduce(jnp.maximum, [jnp.max(t, axis=1, keepdims=True) for t in s])
            if causal:
                real = jnp.where(pq_ref[r, :] < len_ref[0], m, neg_large)
                top = jnp.maximum(top, jnp.max(real, axis=0, keepdims=True))
            e = [jnp.exp(t - m) for t in s]
            mass = total([jnp.sum(t, axis=1, keepdims=True) for t in e])
            scale = 1.0 / mass
            mix = total([dot((t * scale).astype(bf16), v[a:b], ((1,), (0,))) for t, (a, b) in zip(e, spans)])
            if head == 0:
                o_ref[r, :] = mix.astype(bf16)
            else:
                o_ref[r, :] = (o_ref[r, :].astype(f32) + mix).astype(bf16)
            lse_ref[0, r, head : head + 1] = m + jnp.log(mass)
        tops.append(top)
    lanes = lax.broadcasted_iota(jnp.int32, (8, 128), 1)
    top_ref[0] = jnp.where(lanes == 0, tops[0], tops[1])


def attend_back_kernel(
    causal, size, q_ref, k_ref, v_ref, pq_ref, pk_ref, lse_ref, do_ref, dq_ref, dk_ref, dv_ref, dk_acc, dv_acc
):
    rows, keys = q_ref.shape[0], k_ref.shape[0]
    dk_acc[...] = jnp.zeros_like(dk_acc)
    dv_acc[...] = jnp.zeros_like(dv_acc)
    for head in range(2):
        k, v = head_lanes(k_ref[...], head), head_lanes(v_ref[...], head)
        own = slice(DK * head, DK * head + DK)
        for start in range(0, rows, size):
            r = slice(start, start + size)
            spans = key_spans(rows, keys, start, size, causal)
            q, do, lse = q_ref[r, :], do_ref[r, :], lse_ref[0, r, head : head + 1]
            soft, grad = [], []
            for a, b in spans:
                s = dot(q, k[a:b], ((1,), (1,)))
                if causal:
                    s = jnp.where(pk_ref[:, a:b] <= pq_ref[r, :], s, neg_large)
                soft.append(jnp.exp(s - lse))
                grad.append(dot(do, v[a:b], ((1,), (1,))))
            row_dot = total([jnp.sum(p * t, axis=1, keepdims=True) for p, t in zip(soft, grad)])
            q_t, do_t = q.T[own], do.T[own]
            parts = []
            for (a, b), p, t in zip(spans, soft, grad):
                ds = (p * (t - row_dot)).astype(bf16)
                parts.append(dot(ds, k[a:b], ((1,), (0,))))
                dv_acc[own, a:b] += dot(do_t, p.astype(bf16), ((1,), (0,)))
                dk_acc[own, a:b] += dot(q_t, ds, ((1,), (0,)))
            dq = total(parts)
            if head == 0:
                dq_ref[r, :] = dq.astype(bf16)
            else:
                dq_ref[r, :] = (dq_ref[r, :].astype(f32) + dq).astype(bf16)
    dk_ref[...] = dk_acc[...].T.astype(bf16)
    dv_ref[...] = dv_acc[...].T.astype(bf16)


def attend_cost(rows, keys, pairs, dots):
    return cost(0, 0)


def lane_pairs(count, first):
    return pl.BlockSpec((count, 2 * DK), lambda p: (0, first + p))


def attend(q, k, v, pos_col, pos_row, length, causal, size):
    rows, keys, pairs = q[0].shape[0], k[0].shape[0], q[2]
    mixed, lse, top = pl.pallas_call(
        functools.partial(attend_kernel, causal, size),
        grid=(pairs,),
        in_specs=[
            lane_pairs(rows, q[1]),
            lane_pairs(keys, k[1]),
            lane_pairs(keys, v[1]),
            pl.BlockSpec((rows, 1), lambda p: (0, 0)),
            pl.BlockSpec((1, keys), lambda p: (0, 0)),
            pl.BlockSpec(memory_space=pltpu.SMEM),
        ],
        out_specs=[
            lane_pairs(rows, 0),
            pl.BlockSpec((1, rows, 2), lambda p: (p, 0, 0)),
            pl.BlockSpec((1, 8, 128), lambda p: (p, 0, 0)),
        ],
        out_shape=[
            jax.ShapeDtypeStruct((rows, pairs * 2 * DK), bf16),
            jax.ShapeDtypeStruct((pairs, rows, 2), f32),
            jax.ShapeDtypeStruct((pairs, 8, 128), f32),
        ],
        compiler_params=pltpu.CompilerParams(vmem_limit_bytes=vmem_room),
        cost_estimate=attend_cost(rows, keys, pairs, 2),
        name="attend",
    )(q[0], k[0], v[0], pos_col, pos_row, length)
    return mixed, lse, top[:, 0, :2].reshape(-1)


def attend_back(q, k, v, pos_col, pos_row, lse, grad, causal, size):
    rows, keys, pairs = q[0].shape[0], k[0].shape[0], q[2]
    return pl.pallas_call(
        functools.partial(attend_back_kernel, causal, size),
        grid=(pairs,),
        in_specs=[
            lane_pairs(rows, q[1]),
            lane_pairs(keys, k[1]),
            lane_pairs(keys, v[1]),
            pl.BlockSpec((rows, 1), lambda p: (0, 0)),
            pl.BlockSpec((1, keys), lambda p: (0, 0)),
            pl.BlockSpec((1, rows, 2), lambda p: (p, 0, 0)),
            lane_pairs(rows, 0),
        ],
        out_specs=[lane_pairs(rows, 0), lane_pairs(keys, 0), lane_pairs(keys, 0)],
        out_shape=[jax.ShapeDtypeStruct((n, pairs * 2 * DK), bf16) for n in (rows, keys, keys)],
        scratch_shapes=[pltpu.VMEM((2 * DK, keys), f32)] * 2,
        compiler_params=pltpu.CompilerParams(vmem_limit_bytes=vmem_room),
        cost_estimate=attend_cost(rows, keys, pairs, 5),
        name="attend_back",
    )(q[0], k[0], v[0], pos_col, pos_row, lse, grad)


def apply_update(weight, grad_sum, moment, average, factor, grad_scale):
    grad_now = grad_sum * grad_scale
    moment_new = momentum_rate * moment + grad_now
    master_new = (weight - learn_rate * (grad_now + momentum_rate * moment_new)) * factor
    average_new = average_rate * average + (1.0 - average_rate) * master_new
    return (grad_now, moment_new, average_new, master_new)


def flat_columns(block):
    return jnp.swapaxes(block, 0, 1).reshape(block.shape[1], -1)


def row_major(values):
    return with_layout_constraint(values, Layout(major_to_minor=tuple(range(values.ndim))))


spec = pl.BlockSpec


def cost(flops, moved):
    return pl.CostEstimate(flops=1, bytes_accessed=1, transcendentals=0)


def reorder(parts, block, dy, to_own, keep=None):
    arrays = halves(parts)
    rows, width = arrays[0].shape[0], D
    steps = width // block // 2
    extra = [] if keep is None else [keep]
    if block % 128:
        value = total([(jnp.concatenate(p, axis=1) if isinstance(p, (list, tuple)) else p).astype(f32) for p in parts])
        value = value * (1.0 if keep is None else keep)
        axis = 2 if to_own else 1
        value = value.reshape((rows, steps, 2, block) if to_own else (rows, 2, steps, block))
        low, high = (lax.index_in_dim(value, n, axis, keepdims=False) for n in range(2))
        pair = jnp.where(dy == 0, low, high), jnp.where(dy == 0, high, low)
        return jnp.stack(pair, axis=3 - axis).reshape(rows, width).astype(bf16)

    def source(j, flag):
        if to_own:
            return j % steps * 2 + (j // steps + flag) % 2
        return j // 2 + (j % 2 + flag) % 2 * steps

    def kernel(flag_ref, *refs):
        out = refs[-1]
        whole = len(arrays) == 1
        value = refs[0] if whole else read_total(parts, refs[: len(arrays)])
        for j in range(2 * steps):
            spans = [slice(source(j, flag) * block, (source(j, flag) + 1) * block) for flag in range(2)]
            picked = jnp.where(flag_ref[0] == 0, value[:, spans[0]], value[:, spans[1]])
            if extra:
                picked = picked.astype(f32) * refs[len(arrays)][...]
            out[:, j * block : (j + 1) * block] = picked.astype(bf16)

    return pl.pallas_call(
        kernel,
        grid=(4,),
        in_specs=[
            spec(memory_space=pltpu.SMEM),
            *[by_rows(p, rows // 4) for p in [*arrays, *extra]],
        ],
        out_specs=spec((rows // 4, width), lambda i: (i, 0)),
        out_shape=jax.ShapeDtypeStruct((rows, width), bf16),
        compiler_params=pltpu.CompilerParams(vmem_limit_bytes=vmem_room),
        cost_estimate=cost(0, rows * width * 4),
        name="reorder",
    )(dy[None], *arrays, *extra)


def weight_specs(weights):
    specs, arrays = [], []
    for own, other, width, *places in weights:
        for array, place in zip((own, other), (places[0], places[-1])):
            specs.append(spec((array.shape[0], width), lambda i, place=place: (0, place)))
            arrays.append(array)
    return specs, arrays


def project(rows, weights, mode="plain", scales=()):
    own, other = rows
    half, size = own.shape[0], own.shape[0] // 2
    specs, arrays = weight_specs(weights)
    widths = [w[2] for w in weights]
    count = len(weights)
    out_widths = {"plain": widths, "gelu": widths[:1] * 3, "scale": [w for w in widths for _ in range(2)]}[mode]

    def kernel(own_ref, other_ref, *refs):
        here = pl.program_id(0) < 2
        x = jnp.where(here, own_ref[...], other_ref[...])
        split = x.shape[1] // 2
        made = []
        for j in range(count):
            low, high = refs[2 * j], refs[2 * j + 1]
            made.append(
                dot(x[:, :split], low[...], ((1,), (0,))) + dot(x[:, split:], high[...], ((1,), (0,)))
            )
        outs = refs[2 * count + len(scales) :]
        if mode == "plain":
            for out, value in zip(outs, made):
                out[...] = value.astype(bf16)
        elif mode == "gelu":
            gate, up = made
            square = gate * gate
            bend = jnp.tanh(tanh_rate * gate * (1.0 + tanh_cube * square))
            rise = 0.5 * (1.0 + bend)
            value = gate * rise
            slope = rise + 0.5 * gate * (1.0 - bend * bend) * tanh_rate * (1.0 + 3.0 * tanh_cube * square)
            outs[0][...] = (value * up).astype(bf16)
            outs[1][...] = (slope * up).astype(bf16)
            outs[2][...] = value.astype(bf16)
        else:
            for j, out in enumerate(outs):
                out[...] = (made[j // 2] * refs[2 * count + j][...].astype(f32)).astype(bf16)

    by_rows = lambda width: spec((size, width), lambda i: (i, 0))
    width_all = own.shape[1]
    return pl.pallas_call(
        kernel,
        grid=(4,),
        in_specs=[
            spec((size, width_all), lambda i: (jnp.minimum(i, 1), 0)),
            spec((size, width_all), lambda i: (jnp.maximum(i - 2, 0), 0)),
            *specs,
            *[by_rows(t.shape[1]) for t in scales],
        ],
        out_specs=[by_rows(w) for w in out_widths],
        out_shape=[jax.ShapeDtypeStruct((2 * half, w), bf16) for w in out_widths],
        compiler_params=pltpu.CompilerParams(vmem_limit_bytes=vmem_room),
        cost_estimate=cost(4 * half * width_all * sum(widths), half * width_all * 4 + width_all * sum(widths) * 2),
        name="project_" + mode,
    )(own, other, *arrays, *scales)


def combine(values, weights, which):
    specs, arrays = weight_specs(weights)
    half = values[0].shape[0] // 2
    size = half // 2
    count = len(values)
    depth = weights[0][0].shape[0]

    def kernel(*refs):
        for side in range(2):
            parts = [
                dot(refs[j][...], refs[count + 2 * j + side][...], ((1,), (1,))) for j in range(count)
            ]
            refs[side - 2][...] = total(parts)

    return pl.pallas_call(
        kernel,
        grid=(2,),
        in_specs=[spec((size, v.shape[1]), lambda i: (2 * which + i, 0)) for v in values] + specs,
        out_specs=[spec((size, depth), lambda i: (i, 0))] * 2,
        out_shape=[jax.ShapeDtypeStruct((half, depth), f32)] * 2,
        compiler_params=pltpu.CompilerParams(vmem_limit_bytes=vmem_room),
        cost_estimate=cost(0, 0),
        name="combine",
    )(*values, *arrays)


def weight_grad(items, part, arrived=()):
    sources = []
    for rows, _ in items:
        if not any(rows is t for t in sources):
            sources.append(rows)
    half, width = sources[0][0].shape
    size = width // 2
    steps, base = (2, 0) if part is None else (1, part)
    spans, last = [], 0
    for _, value in items:
        spans.append((last, last + value.shape[1]))
        last = spans[-1][1]
    first = len(sources) * 2

    def kernel(*refs):
        out = refs[-1]
        for (rows, _), value, (a, b) in zip(items, refs[first:], spans):
            place = [rows is t for t in sources].index(True)
            own, other = refs[2 * place], refs[2 * place + 1]
            made = dot(own[...], value[:half], ((0,), (0,))) + dot(other[...], value[half:], ((0,), (0,)))
            for (array, _, start), came in zip(arrived, refs[first + len(items) :]):
                if start <= a < start + array.shape[1]:
                    made = made + came[:, a - start : b - start].astype(f32)
            out[:, a:b] = made.astype(bf16)

    columns = spec((half, size), lambda i: (0, base + i))
    return pl.pallas_call(
        kernel,
        grid=(steps,),
        in_specs=[columns] * first
        + [spec(v.shape, lambda i: (0, 0)) for _, v in items]
        + [spec((size, a.shape[1]), lambda i, place=place: (place + i, 0)) for a, place, _ in arrived],
        out_specs=spec((size, last), lambda i: (i, 0)),
        out_shape=jax.ShapeDtypeStruct((steps * size, last), bf16),
        compiler_params=pltpu.CompilerParams(vmem_limit_bytes=vmem_room),
        cost_estimate=cost(4 * half * steps * size * last, half * width * 4 + half * 4 * last),
        name="weight_grad",
    )(*[t for pair in sources for t in pair], *[v for _, v in items], *[a for a, _, _ in arrived])


def halves(parts):
    return [t for p in parts for t in (p if isinstance(p, (list, tuple)) else [p])]


def read_total(parts, refs):
    refs, read = list(refs), []
    for p in parts:
        if isinstance(p, (list, tuple)):
            read.append(jnp.concatenate([refs.pop(0)[...] for _ in p], axis=1))
        else:
            read.append(refs.pop(0)[...])
    return total([r.astype(f32) for r in read])


def by_rows(array, size=256):
    if array.shape[0] == 1:
        return spec(array.shape, lambda i: (0, 0))
    return spec((size, array.shape[1]), lambda i: (i, 0))


def add_norm(parts, gain_row):
    arrays = halves(parts)
    rows, width = arrays[0].shape[0], D

    def kernel(gain_ref, *refs):
        hidden = read_total(parts, refs[: len(arrays)])
        scale = lax.rsqrt(jnp.mean(hidden * hidden, axis=-1, keepdims=True) + epsilon)
        refs[-1][...] = (hidden * scale * gain_ref[...]).astype(bf16)
        if len(parts) > 1:
            refs[-2][...] = hidden

    kinds = [f32, bf16] if len(parts) > 1 else [bf16]
    shapes = [jax.ShapeDtypeStruct((rows, width), k) for k in kinds]
    return pl.pallas_call(
        kernel,
        grid=(rows // 256,),
        in_specs=[by_rows(gain_row), *[by_rows(p) for p in arrays]],
        out_specs=[by_rows(t) for t in shapes],
        out_shape=shapes,
        compiler_params=pltpu.CompilerParams(vmem_limit_bytes=vmem_room),
        cost_estimate=cost(rows * width * 8, rows * width * 14),
        name="add_norm",
    )(gain_row, *arrays)


def norm_back(hidden, gain_row, grads, base):
    rows, width = hidden.shape
    arrays = halves(grads)

    def kernel(gain_ref, hidden_ref, base_ref, *refs):
        grad = read_total(grads, refs[: len(arrays)])
        out, low, gain_grad = refs[len(arrays) :]
        hidden = hidden_ref[...].astype(f32)
        scale = lax.rsqrt(jnp.mean(hidden * hidden, axis=-1, keepdims=True) + epsilon)
        z = hidden * scale
        grad_z = grad * gain_ref[...]
        grad_hidden = scale * (grad_z - z * jnp.mean(grad_z * z, axis=-1, keepdims=True))
        value = base_ref[...].astype(f32) + grad_hidden
        out[...] = value
        low[...] = value.astype(bf16)

        @pl.when(pl.program_id(0) == 0)
        def _():
            gain_grad[...] = jnp.zeros_like(gain_grad)

        gain_grad[...] += jnp.sum(grad * z, axis=0, keepdims=True)

    shapes = [jax.ShapeDtypeStruct((rows, width), f32), jax.ShapeDtypeStruct((rows, width), bf16)]
    return pl.pallas_call(
        kernel,
        grid=(rows // 256,),
        in_specs=[by_rows(gain_row), by_rows(hidden), by_rows(base), *[by_rows(g) for g in arrays]],
        out_specs=[*[by_rows(t) for t in shapes], spec((1, width), lambda i: (0, 0))],
        out_shape=[*shapes, jax.ShapeDtypeStruct((1, width), f32)],
        compiler_params=pltpu.CompilerParams(vmem_limit_bytes=vmem_room),
        cost_estimate=cost(rows * width * 16, rows * width * 22),
        name="norm_back",
    )(gain_row, hidden, base, *arrays)


def after(value, *others):
    return lax.optimization_barrier((value, *others))[0]


def swap_cores(values):
    return lax.ppermute(values, "mc", swap)


def swap_x(values):
    return row_major(lax.ppermute(row_major(values), "mx", swap))


def swap_y(values):
    return row_major(lax.ppermute(row_major(values), "dy", swap))


def gather_part(local):
    return row_major(lax.all_gather(row_major(local), "dz", axis=0, tiled=True))


def spread(part, x_last):
    if x_last:
        high = swap_y(part)
        return (part, high), (swap_x(part), swap_x(high))
    beside = swap_x(part)
    return (part, swap_y(part)), (beside, swap_y(beside))


def pieces(value, count):
    made = []
    for _ in range(count):
        made.append(value.astype(bf16))
        value = value - made[-1].astype(f32)
    return made


class Group:
    def __init__(self, x_items, y_items):
        self.own = [(r, v) for r, v, _ in (*x_items, *y_items)]
        self.own_x, self.own_y = self.own[: len(x_items)], self.own[len(x_items) :]
        self.other_x, self.other_y = ([(r, v) for r, _, v in items] for items in (x_items, y_items))

    def first(self, *deps):
        self.sent = [weight_grad(self.other_x, None), weight_grad([*self.own_y, *self.other_y], 1)]
        to_x, to_y = (after(t, *deps) if deps else t for t in self.sent)
        self.from_x, self.from_y = swap_x(to_x), swap_y(to_y)
        return self.sent

    def second(self, *deps):
        self.from_x, self.from_y = after(self.from_x, *deps), after(self.from_y, *deps)
        wide_y = self.from_y.shape[1] // 2
        self.sent = [
            weight_grad(self.own_x, 1, [(self.from_x, 1, 0)]),
            weight_grad(self.other_y, 0, [(self.from_y, 0, -wide_y)]),
        ]
        self.late_y, self.late_x = swap_y(self.sent[0]), swap_x(self.sent[1])
        return self.sent

    def third(self, *deps, behind=()):
        wide_x = self.from_x.shape[1]
        late_y, late_x = after(self.late_y, *deps), after(self.late_x, *deps)
        summed = weight_grad(
            self.own, 0, [(self.from_x, 0, 0), (late_y, 0, 0), (self.from_y, 0, wide_x), (late_x, 0, wide_x)]
        )
        self.sent = [summed]
        summed = after(summed, *behind) if behind else summed
        self.low = lax.psum_scatter(row_major(summed), "dz", scatter_dimension=0, tiled=True)
        self.result = self.low.astype(f32)
        return self.sent


def on_device(
    tokens,
    encoder,
    cotangent,
    lengths,
    deal,
    attn_in,
    attn_out,
    ff_in,
    ff_out,
    gains,
    mom_attn_in,
    mom_attn_out,
    mom_ff_in,
    mom_ff_out,
    mom_gains,
    avg_attn_in,
    avg_attn_out,
    avg_ff_in,
    avg_ff_out,
    avg_gains,
):
    seq_count, block_rows = tokens.shape[0], tokens.shape[1]
    core = lax.axis_index("mc")
    dy = lax.axis_index("dy")
    chip = lax.axis_index(chips)
    own_rows = block_rows * seq_count
    slot_len = 2 * own_rows
    heads_cols = attn_in.shape[2]
    hidden = ff_in.shape[2]
    model_rows = attn_in.shape[1]

    def exchange(values):
        return lax.all_to_all(values, chips, split_axis=0, concat_axis=0, tiled=True)

    def to_chips(values):
        return exchange(values).reshape(own_rows, D)

    def from_chips(rows):
        return exchange(rows.reshape(seq_count, block_rows, D))

    seq_len = lengths[deal[chip]]
    row_ids = jnp.arange(own_rows, dtype=jnp.int32)
    lane = row_ids % block_rows
    pos_own = (row_ids // block_rows * 2 + core) * block_rows + lane
    pos_other = (row_ids // block_rows * 2 + 1 - core) * block_rows + lane
    pos = jnp.concatenate([pos_own, pos_other])
    places = (pos[:, None], pos[None, :])
    length = seq_len[None]
    valid_own = (pos_own < seq_len).astype(f32)[:, None]

    hc = heads_cols
    pairs = hc // (2 * DK)
    spare = -hidden % 256
    deep = hidden + spare
    widen = lambda t: jnp.pad(t.astype(bf16), ((0, 0), (0, spare)))
    out_t = jnp.swapaxes(attn_out.astype(bf16), 1, 2)
    low_in = attn_in.astype(bf16)
    pad = jnp.zeros((model_rows, 125), bf16)
    chunk_a = jnp.concatenate([*low_in[0:3], out_t[0], gains.astype(bf16).T, pad], axis=1)
    chunk_b = jnp.concatenate([*low_in[3:6], out_t[1]], axis=1)
    chunk_c = jnp.concatenate([widen(ff_in[0]), widen(ff_in[1]), widen(ff_out.T)], axis=1)

    part_a, part_b, part_c = (gather_part(t) for t in (chunk_a, chunk_b, chunk_c))
    got_a = spread(part_a, True)
    tok_own = to_chips(after(tokens, part_a))
    cot_own = to_chips(cotangent)

    gain_f = jnp.concatenate([g[:, 4 * hc : 4 * hc + 3] for g in got_a[0]]).astype(f32).T
    gain_rows = [gain_f[n : n + 1] for n in range(3)]
    w_qkv = [(*g, 3 * hc, 0) for g in got_a]
    w_q, w_k, w_v, w_ot = ([(*g, hc, n) for g in got_a] for n in range(4))

    def both(own):
        return own, swap_cores(own)

    def over_cores(values, weights):
        away = [swap_cores(t) for t in combine(values, weights, 1)]
        return combine(values, weights, 0), away

    x_own = reorder([after(tok_own, chunk_b, chunk_c)], model_rows, dy, True)
    norm_one = both(add_norm([x_own], gain_rows[0])[0])
    norm_one = after(norm_one[0], part_b), norm_one[1]
    qkv = [project(norm_one, [w_qkv[0]])[0]]
    self_qkv = [[(qkv[0], n * pairs, pairs) for n in range(3)]]
    self_out = [attend(*self_qkv[0], *places, length, True, 256)]
    qkv += project((after(norm_one[0], self_out[0][0]), norm_one[1]), [w_qkv[1]])
    self_qkv += [[(qkv[1], n * pairs, pairs) for n in range(3)]]
    high_b, beside_b = swap_y(part_b), swap_x(part_b)
    self_out += [attend(*self_qkv[1], *places, length, True, 256)]
    far_b = swap_y(after(beside_b, self_out[1][0], high_b))
    got_b = (part_b, high_b), (beside_b, far_b)
    w_cq, w_ck, w_cv, w_cot = ([(*g, hc, n) for g in got_b] for n in range(4))

    enc_own = to_chips(after(encoder, part_c, self_out[1][0]))
    part_c = after(part_c, self_out[1][0], far_b)
    high_c, beside_c = swap_y(part_c), swap_x(part_c)
    far_gu, far_d = swap_x(high_c[:, : 2 * deep]), swap_y(beside_c[:, 2 * deep :])
    w_g, w_u, w_dt = (
        [(part_c, high_c, deep, n), (beside_c, far, deep, n, place)]
        for n, far, place in ((0, far_gu, 0), (1, far_gu, 1), (2, far_d, 0))
    )

    self_mixed = [o[0] for o in self_out]
    hidden_one, norm_two = add_norm([x_own, *over_cores(self_mixed, w_ot)], gain_rows[1])
    norm_two = both(norm_two)
    e_own = reorder([enc_own], model_rows, dy, True)
    enc_rows = both(e_own)
    cross_kv = project(enc_rows, [*w_ck, *w_cv])
    cross_q = project(norm_two, w_cq)
    cross_qkv = [
        [(t, 0, pairs) for t in (cross_q[n], cross_kv[n], cross_kv[2 + n])] for n in range(2)
    ]
    cross_qkv[0][0] = (after(cross_q[0], cross_q[1], high_c, beside_c), 0, pairs)
    cross_out = [attend(*t, *places, length, False, 512) for t in cross_qkv]
    cross_mixed = [o[0] for o in cross_out]
    hidden_two, norm_three = add_norm(
        [hidden_one, *over_cores(cross_mixed, w_cot)], gain_rows[2]
    )
    norm_three = both(norm_three)
    dy_own = reorder([cot_own], model_rows, dy, True, valid_own)
    grad_out = both(dy_own)
    inner, slope, value = zip(*[project(norm_three, list(w), "gelu") for w in zip(w_g, w_u)])

    scales = [t for pair in zip(slope, value) for t in pair]
    grad_gu = project(grad_out, w_dt, "scale", scales)
    grad_gate, grad_up = grad_gu[::2], grad_gu[1::2]
    group_c = Group([(norm_three, *grad_gate), (grad_out, *inner)], [(norm_three, *grad_up)])
    sent = group_c.first()
    parts = over_cores([after(grad_gate[0], *sent), grad_gate[1], *grad_up], [*w_g, *w_u])
    grad_two, low_two, gain_three = norm_back(hidden_two, gain_rows[2], parts, dy_own)
    grad_co = both(low_two)
    out_parts = over_cores([after(inner[0], low_two), inner[1]], w_dt)
    grad_ca = project((after(grad_co[0], out_parts[0][0]), grad_co[1]), w_cot)
    out_block = reorder([after(hidden_two, *grad_ca), *out_parts], model_rows, dy, False, valid_own)
    block_output = from_chips(out_block)
    cross_back = [attend_back(*cross_qkv[0], *places, cross_out[0][1], after(grad_ca[0], out_block), False, 512)]
    grad_late = after(grad_ca[1], group_c.from_y, *cross_back[0])
    cross_back += [attend_back(*cross_qkv[1], *places, cross_out[1][1], grad_late, False, 512)]
    grad_cq, grad_ck, grad_cv = zip(*cross_back)
    sent = group_c.second(*grad_cq)
    grad_cq = (after(grad_cq[0], *sent), grad_cq[1])
    group_b = Group(
        [(norm_two, *grad_cq), (grad_co, *[o[0] for o in cross_out])],
        [(enc_rows, *grad_ck), (enc_rows, *grad_cv)],
    )
    parts = over_cores(grad_cq, w_cq)
    sent = group_b.first()
    parts_enc = over_cores([after(grad_ck[0], *sent), grad_ck[1], *grad_cv], [*w_ck, *w_cv])
    grad_one, low_one, gain_two = norm_back(
        hidden_one, gain_rows[1], [parts[0], [after(parts[1][0], parts_enc[0][0]), parts[1][1]]], grad_two
    )
    grad_o = both(low_one)
    out_enc = reorder([parts_enc[0], [after(parts_enc[1][0], low_one), parts_enc[1][1]]], model_rows, dy, False)
    grad_encoder = from_chips(out_enc)
    grad_a = project((after(grad_o[0], out_enc, block_output), grad_o[1]), w_ot)
    self_back = [attend_back(*self_qkv[0], *places, self_out[0][1], grad_a[0], True, 256)]
    sent = group_c.third(*self_back[0])
    self_back.append(attend_back(*self_qkv[1], *places, self_out[1][1], after(grad_a[1], *sent), True, 256))
    sent = group_b.second(*self_back[1])
    self_back[1] = [*[after(t, *sent) for t in self_back[1][:2]], self_back[1][2]]
    grad_q, grad_k, grad_v = zip(*self_back)
    group_a = Group(
        [(norm_one, *grad_q), (grad_o, *[o[0] for o in self_out])],
        [(norm_one, *grad_k), (norm_one, *grad_v)],
    )
    sent = group_a.first(group_b.late_x, group_b.late_y)
    sent = [*sent, *group_b.third(*sent, behind=[group_c.low])]
    parts = over_cores(
        [after(grad_q[0], *sent, grad_encoder), grad_q[1], *grad_k, *grad_v], [*w_q, *w_k, *w_v]
    )
    _, low_tok, gain_one = norm_back(
        x_own, gain_rows[0], [[after(parts[0][0], *sent), parts[0][1]], parts[1]], grad_one
    )
    group_a.second(low_tok)
    out_tok = reorder([after(low_tok, *group_a.sent)], model_rows, dy, False)
    dp_count = seq_count // 2
    gain_part = jnp.concatenate([gain_one, gain_two, gain_three])
    parts = [gain_part[:, n * D // 2 : (n + 1) * D // 2].reshape(3, dp_count // 2, model_rows) for n in range(2)]
    gain_part = jnp.stack([jnp.where(dy == 0, *parts), jnp.where(dy == 0, *parts[::-1])], axis=2)
    gain_part = jnp.swapaxes(gain_part.reshape(3, dp_count, model_rows), 0, 1).reshape(dp_count, -1)
    mx = lax.axis_index("mx")
    tops = jnp.stack([jnp.where(mx == n, self_out[0][2], self_out[1][2]) for n in range(2)])
    tops = jnp.broadcast_to(tops[None], (dp_count, *tops.shape)).reshape(seq_count, -1)
    small = jnp.concatenate([*pieces(jnp.repeat(gain_part, 2, axis=0), 2), *pieces(tops, 3)], axis=1)
    small = jnp.pad(small, ((0, 0), (0, D - small.shape[1])))[:, None]
    sent = jnp.concatenate([out_tok.reshape(seq_count, block_rows, D), small], axis=1)
    came = exchange(sent)
    grad_tokens, small = came[:, :block_rows], came[:, block_rows].astype(f32)
    group_a.third(out_tok, behind=[group_b.low])
    sum_a, sum_b, sum_c = group_a.result, group_b.result, group_c.result

    small = after(small, group_a.low)
    wide = 3 * model_rows
    red_gain = jnp.sum(small[:, :wide] + small[:, wide : 2 * wide], axis=0).reshape(3, model_rows)
    red_gain = red_gain + swap_cores(red_gain)
    tops = small[:, 2 * wide : 2 * wide + 3 * (hc // DK)].reshape(seq_count, 3, -1)
    head_peak = jnp.max(tops[:, 0] + tops[:, 1] + tops[:, 2], axis=0)

    cut = lambda t, n: t[:, n * hc : (n + 1) * hc]
    red_in = jnp.stack([cut(t, n) for t in (sum_a, sum_b) for n in (0, 2, 3)])
    red_out = jnp.stack([cut(sum_a, 1).T, cut(sum_b, 1).T])
    red_ff = jnp.stack([sum_c[:, n * deep : n * deep + hidden] for n in (0, 2)])
    red_in = row_major(red_in)
    red_out = with_layout_constraint(red_out, Layout(major_to_minor=(0, 1, 2)))
    red_ff = with_layout_constraint(red_ff, Layout(major_to_minor=(0, 2, 1)))
    red_down = with_layout_constraint(sum_c[:, deep : deep + hidden].T, Layout(major_to_minor=(0, 1)))
    clip_factors = clip_limit / jnp.maximum(head_peak, clip_limit)
    column = jnp.repeat(jnp.sqrt(clip_factors), DK)
    factor = jnp.where((jnp.arange(6) < 2)[:, None, None], column[None, None, :], 1.0)
    grad_scale = float(seq_count * slot_len) ** (-0.5)
    up_a = apply_update(attn_in, red_in, mom_attn_in, avg_attn_in, factor, grad_scale)
    up_b = apply_update(attn_out, red_out, mom_attn_out, avg_attn_out, 1.0, grad_scale)
    up_c = apply_update(ff_in, red_ff, mom_ff_in, avg_ff_in, 1.0, grad_scale)
    up_d = apply_update(ff_out, red_down, mom_ff_out, avg_ff_out, 1.0, grad_scale)
    up_e = apply_update(gains, red_gain, mom_gains, avg_gains, 1.0, grad_scale)
    return (
        block_output.astype(f32),
        grad_tokens.astype(f32),
        grad_encoder.astype(f32),
        *up_a,
        *up_b,
        *up_c,
        *up_d,
        *up_e,
        head_peak,
        clip_factors,
    )


def solution(mesh):
    dp, mp = mesh.shape["dp"], mesh.shape["mp"]
    fine = Mesh(mesh.devices.reshape(dp // 2, 2, mp // 2, 2), ("dz", "dy", "mx", "mc"))
    dp_axes, mp_axes = ("dz", "dy"), ("mx", "mc")
    rows = P(None, (*dp_axes, *mp_axes), None)
    wide = P(None, dp_axes, mp_axes)
    tall = P(None, mp_axes, dp_axes)
    down = P(mp_axes, dp_axes)
    gain = P(None, dp_axes)
    state = (wide, tall, wide, down, gain)
    in_specs = (rows, rows, rows, P(), P(), *state, *state, *state)
    out_specs = (
        rows,
        rows,
        rows,
        *[wide] * 4,
        *[tall] * 4,
        *[wide] * 4,
        *[down] * 4,
        *[gain] * 4,
        P(mp_axes),
        P(mp_axes),
    )
    return jax.shard_map(
        on_device, mesh=fine, in_specs=in_specs, out_specs=out_specs, check_vma=False
    )
```

```python
import functools

import jax
import jax.numpy as jnp
from jax import lax
from jax.experimental import pallas as pl
from jax.experimental.layout import Layout, with_layout_constraint
from jax.experimental.pallas import tpu as pltpu
from jax.sharding import Mesh, PartitionSpec as P

D = 1024
DK = 64

epsilon = 1e-06
clip_limit = 10.0
momentum_rate = 0.9
learn_rate = 0.01
average_rate = 0.5
neg_large = -1e30
vmem_room = 24 << 20
tanh_rate = 0.7978845608
tanh_cube = 0.044715
bf16 = jnp.bfloat16
f32 = jnp.float32
swap = ((0, 1), (1, 0))
chips = ("dz", "dy", "mx")


def dot(left, right, dims):
    return lax.dot_general(left, right, (dims, ((), ())), preferred_element_type=f32)


def head_lanes(block, head):
    lanes = lax.broadcasted_iota(jnp.int32, block.shape, 1)
    return jnp.where((lanes >= DK) == (head == 1), block, jnp.zeros_like(block))


def key_spans(rows, keys, start, size, causal):
    half = rows // 2
    reach = start % half + size
    return [(0, reach), (half, half + reach)] if causal and reach < half else [(0, keys)]


def total(parts):
    return functools.reduce(jnp.add, parts)


def attend_kernel(causal, size, q_ref, k_ref, v_ref, pq_ref, pk_ref, len_ref, o_ref, lse_ref, top_ref):
    rows, keys = q_ref.shape[0], k_ref.shape[0]
    tops = []
    for head in range(2):
        k, v = head_lanes(k_ref[...], head), head_lanes(v_ref[...], head)
        top = jnp.full((1, 1), neg_large, f32)
        for start in range(0, rows, size):
            r = slice(start, start + size)
            spans = key_spans(rows, keys, start, size, causal)
            q = q_ref[r, :]
            s = [dot(q, k[a:b], ((1,), (1,))) for a, b in spans]
            if causal:
                s = [jnp.where(pk_ref[:, a:b] <= pq_ref[r, :], t, neg_large) for t, (a, b) in zip(s, spans)]
            m = functools.reduce(jnp.maximum, [jnp.max(t, axis=1, keepdims=True) for t in s])
            if causal:
                real = jnp.where(pq_ref[r, :] < len_ref[0], m, neg_large)
                top = jnp.maximum(top, jnp.max(real, axis=0, keepdims=True))
            e = [jnp.exp(t - m) for t in s]
            mass = total([jnp.sum(t, axis=1, keepdims=True) for t in e])
            scale = 1.0 / mass
            mix = total([dot((t * scale).astype(bf16), v[a:b], ((1,), (0,))) for t, (a, b) in zip(e, spans)])
            if head == 0:
                o_ref[r, :] = mix.astype(bf16)
            else:
                o_ref[r, :] = (o_ref[r, :].astype(f32) + mix).astype(bf16)
            lse_ref[0, r, head : head + 1] = m + jnp.log(mass)
        tops.append(top)
    lanes = lax.broadcasted_iota(jnp.int32, (8, 128), 1)
    top_ref[0] = jnp.where(lanes == 0, tops[0], tops[1])


def attend_back_kernel(
    causal, size, q_ref, k_ref, v_ref, pq_ref, pk_ref, lse_ref, do_ref, dq_ref, dk_ref, dv_ref, dk_acc, dv_acc
):
    rows, keys = q_ref.shape[0], k_ref.shape[0]
    dk_acc[...] = jnp.zeros_like(dk_acc)
    dv_acc[...] = jnp.zeros_like(dv_acc)
    for head in range(2):
        k, v = head_lanes(k_ref[...], head), head_lanes(v_ref[...], head)
        own = slice(DK * head, DK * head + DK)
        for start in range(0, rows, size):
            r = slice(start, start + size)
            spans = key_spans(rows, keys, start, size, causal)
            q, do, lse = q_ref[r, :], do_ref[r, :], lse_ref[0, r, head : head + 1]
            soft, grad = [], []
            for a, b in spans:
                s = dot(q, k[a:b], ((1,), (1,)))
                if causal:
                    s = jnp.where(pk_ref[:, a:b] <= pq_ref[r, :], s, neg_large)
                soft.append(jnp.exp(s - lse))
                grad.append(dot(do, v[a:b], ((1,), (1,))))
            row_dot = total([jnp.sum(p * t, axis=1, keepdims=True) for p, t in zip(soft, grad)])
            q_t, do_t = q.T[own], do.T[own]
            parts = []
            for (a, b), p, t in zip(spans, soft, grad):
                ds = (p * (t - row_dot)).astype(bf16)
                parts.append(dot(ds, k[a:b], ((1,), (0,))))
                dv_acc[own, a:b] += dot(do_t, p.astype(bf16), ((1,), (0,)))
                dk_acc[own, a:b] += dot(q_t, ds, ((1,), (0,)))
            dq = total(parts)
            if head == 0:
                dq_ref[r, :] = dq.astype(bf16)
            else:
                dq_ref[r, :] = (dq_ref[r, :].astype(f32) + dq).astype(bf16)
    dk_ref[...] = dk_acc[...].T.astype(bf16)
    dv_ref[...] = dv_acc[...].T.astype(bf16)


def attend_cost(rows, keys, pairs, dots):
    return cost(0, 0)


def lane_pairs(count, first):
    return pl.BlockSpec((count, 2 * DK), lambda p: (0, first + p))


def attend(q, k, v, pos_col, pos_row, length, causal, size):
    rows, keys, pairs = q[0].shape[0], k[0].shape[0], q[2]
    mixed, lse, top = pl.pallas_call(
        functools.partial(attend_kernel, causal, size),
        grid=(pairs,),
        in_specs=[
            lane_pairs(rows, q[1]),
            lane_pairs(keys, k[1]),
            lane_pairs(keys, v[1]),
            pl.BlockSpec((rows, 1), lambda p: (0, 0)),
            pl.BlockSpec((1, keys), lambda p: (0, 0)),
            pl.BlockSpec(memory_space=pltpu.SMEM),
        ],
        out_specs=[
            lane_pairs(rows, 0),
            pl.BlockSpec((1, rows, 2), lambda p: (p, 0, 0)),
            pl.BlockSpec((1, 8, 128), lambda p: (p, 0, 0)),
        ],
        out_shape=[
            jax.ShapeDtypeStruct((rows, pairs * 2 * DK), bf16),
            jax.ShapeDtypeStruct((pairs, rows, 2), f32),
            jax.ShapeDtypeStruct((pairs, 8, 128), f32),
        ],
        compiler_params=pltpu.CompilerParams(vmem_limit_bytes=vmem_room),
        cost_estimate=attend_cost(rows, keys, pairs, 2),
        name="attend",
    )(q[0], k[0], v[0], pos_col, pos_row, length)
    return mixed, lse, top[:, 0, :2].reshape(-1)


def attend_back(q, k, v, pos_col, pos_row, lse, grad, causal, size):
    rows, keys, pairs = q[0].shape[0], k[0].shape[0], q[2]
    return pl.pallas_call(
        functools.partial(attend_back_kernel, causal, size),
        grid=(pairs,),
        in_specs=[
            lane_pairs(rows, q[1]),
            lane_pairs(keys, k[1]),
            lane_pairs(keys, v[1]),
            pl.BlockSpec((rows, 1), lambda p: (0, 0)),
            pl.BlockSpec((1, keys), lambda p: (0, 0)),
            pl.BlockSpec((1, rows, 2), lambda p: (p, 0, 0)),
            lane_pairs(rows, 0),
        ],
        out_specs=[lane_pairs(rows, 0), lane_pairs(keys, 0), lane_pairs(keys, 0)],
        out_shape=[jax.ShapeDtypeStruct((n, pairs * 2 * DK), bf16) for n in (rows, keys, keys)],
        scratch_shapes=[pltpu.VMEM((2 * DK, keys), f32)] * 2,
        compiler_params=pltpu.CompilerParams(vmem_limit_bytes=vmem_room),
        cost_estimate=attend_cost(rows, keys, pairs, 5),
        name="attend_back",
    )(q[0], k[0], v[0], pos_col, pos_row, lse, grad)


def apply_update(weight, grad_sum, moment, average, factor, grad_scale):
    grad_now = grad_sum * grad_scale
    moment_new = momentum_rate * moment + grad_now
    master_new = (weight - learn_rate * (grad_now + momentum_rate * moment_new)) * factor
    average_new = average_rate * average + (1.0 - average_rate) * master_new
    return (grad_now, moment_new, average_new, master_new)


def flat_columns(block):
    return jnp.swapaxes(block, 0, 1).reshape(block.shape[1], -1)


def row_major(values):
    return with_layout_constraint(values, Layout(major_to_minor=tuple(range(values.ndim))))


spec = pl.BlockSpec


def cost(flops, moved):
    return pl.CostEstimate(flops=1, bytes_accessed=1, transcendentals=0)


def reorder(parts, block, dy, to_own, keep=None):
    arrays = halves(parts)
    rows, width = arrays[0].shape[0], D
    steps = width // block // 2
    extra = [] if keep is None else [keep]
    if block % 128:
        value = total([(jnp.concatenate(p, axis=1) if isinstance(p, (list, tuple)) else p).astype(f32) for p in parts])
        value = value * (1.0 if keep is None else keep)
        axis = 2 if to_own else 1
        value = value.reshape((rows, steps, 2, block) if to_own else (rows, 2, steps, block))
        low, high = (lax.index_in_dim(value, n, axis, keepdims=False) for n in range(2))
        pair = jnp.where(dy == 0, low, high), jnp.where(dy == 0, high, low)
        return jnp.stack(pair, axis=3 - axis).reshape(rows, width).astype(bf16)

    def source(j, flag):
        if to_own:
            return j % steps * 2 + (j // steps + flag) % 2
        return j // 2 + (j % 2 + flag) % 2 * steps

    def kernel(flag_ref, *refs):
        out = refs[-1]
        whole = len(arrays) == 1
        value = refs[0] if whole else read_total(parts, refs[: len(arrays)])
        for j in range(2 * steps):
            spans = [slice(source(j, flag) * block, (source(j, flag) + 1) * block) for flag in range(2)]
            picked = jnp.where(flag_ref[0] == 0, value[:, spans[0]], value[:, spans[1]])
            if extra:
                picked = picked.astype(f32) * refs[len(arrays)][...]
            out[:, j * block : (j + 1) * block] = picked.astype(bf16)

    return pl.pallas_call(
        kernel,
        grid=(4,),
        in_specs=[
            spec(memory_space=pltpu.SMEM),
            *[by_rows(p, rows // 4) for p in [*arrays, *extra]],
        ],
        out_specs=spec((rows // 4, width), lambda i: (i, 0)),
        out_shape=jax.ShapeDtypeStruct((rows, width), bf16),
        compiler_params=pltpu.CompilerParams(vmem_limit_bytes=vmem_room),
        cost_estimate=cost(0, rows * width * 4),
        name="reorder",
    )(dy[None], *arrays, *extra)


def weight_specs(weights):
    specs, arrays = [], []
    for own, other, width, *places in weights:
        for array, place in zip((own, other), (places[0], places[-1])):
            specs.append(spec((array.shape[0], width), lambda i, place=place: (0, place)))
            arrays.append(array)
    return specs, arrays


def project(rows, weights, mode="plain", scales=()):
    own, other = rows
    half, size = own.shape[0], own.shape[0] // 2
    specs, arrays = weight_specs(weights)
    widths = [w[2] for w in weights]
    count = len(weights)
    out_widths = {"plain": widths, "gelu": widths[:1] * 3, "scale": [w for w in widths for _ in range(2)]}[mode]

    def kernel(own_ref, other_ref, *refs):
        here = pl.program_id(0) < 2
        x = jnp.where(here, own_ref[...], other_ref[...])
        split = x.shape[1] // 2
        made = []
        for j in range(count):
            low, high = refs[2 * j], refs[2 * j + 1]
            made.append(
                dot(x[:, :split], low[...], ((1,), (0,))) + dot(x[:, split:], high[...], ((1,), (0,)))
            )
        outs = refs[2 * count + len(scales) :]
        if mode == "plain":
            for out, value in zip(outs, made):
                out[...] = value.astype(bf16)
        elif mode == "gelu":
            gate, up = made
            square = gate * gate
            bend = jnp.tanh(tanh_rate * gate * (1.0 + tanh_cube * square))
            rise = 0.5 * (1.0 + bend)
            value = gate * rise
            slope = rise + 0.5 * gate * (1.0 - bend * bend) * tanh_rate * (1.0 + 3.0 * tanh_cube * square)
            outs[0][...] = (value * up).astype(bf16)
            outs[1][...] = (slope * up).astype(bf16)
            outs[2][...] = value.astype(bf16)
        else:
            for j, out in enumerate(outs):
                out[...] = (made[j // 2] * refs[2 * count + j][...].astype(f32)).astype(bf16)

    by_rows = lambda width: spec((size, width), lambda i: (i, 0))
    width_all = own.shape[1]
    return pl.pallas_call(
        kernel,
        grid=(4,),
        in_specs=[
            spec((size, width_all), lambda i: (jnp.minimum(i, 1), 0)),
            spec((size, width_all), lambda i: (jnp.maximum(i - 2, 0), 0)),
            *specs,
            *[by_rows(t.shape[1]) for t in scales],
        ],
        out_specs=[by_rows(w) for w in out_widths],
        out_shape=[jax.ShapeDtypeStruct((2 * half, w), bf16) for w in out_widths],
        compiler_params=pltpu.CompilerParams(vmem_limit_bytes=vmem_room),
        cost_estimate=cost(4 * half * width_all * sum(widths), half * width_all * 4 + width_all * sum(widths) * 2),
        name="project_" + mode,
    )(own, other, *arrays, *scales)


def combine(values, weights, which):
    specs, arrays = weight_specs(weights)
    half = values[0].shape[0] // 2
    size = half // 2
    count = len(values)
    depth = weights[0][0].shape[0]

    def kernel(*refs):
        for side in range(2):
            parts = [
                dot(refs[j][...], refs[count + 2 * j + side][...], ((1,), (1,))) for j in range(count)
            ]
            refs[side - 2][...] = total(parts)

    return pl.pallas_call(
        kernel,
        grid=(2,),
        in_specs=[spec((size, v.shape[1]), lambda i: (2 * which + i, 0)) for v in values] + specs,
        out_specs=[spec((size, depth), lambda i: (i, 0))] * 2,
        out_shape=[jax.ShapeDtypeStruct((half, depth), f32)] * 2,
        compiler_params=pltpu.CompilerParams(vmem_limit_bytes=vmem_room),
        cost_estimate=cost(0, 0),
        name="combine",
    )(*values, *arrays)


def weight_grad(items, part, arrived=()):
    sources = []
    for rows, _ in items:
        if not any(rows is t for t in sources):
            sources.append(rows)
    half, width = sources[0][0].shape
    size = width // 2
    steps, base = (2, 0) if part is None else (1, part)
    spans, last = [], 0
    for _, value in items:
        spans.append((last, last + value.shape[1]))
        last = spans[-1][1]
    first = len(sources) * 2

    def kernel(*refs):
        out = refs[-1]
        for (rows, _), value, (a, b) in zip(items, refs[first:], spans):
            place = [rows is t for t in sources].index(True)
            own, other = refs[2 * place], refs[2 * place + 1]
            made = dot(own[...], value[:half], ((0,), (0,))) + dot(other[...], value[half:], ((0,), (0,)))
            for (array, _, start), came in zip(arrived, refs[first + len(items) :]):
                if start <= a < start + array.shape[1]:
                    made = made + came[:, a - start : b - start].astype(f32)
            out[:, a:b] = made.astype(bf16)

    columns = spec((half, size), lambda i: (0, base + i))
    return pl.pallas_call(
        kernel,
        grid=(steps,),
        in_specs=[columns] * first
        + [spec(v.shape, lambda i: (0, 0)) for _, v in items]
        + [spec((size, a.shape[1]), lambda i, place=place: (place + i, 0)) for a, place, _ in arrived],
        out_specs=spec((size, last), lambda i: (i, 0)),
        out_shape=jax.ShapeDtypeStruct((steps * size, last), bf16),
        compiler_params=pltpu.CompilerParams(vmem_limit_bytes=vmem_room),
        cost_estimate=cost(4 * half * steps * size * last, half * width * 4 + half * 4 * last),
        name="weight_grad",
    )(*[t for pair in sources for t in pair], *[v for _, v in items], *[a for a, _, _ in arrived])


def halves(parts):
    return [t for p in parts for t in (p if isinstance(p, (list, tuple)) else [p])]


def read_total(parts, refs):
    refs, read = list(refs), []
    for p in parts:
        if isinstance(p, (list, tuple)):
            read.append(jnp.concatenate([refs.pop(0)[...] for _ in p], axis=1))
        else:
            read.append(refs.pop(0)[...])
    return total([r.astype(f32) for r in read])


def by_rows(array, size=256):
    if array.shape[0] == 1:
        return spec(array.shape, lambda i: (0, 0))
    return spec((size, array.shape[1]), lambda i: (i, 0))


def add_norm(parts, gain_row):
    arrays = halves(parts)
    rows, width = arrays[0].shape[0], D

    def kernel(gain_ref, *refs):
        hidden = read_total(parts, refs[: len(arrays)])
        scale = lax.rsqrt(jnp.mean(hidden * hidden, axis=-1, keepdims=True) + epsilon)
        refs[-1][...] = (hidden * scale * gain_ref[...]).astype(bf16)
        if len(parts) > 1:
            refs[-2][...] = hidden

    kinds = [f32, bf16] if len(parts) > 1 else [bf16]
    shapes = [jax.ShapeDtypeStruct((rows, width), k) for k in kinds]
    return pl.pallas_call(
        kernel,
        grid=(rows // 256,),
        in_specs=[by_rows(gain_row), *[by_rows(p) for p in arrays]],
        out_specs=[by_rows(t) for t in shapes],
        out_shape=shapes,
        compiler_params=pltpu.CompilerParams(vmem_limit_bytes=vmem_room),
        cost_estimate=cost(rows * width * 8, rows * width * 14),
        name="add_norm",
    )(gain_row, *arrays)


def norm_back(hidden, gain_row, grads, base):
    rows, width = hidden.shape
    arrays = halves(grads)

    def kernel(gain_ref, hidden_ref, base_ref, *refs):
        grad = read_total(grads, refs[: len(arrays)])
        out, low, gain_grad = refs[len(arrays) :]
        hidden = hidden_ref[...].astype(f32)
        scale = lax.rsqrt(jnp.mean(hidden * hidden, axis=-1, keepdims=True) + epsilon)
        z = hidden * scale
        grad_z = grad * gain_ref[...]
        grad_hidden = scale * (grad_z - z * jnp.mean(grad_z * z, axis=-1, keepdims=True))
        value = base_ref[...].astype(f32) + grad_hidden
        out[...] = value
        low[...] = value.astype(bf16)

        @pl.when(pl.program_id(0) == 0)
        def _():
            gain_grad[...] = jnp.zeros_like(gain_grad)

        gain_grad[...] += jnp.sum(grad * z, axis=0, keepdims=True)

    shapes = [jax.ShapeDtypeStruct((rows, width), f32), jax.ShapeDtypeStruct((rows, width), bf16)]
    return pl.pallas_call(
        kernel,
        grid=(rows // 256,),
        in_specs=[by_rows(gain_row), by_rows(hidden), by_rows(base), *[by_rows(g) for g in arrays]],
        out_specs=[*[by_rows(t) for t in shapes], spec((1, width), lambda i: (0, 0))],
        out_shape=[*shapes, jax.ShapeDtypeStruct((1, width), f32)],
        compiler_params=pltpu.CompilerParams(vmem_limit_bytes=vmem_room),
        cost_estimate=cost(rows * width * 16, rows * width * 22),
        name="norm_back",
    )(gain_row, hidden, base, *arrays)


def after(value, *others):
    return lax.optimization_barrier((value, *others))[0]


def swap_cores(values):
    return lax.ppermute(values, "mc", swap)


def swap_x(values):
    return row_major(lax.ppermute(row_major(values), "mx", swap))


def swap_y(values):
    return row_major(lax.ppermute(row_major(values), "dy", swap))


def gather_part(local):
    return row_major(lax.all_gather(row_major(local), "dz", axis=0, tiled=True))


def spread(part, x_last):
    if x_last:
        high = swap_y(part)
        return (part, high), (swap_x(part), swap_x(high))
    beside = swap_x(part)
    return (part, swap_y(part)), (beside, swap_y(beside))


def pieces(value, count):
    made = []
    for _ in range(count):
        made.append(value.astype(bf16))
        value = value - made[-1].astype(f32)
    return made


class Group:
    def __init__(self, x_items, y_items):
        self.own = [(r, v) for r, v, _ in (*x_items, *y_items)]
        self.own_x, self.own_y = self.own[: len(x_items)], self.own[len(x_items) :]
        self.other_x, self.other_y = ([(r, v) for r, _, v in items] for items in (x_items, y_items))

    def first(self):
        self.sent = [weight_grad(self.other_x, None), weight_grad([*self.own_y, *self.other_y], 1)]
        return self.sent

    def send(self, *deps):
        to_x, to_y = (after(t, *deps) if deps else t for t in self.sent)
        self.from_x, self.from_y = swap_x(to_x), swap_y(to_y)

    def second(self, *deps):
        self.from_x, self.from_y = after(self.from_x, *deps), after(self.from_y, *deps)
        wide_y = self.from_y.shape[1] // 2
        self.sent = [
            weight_grad(self.own_x, 1, [(self.from_x, 1, 0)]),
            weight_grad(self.other_y, 0, [(self.from_y, 0, -wide_y)]),
        ]
        self.sent2 = self.sent
        self.late_y, self.late_x = swap_y(self.sent[0]), swap_x(self.sent[1])
        return self.sent

    def third(self, *deps, behind=()):
        wide_x = self.from_x.shape[1]
        late_y, late_x = after(self.late_y, *deps), after(self.late_x, *deps)
        summed = weight_grad(
            self.own, 0, [(self.from_x, 0, 0), (late_y, 0, 0), (self.from_y, 0, wide_x), (late_x, 0, wide_x)]
        )
        self.sent = [summed]
        summed = after(summed, *behind) if behind else summed
        self.low = lax.psum_scatter(row_major(summed), "dz", scatter_dimension=0, tiled=True)
        self.result = self.low.astype(f32)
        return self.sent


def on_device(
    tokens,
    encoder,
    cotangent,
    lengths,
    deal,
    attn_in,
    attn_out,
    ff_in,
    ff_out,
    gains,
    mom_attn_in,
    mom_attn_out,
    mom_ff_in,
    mom_ff_out,
    mom_gains,
    avg_attn_in,
    avg_attn_out,
    avg_ff_in,
    avg_ff_out,
    avg_gains,
):
    seq_count, block_rows = tokens.shape[0], tokens.shape[1]
    core = lax.axis_index("mc")
    dy = lax.axis_index("dy")
    chip = lax.axis_index(chips)
    own_rows = block_rows * seq_count
    slot_len = 2 * own_rows
    heads_cols = attn_in.shape[2]
    hidden = ff_in.shape[2]
    model_rows = attn_in.shape[1]

    def exchange(values):
        return lax.all_to_all(values, chips, split_axis=0, concat_axis=0, tiled=True)

    def to_chips(values):
        return exchange(values).reshape(own_rows, D)

    def from_chips(rows):
        return exchange(rows.reshape(seq_count, block_rows, D))

    seq_len = lengths[deal[chip]]
    row_ids = jnp.arange(own_rows, dtype=jnp.int32)
    lane = row_ids % block_rows
    pos_own = (row_ids // block_rows * 2 + core) * block_rows + lane
    pos_other = (row_ids // block_rows * 2 + 1 - core) * block_rows + lane
    pos = jnp.concatenate([pos_own, pos_other])
    places = (pos[:, None], pos[None, :])
    length = seq_len[None]
    valid_own = (pos_own < seq_len).astype(f32)[:, None]

    hc = heads_cols
    pairs = hc // (2 * DK)
    spare = -hidden % 256
    deep = hidden + spare
    widen = lambda t: jnp.pad(t.astype(bf16), ((0, 0), (0, spare)))
    out_t = jnp.swapaxes(attn_out.astype(bf16), 1, 2)
    low_in = attn_in.astype(bf16)
    pad = jnp.zeros((model_rows, 125), bf16)
    chunk_a = jnp.concatenate([*low_in[0:3], out_t[0], gains.astype(bf16).T, pad], axis=1)
    chunk_b = jnp.concatenate([*low_in[3:6], out_t[1]], axis=1)
    chunk_c = jnp.concatenate([widen(ff_in[0]), widen(ff_in[1]), widen(ff_out.T)], axis=1)

    part_a, part_b, part_c = (gather_part(t) for t in (chunk_a, chunk_b, chunk_c))
    got_a = spread(part_a, True)
    tok_own = to_chips(after(tokens, part_a))
    cot_own = to_chips(cotangent)

    gain_f = jnp.concatenate([g[:, 4 * hc : 4 * hc + 3] for g in got_a[0]]).astype(f32).T
    gain_rows = [gain_f[n : n + 1] for n in range(3)]
    w_qkv = [(*g, 3 * hc, 0) for g in got_a]
    w_q, w_k, w_v, w_ot = ([(*g, hc, n) for g in got_a] for n in range(4))

    def both(own):
        return own, swap_cores(own)

    def over_cores(values, weights):
        away = [swap_cores(t) for t in combine(values, weights, 1)]
        return combine(values, weights, 0), away

    x_own = reorder([after(tok_own, chunk_b, chunk_c)], model_rows, dy, True)
    norm_one = both(add_norm([x_own], gain_rows[0])[0])
    norm_one = after(norm_one[0], part_b), norm_one[1]
    qkv = [project(norm_one, [w_qkv[0]])[0]]
    self_qkv = [[(qkv[0], n * pairs, pairs) for n in range(3)]]
    self_out = [attend(*self_qkv[0], *places, length, True, 256)]
    qkv += project((after(norm_one[0], self_out[0][0]), norm_one[1]), [w_qkv[1]])
    self_qkv += [[(qkv[1], n * pairs, pairs) for n in range(3)]]
    high_b, beside_b = swap_y(part_b), swap_x(part_b)
    self_out += [attend(*self_qkv[1], *places, length, True, 256)]
    far_b = swap_y(after(beside_b, self_out[1][0], high_b))
    got_b = (part_b, high_b), (beside_b, far_b)
    w_cq, w_ck, w_cv, w_cot = ([(*g, hc, n) for g in got_b] for n in range(4))

    enc_own = to_chips(after(encoder, self_out[0][0]))
    part_c = after(part_c, self_out[1][0], far_b)
    high_c, beside_c = swap_y(part_c), swap_x(part_c)
    far_gu, far_d = swap_x(high_c[:, : 2 * deep]), swap_y(beside_c[:, 2 * deep :])
    w_g, w_u, w_dt = (
        [(part_c, high_c, deep, n), (beside_c, far, deep, n, place)]
        for n, far, place in ((0, far_gu, 0), (1, far_gu, 1), (2, far_d, 0))
    )

    self_mixed = [o[0] for o in self_out]
    hidden_one, norm_two = add_norm([x_own, *over_cores(self_mixed, w_ot)], gain_rows[1])
    norm_two = both(norm_two)
    e_own = reorder([enc_own], model_rows, dy, True)
    enc_rows = both(e_own)
    cross_kv = project(enc_rows, [*w_ck, *w_cv])
    cross_q = project(norm_two, w_cq)
    cross_qkv = [
        [(t, 0, pairs) for t in (cross_q[n], cross_kv[n], cross_kv[2 + n])] for n in range(2)
    ]
    cross_qkv[0][0] = (after(cross_q[0], cross_q[1], high_c, beside_c), 0, pairs)
    cross_out = [attend(*t, *places, length, False, 1024) for t in cross_qkv]
    cross_mixed = [o[0] for o in cross_out]
    hidden_two, norm_three = add_norm(
        [hidden_one, *over_cores(cross_mixed, w_cot)], gain_rows[2]
    )
    norm_three = both(norm_three)
    dy_own = reorder([cot_own], model_rows, dy, True, valid_own)
    grad_out = both(dy_own)
    inner, slope, value = zip(*[project(norm_three, list(w), "gelu") for w in zip(w_g, w_u)])

    scales = [t for pair in zip(slope, value) for t in pair]
    grad_gu = project(grad_out, w_dt, "scale", scales)
    grad_gate, grad_up = grad_gu[::2], grad_gu[1::2]
    group_c = Group([(norm_three, *grad_gate), (grad_out, *inner)], [(norm_three, *grad_up)])
    sent = group_c.first()
    group_c.send()
    parts = over_cores([after(grad_gate[0], *sent), grad_gate[1], *grad_up], [*w_g, *w_u])
    grad_two, low_two, gain_three = norm_back(hidden_two, gain_rows[2], parts, dy_own)
    grad_co = both(low_two)
    out_parts = over_cores([after(inner[0], low_two), inner[1]], w_dt)
    grad_ca = project((after(grad_co[0], out_parts[0][0]), grad_co[1]), w_cot)
    out_block = reorder([after(hidden_two, *grad_ca), *out_parts], model_rows, dy, False, valid_own)
    block_output = from_chips(out_block)
    cross_back = [attend_back(*cross_qkv[0], *places, cross_out[0][1], after(grad_ca[0], out_block), False, 1024)]
    grad_late = after(grad_ca[1], group_c.from_y, *cross_back[0])
    cross_back += [attend_back(*cross_qkv[1], *places, cross_out[1][1], grad_late, False, 1024)]
    grad_cq, grad_ck, grad_cv = zip(*cross_back)
    sent = group_c.second(*grad_cq)
    grad_cq = (after(grad_cq[0], *sent), grad_cq[1])
    group_b = Group(
        [(norm_two, *grad_cq), (grad_co, *[o[0] for o in cross_out])],
        [(enc_rows, *grad_ck), (enc_rows, *grad_cv)],
    )
    parts = over_cores(grad_cq, w_cq)
    sent = group_b.first()
    group_b.send()
    parts_enc = over_cores([after(grad_ck[0], *sent), grad_ck[1], *grad_cv], [*w_ck, *w_cv])
    grad_one, low_one, gain_two = norm_back(
        hidden_one, gain_rows[1], [parts[0], [after(parts[1][0], parts_enc[0][0]), parts[1][1]]], grad_two
    )
    grad_o = both(low_one)
    out_enc = reorder([parts_enc[0], [after(parts_enc[1][0], low_one), parts_enc[1][1]]], model_rows, dy, False)
    grad_encoder = from_chips(out_enc)
    grad_a = project((after(grad_o[0], out_enc, block_output), grad_o[1]), w_ot)
    self_back = [attend_back(*self_qkv[0], *places, self_out[0][1], grad_a[0], True, 256)]
    sent = group_c.third(*self_back[0])
    self_back.append(attend_back(*self_qkv[1], *places, self_out[1][1], after(grad_a[1], *sent), True, 256))
    grad_q, grad_k, grad_v = zip(*self_back)
    group_a = Group(
        [(norm_one, *grad_q), (grad_o, *[o[0] for o in self_out])],
        [(norm_one, *grad_k), (norm_one, *grad_v)],
    )
    sent = group_a.first()
    parts = over_cores(
        [after(grad_q[0], *sent), grad_q[1], *grad_k, *grad_v], [*w_q, *w_k, *w_v]
    )
    sent = group_b.second(*parts[0])
    group_a.send(group_b.late_x, group_b.late_y)
    _, low_tok, gain_one = norm_back(
        x_own, gain_rows[0], [[after(parts[0][0], *sent), parts[0][1]], parts[1]], grad_one
    )
    out_tok = reorder([after(low_tok, grad_encoder)], model_rows, dy, False)
    sent = group_b.third(low_tok, behind=[group_c.low])
    group_a.second(*sent)
    group_a.third(behind=[group_b.low])
    dp_count = seq_count // 2
    gain_part = jnp.concatenate([gain_one, gain_two, gain_three])
    parts = [gain_part[:, n * D // 2 : (n + 1) * D // 2].reshape(3, dp_count // 2, model_rows) for n in range(2)]
    gain_part = jnp.stack([jnp.where(dy == 0, *parts), jnp.where(dy == 0, *parts[::-1])], axis=2)
    gain_part = jnp.swapaxes(gain_part.reshape(3, dp_count, model_rows), 0, 1).reshape(dp_count, -1)
    mx = lax.axis_index("mx")
    tops = jnp.stack([jnp.where(mx == n, self_out[0][2], self_out[1][2]) for n in range(2)])
    tops = jnp.broadcast_to(tops[None], (dp_count, *tops.shape)).reshape(seq_count, -1)
    small = jnp.concatenate([*pieces(jnp.repeat(gain_part, 2, axis=0), 2), *pieces(tops, 3)], axis=1)
    small = jnp.pad(small, ((0, 0), (0, D - small.shape[1])))[:, None]
    sent = jnp.concatenate([out_tok.reshape(seq_count, block_rows, D), small], axis=1)
    came = exchange(after(sent, *group_a.sent2))
    grad_tokens, small = came[:, :block_rows], came[:, block_rows].astype(f32)
    group_a.third(out_tok, behind=[group_b.low])
    sum_a, sum_b, sum_c = group_a.result, group_b.result, group_c.result

    small = after(small, group_a.low)
    wide = 3 * model_rows
    red_gain = jnp.sum(small[:, :wide] + small[:, wide : 2 * wide], axis=0).reshape(3, model_rows)
    red_gain = red_gain + swap_cores(red_gain)
    tops = small[:, 2 * wide : 2 * wide + 3 * (hc // DK)].reshape(seq_count, 3, -1)
    head_peak = jnp.max(tops[:, 0] + tops[:, 1] + tops[:, 2], axis=0)

    cut = lambda t, n: t[:, n * hc : (n + 1) * hc]
    red_in = jnp.stack([cut(t, n) for t in (sum_a, sum_b) for n in (0, 2, 3)])
    red_out = jnp.stack([cut(sum_a, 1).T, cut(sum_b, 1).T])
    red_ff = jnp.stack([sum_c[:, n * deep : n * deep + hidden] for n in (0, 2)])
    red_in = row_major(red_in)
    red_out = with_layout_constraint(red_out, Layout(major_to_minor=(0, 1, 2)))
    red_ff = with_layout_constraint(red_ff, Layout(major_to_minor=(0, 2, 1)))
    red_down = with_layout_constraint(sum_c[:, deep : deep + hidden].T, Layout(major_to_minor=(0, 1)))
    clip_factors = clip_limit / jnp.maximum(head_peak, clip_limit)
    column = jnp.repeat(jnp.sqrt(clip_factors), DK)
    factor = jnp.where((jnp.arange(6) < 2)[:, None, None], column[None, None, :], 1.0)
    grad_scale = float(seq_count * slot_len) ** (-0.5)
    up_a = apply_update(attn_in, red_in, mom_attn_in, avg_attn_in, factor, grad_scale)
    up_b = apply_update(attn_out, red_out, mom_attn_out, avg_attn_out, 1.0, grad_scale)
    up_c = apply_update(ff_in, red_ff, mom_ff_in, avg_ff_in, 1.0, grad_scale)
    up_d = apply_update(ff_out, red_down, mom_ff_out, avg_ff_out, 1.0, grad_scale)
    up_e = apply_update(gains, red_gain, mom_gains, avg_gains, 1.0, grad_scale)
    return (
        block_output.astype(f32),
        grad_tokens.astype(f32),
        grad_encoder.astype(f32),
        *up_a,
        *up_b,
        *up_c,
        *up_d,
        *up_e,
        head_peak,
        clip_factors,
    )


def solution(mesh):
    dp, mp = mesh.shape["dp"], mesh.shape["mp"]
    fine = Mesh(mesh.devices.reshape(dp // 2, 2, mp // 2, 2), ("dz", "dy", "mx", "mc"))
    dp_axes, mp_axes = ("dz", "dy"), ("mx", "mc")
    rows = P(None, (*dp_axes, *mp_axes), None)
    wide = P(None, dp_axes, mp_axes)
    tall = P(None, mp_axes, dp_axes)
    down = P(mp_axes, dp_axes)
    gain = P(None, dp_axes)
    state = (wide, tall, wide, down, gain)
    in_specs = (rows, rows, rows, P(), P(), *state, *state, *state)
    out_specs = (
        rows,
        rows,
        rows,
        *[wide] * 4,
        *[tall] * 4,
        *[wide] * 4,
        *[down] * 4,
        *[gain] * 4,
        P(mp_axes),
        P(mp_axes),
    )
    return jax.shard_map(
        on_device, mesh=fine, in_specs=in_specs, out_specs=out_specs, check_vma=False
    )
```

```python
import functools

import jax
import jax.numpy as jnp
from jax import lax
from jax.experimental import pallas as pl
from jax.experimental.layout import Layout, with_layout_constraint
from jax.experimental.pallas import tpu as pltpu
from jax.sharding import Mesh, PartitionSpec as P

D = 1024
DK = 64

epsilon = 1e-06
clip_limit = 10.0
momentum_rate = 0.9
learn_rate = 0.01
average_rate = 0.5
neg_large = -1e30
vmem_room = 24 << 20
tanh_rate = 0.7978845608
tanh_cube = 0.044715
bf16 = jnp.bfloat16
f32 = jnp.float32
swap = ((0, 1), (1, 0))
chips = ("dz", "dy", "mx")


def dot(left, right, dims):
    return lax.dot_general(left, right, (dims, ((), ())), preferred_element_type=f32)


def head_lanes(block, head):
    lanes = lax.broadcasted_iota(jnp.int32, block.shape, 1)
    return jnp.where((lanes >= DK) == (head == 1), block, jnp.zeros_like(block))


def key_spans(rows, keys, start, size, causal):
    half = rows // 2
    reach = start % half + size
    return [(0, reach), (half, half + reach)] if causal and reach < half else [(0, keys)]


def total(parts):
    return functools.reduce(jnp.add, parts)


def attend_kernel(causal, size, q_ref, k_ref, v_ref, pq_ref, pk_ref, len_ref, o_ref, lse_ref, top_ref):
    rows, keys = q_ref.shape[0], k_ref.shape[0]
    tops = []
    for head in range(2):
        k, v = head_lanes(k_ref[...], head), head_lanes(v_ref[...], head)
        top = jnp.full((1, 1), neg_large, f32)
        for start in range(0, rows, size):
            r = slice(start, start + size)
            spans = key_spans(rows, keys, start, size, causal)
            q = q_ref[r, :]
            s = [dot(q, k[a:b], ((1,), (1,))) for a, b in spans]
            if causal:
                s = [jnp.where(pk_ref[:, a:b] <= pq_ref[r, :], t, neg_large) for t, (a, b) in zip(s, spans)]
            m = functools.reduce(jnp.maximum, [jnp.max(t, axis=1, keepdims=True) for t in s])
            if causal:
                real = jnp.where(pq_ref[r, :] < len_ref[0], m, neg_large)
                top = jnp.maximum(top, jnp.max(real, axis=0, keepdims=True))
            e = [jnp.exp(t - m) for t in s]
            mass = total([jnp.sum(t, axis=1, keepdims=True) for t in e])
            scale = 1.0 / mass
            mix = total([dot((t * scale).astype(bf16), v[a:b], ((1,), (0,))) for t, (a, b) in zip(e, spans)])
            if head == 0:
                o_ref[r, :] = mix.astype(bf16)
            else:
                o_ref[r, :] = (o_ref[r, :].astype(f32) + mix).astype(bf16)
            lse_ref[0, r, head : head + 1] = m + jnp.log(mass)
        tops.append(top)
    lanes = lax.broadcasted_iota(jnp.int32, (8, 128), 1)
    top_ref[0] = jnp.where(lanes == 0, tops[0], tops[1])


def attend_back_kernel(
    causal, size, q_ref, k_ref, v_ref, pq_ref, pk_ref, lse_ref, do_ref, dq_ref, dk_ref, dv_ref, dk_acc, dv_acc
):
    rows, keys = q_ref.shape[0], k_ref.shape[0]
    dk_acc[...] = jnp.zeros_like(dk_acc)
    dv_acc[...] = jnp.zeros_like(dv_acc)
    for head in range(2):
        k, v = head_lanes(k_ref[...], head), head_lanes(v_ref[...], head)
        own = slice(DK * head, DK * head + DK)
        for start in range(0, rows, size):
            r = slice(start, start + size)
            spans = key_spans(rows, keys, start, size, causal)
            q, do, lse = q_ref[r, :], do_ref[r, :], lse_ref[0, r, head : head + 1]
            soft, grad = [], []
            for a, b in spans:
                s = dot(q, k[a:b], ((1,), (1,)))
                if causal:
                    s = jnp.where(pk_ref[:, a:b] <= pq_ref[r, :], s, neg_large)
                soft.append(jnp.exp(s - lse))
                grad.append(dot(do, v[a:b], ((1,), (1,))))
            row_dot = total([jnp.sum(p * t, axis=1, keepdims=True) for p, t in zip(soft, grad)])
            q_t, do_t = q.T[own], do.T[own]
            parts = []
            for (a, b), p, t in zip(spans, soft, grad):
                ds = (p * (t - row_dot)).astype(bf16)
                parts.append(dot(ds, k[a:b], ((1,), (0,))))
                dv_acc[own, a:b] += dot(do_t, p.astype(bf16), ((1,), (0,)))
                dk_acc[own, a:b] += dot(q_t, ds, ((1,), (0,)))
            dq = total(parts)
            if head == 0:
                dq_ref[r, :] = dq.astype(bf16)
            else:
                dq_ref[r, :] = (dq_ref[r, :].astype(f32) + dq).astype(bf16)
    dk_ref[...] = dk_acc[...].T.astype(bf16)
    dv_ref[...] = dv_acc[...].T.astype(bf16)


def attend_cost(rows, keys, pairs, dots):
    return cost(0, 0)


def lane_pairs(count, first):
    return pl.BlockSpec((count, 2 * DK), lambda p: (0, first + p))


def attend(q, k, v, pos_col, pos_row, length, causal, size):
    rows, keys, pairs = q[0].shape[0], k[0].shape[0], q[2]
    mixed, lse, top = pl.pallas_call(
        functools.partial(attend_kernel, causal, size),
        grid=(pairs,),
        in_specs=[
            lane_pairs(rows, q[1]),
            lane_pairs(keys, k[1]),
            lane_pairs(keys, v[1]),
            pl.BlockSpec((rows, 1), lambda p: (0, 0)),
            pl.BlockSpec((1, keys), lambda p: (0, 0)),
            pl.BlockSpec(memory_space=pltpu.SMEM),
        ],
        out_specs=[
            lane_pairs(rows, 0),
            pl.BlockSpec((1, rows, 2), lambda p: (p, 0, 0)),
            pl.BlockSpec((1, 8, 128), lambda p: (p, 0, 0)),
        ],
        out_shape=[
            jax.ShapeDtypeStruct((rows, pairs * 2 * DK), bf16),
            jax.ShapeDtypeStruct((pairs, rows, 2), f32),
            jax.ShapeDtypeStruct((pairs, 8, 128), f32),
        ],
        compiler_params=pltpu.CompilerParams(vmem_limit_bytes=vmem_room),
        cost_estimate=attend_cost(rows, keys, pairs, 2),
        name="attend",
    )(q[0], k[0], v[0], pos_col, pos_row, length)
    return mixed, lse, top[:, 0, :2].reshape(-1)


def attend_back(q, k, v, pos_col, pos_row, lse, grad, causal, size):
    rows, keys, pairs = q[0].shape[0], k[0].shape[0], q[2]
    return pl.pallas_call(
        functools.partial(attend_back_kernel, causal, size),
        grid=(pairs,),
        in_specs=[
            lane_pairs(rows, q[1]),
            lane_pairs(keys, k[1]),
            lane_pairs(keys, v[1]),
            pl.BlockSpec((rows, 1), lambda p: (0, 0)),
            pl.BlockSpec((1, keys), lambda p: (0, 0)),
            pl.BlockSpec((1, rows, 2), lambda p: (p, 0, 0)),
            lane_pairs(rows, 0),
        ],
        out_specs=[lane_pairs(rows, 0), lane_pairs(keys, 0), lane_pairs(keys, 0)],
        out_shape=[jax.ShapeDtypeStruct((n, pairs * 2 * DK), bf16) for n in (rows, keys, keys)],
        scratch_shapes=[pltpu.VMEM((2 * DK, keys), f32)] * 2,
        compiler_params=pltpu.CompilerParams(vmem_limit_bytes=vmem_room),
        cost_estimate=attend_cost(rows, keys, pairs, 5),
        name="attend_back",
    )(q[0], k[0], v[0], pos_col, pos_row, lse, grad)


def apply_update(weight, grad_sum, moment, average, factor, grad_scale):
    grad_now = grad_sum * grad_scale
    moment_new = momentum_rate * moment + grad_now
    master_new = (weight - learn_rate * (grad_now + momentum_rate * moment_new)) * factor
    average_new = average_rate * average + (1.0 - average_rate) * master_new
    return (grad_now, moment_new, average_new, master_new)


def flat_columns(block):
    return jnp.swapaxes(block, 0, 1).reshape(block.shape[1], -1)


def row_major(values):
    return with_layout_constraint(values, Layout(major_to_minor=tuple(range(values.ndim))))


spec = pl.BlockSpec


def cost(flops, moved):
    return pl.CostEstimate(flops=1, bytes_accessed=1, transcendentals=0)


def reorder(parts, block, dy, to_own, keep=None):
    arrays = halves(parts)
    rows, width = arrays[0].shape[0], D
    steps = width // block // 2
    extra = [] if keep is None else [keep]
    if block % 128:
        value = total([(jnp.concatenate(p, axis=1) if isinstance(p, (list, tuple)) else p).astype(f32) for p in parts])
        value = value * (1.0 if keep is None else keep)
        axis = 2 if to_own else 1
        value = value.reshape((rows, steps, 2, block) if to_own else (rows, 2, steps, block))
        low, high = (lax.index_in_dim(value, n, axis, keepdims=False) for n in range(2))
        pair = jnp.where(dy == 0, low, high), jnp.where(dy == 0, high, low)
        return jnp.stack(pair, axis=3 - axis).reshape(rows, width).astype(bf16)

    def source(j, flag):
        if to_own:
            return j % steps * 2 + (j // steps + flag) % 2
        return j // 2 + (j % 2 + flag) % 2 * steps

    def kernel(flag_ref, *refs):
        out = refs[-1]
        whole = len(arrays) == 1
        value = refs[0] if whole else read_total(parts, refs[: len(arrays)])
        for j in range(2 * steps):
            spans = [slice(source(j, flag) * block, (source(j, flag) + 1) * block) for flag in range(2)]
            picked = jnp.where(flag_ref[0] == 0, value[:, spans[0]], value[:, spans[1]])
            if extra:
                picked = picked.astype(f32) * refs[len(arrays)][...]
            out[:, j * block : (j + 1) * block] = picked.astype(bf16)

    return pl.pallas_call(
        kernel,
        grid=(4,),
        in_specs=[
            spec(memory_space=pltpu.SMEM),
            *[by_rows(p, rows // 4) for p in [*arrays, *extra]],
        ],
        out_specs=spec((rows // 4, width), lambda i: (i, 0)),
        out_shape=jax.ShapeDtypeStruct((rows, width), bf16),
        compiler_params=pltpu.CompilerParams(vmem_limit_bytes=vmem_room),
        cost_estimate=cost(0, rows * width * 4),
        name="reorder",
    )(dy[None], *arrays, *extra)


def weight_specs(weights):
    specs, arrays = [], []
    for own, other, width, *places in weights:
        for array, place in zip((own, other), (places[0], places[-1])):
            specs.append(spec((array.shape[0], width), lambda i, place=place: (0, place)))
            arrays.append(array)
    return specs, arrays


def project(rows, weights, mode="plain", scales=()):
    own, other = rows
    half, size = own.shape[0], own.shape[0] // 2
    specs, arrays = weight_specs(weights)
    widths = [w[2] for w in weights]
    count = len(weights)
    out_widths = {"plain": widths, "gelu": widths[:1] * 3, "scale": [w for w in widths for _ in range(2)]}[mode]

    def kernel(own_ref, other_ref, *refs):
        here = pl.program_id(0) < 2
        x = jnp.where(here, own_ref[...], other_ref[...])
        split = x.shape[1] // 2
        made = []
        for j in range(count):
            low, high = refs[2 * j], refs[2 * j + 1]
            made.append(
                dot(x[:, :split], low[...], ((1,), (0,))) + dot(x[:, split:], high[...], ((1,), (0,)))
            )
        outs = refs[2 * count + len(scales) :]
        if mode == "plain":
            for out, value in zip(outs, made):
                out[...] = value.astype(bf16)
        elif mode == "gelu":
            gate, up = made
            square = gate * gate
            bend = jnp.tanh(tanh_rate * gate * (1.0 + tanh_cube * square))
            rise = 0.5 * (1.0 + bend)
            value = gate * rise
            slope = rise + 0.5 * gate * (1.0 - bend * bend) * tanh_rate * (1.0 + 3.0 * tanh_cube * square)
            outs[0][...] = (value * up).astype(bf16)
            outs[1][...] = (slope * up).astype(bf16)
            outs[2][...] = value.astype(bf16)
        else:
            for j, out in enumerate(outs):
                out[...] = (made[j // 2] * refs[2 * count + j][...].astype(f32)).astype(bf16)

    by_rows = lambda width: spec((size, width), lambda i: (i, 0))
    width_all = own.shape[1]
    return pl.pallas_call(
        kernel,
        grid=(4,),
        in_specs=[
            spec((size, width_all), lambda i: (jnp.minimum(i, 1), 0)),
            spec((size, width_all), lambda i: (jnp.maximum(i - 2, 0), 0)),
            *specs,
            *[by_rows(t.shape[1]) for t in scales],
        ],
        out_specs=[by_rows(w) for w in out_widths],
        out_shape=[jax.ShapeDtypeStruct((2 * half, w), bf16) for w in out_widths],
        compiler_params=pltpu.CompilerParams(vmem_limit_bytes=vmem_room),
        cost_estimate=cost(4 * half * width_all * sum(widths), half * width_all * 4 + width_all * sum(widths) * 2),
        name="project_" + mode,
    )(own, other, *arrays, *scales)


def combine(values, weights, which):
    specs, arrays = weight_specs(weights)
    half = values[0].shape[0] // 2
    size = half // 2
    count = len(values)
    depth = weights[0][0].shape[0]

    def kernel(*refs):
        for side in range(2):
            parts = [
                dot(refs[j][...], refs[count + 2 * j + side][...], ((1,), (1,))) for j in range(count)
            ]
            refs[side - 2][...] = total(parts)

    return pl.pallas_call(
        kernel,
        grid=(2,),
        in_specs=[spec((size, v.shape[1]), lambda i: (2 * which + i, 0)) for v in values] + specs,
        out_specs=[spec((size, depth), lambda i: (i, 0))] * 2,
        out_shape=[jax.ShapeDtypeStruct((half, depth), f32)] * 2,
        compiler_params=pltpu.CompilerParams(vmem_limit_bytes=vmem_room),
        cost_estimate=cost(0, 0),
        name="combine",
    )(*values, *arrays)


def weight_grad(items, part, arrived=()):
    sources = []
    for rows, _ in items:
        if not any(rows is t for t in sources):
            sources.append(rows)
    half, width = sources[0][0].shape
    size = width // 2
    steps, base = (2, 0) if part is None else (1, part)
    spans, last = [], 0
    for _, value in items:
        spans.append((last, last + value.shape[1]))
        last = spans[-1][1]
    first = len(sources) * 2

    def kernel(*refs):
        out = refs[-1]
        for (rows, _), value, (a, b) in zip(items, refs[first:], spans):
            place = [rows is t for t in sources].index(True)
            own, other = refs[2 * place], refs[2 * place + 1]
            made = dot(own[...], value[:half], ((0,), (0,))) + dot(other[...], value[half:], ((0,), (0,)))
            for (array, _, start), came in zip(arrived, refs[first + len(items) :]):
                if start <= a < start + array.shape[1]:
                    made = made + came[:, a - start : b - start].astype(f32)
            out[:, a:b] = made.astype(bf16)

    columns = spec((half, size), lambda i: (0, base + i))
    return pl.pallas_call(
        kernel,
        grid=(steps,),
        in_specs=[columns] * first
        + [spec(v.shape, lambda i: (0, 0)) for _, v in items]
        + [spec((size, a.shape[1]), lambda i, place=place: (place + i, 0)) for a, place, _ in arrived],
        out_specs=spec((size, last), lambda i: (i, 0)),
        out_shape=jax.ShapeDtypeStruct((steps * size, last), bf16),
        compiler_params=pltpu.CompilerParams(vmem_limit_bytes=vmem_room),
        cost_estimate=cost(4 * half * steps * size * last, half * width * 4 + half * 4 * last),
        name="weight_grad",
    )(*[t for pair in sources for t in pair], *[v for _, v in items], *[a for a, _, _ in arrived])


def halves(parts):
    return [t for p in parts for t in (p if isinstance(p, (list, tuple)) else [p])]


def read_total(parts, refs):
    refs, read = list(refs), []
    for p in parts:
        if isinstance(p, (list, tuple)):
            read.append(jnp.concatenate([refs.pop(0)[...] for _ in p], axis=1))
        else:
            read.append(refs.pop(0)[...])
    return total([r.astype(f32) for r in read])


def by_rows(array, size=256):
    if array.shape[0] == 1:
        return spec(array.shape, lambda i: (0, 0))
    return spec((size, array.shape[1]), lambda i: (i, 0))


def add_norm(parts, gain_row):
    arrays = halves(parts)
    rows, width = arrays[0].shape[0], D

    def kernel(gain_ref, *refs):
        hidden = read_total(parts, refs[: len(arrays)])
        scale = lax.rsqrt(jnp.mean(hidden * hidden, axis=-1, keepdims=True) + epsilon)
        refs[-1][...] = (hidden * scale * gain_ref[...]).astype(bf16)
        if len(parts) > 1:
            refs[-2][...] = hidden

    kinds = [f32, bf16] if len(parts) > 1 else [bf16]
    shapes = [jax.ShapeDtypeStruct((rows, width), k) for k in kinds]
    return pl.pallas_call(
        kernel,
        grid=(rows // 256,),
        in_specs=[by_rows(gain_row), *[by_rows(p) for p in arrays]],
        out_specs=[by_rows(t) for t in shapes],
        out_shape=shapes,
        compiler_params=pltpu.CompilerParams(vmem_limit_bytes=vmem_room),
        cost_estimate=cost(rows * width * 8, rows * width * 14),
        name="add_norm",
    )(gain_row, *arrays)


def norm_back(hidden, gain_row, grads, base):
    rows, width = hidden.shape
    arrays = halves(grads)

    def kernel(gain_ref, hidden_ref, base_ref, *refs):
        grad = read_total(grads, refs[: len(arrays)])
        out, low, gain_grad = refs[len(arrays) :]
        hidden = hidden_ref[...].astype(f32)
        scale = lax.rsqrt(jnp.mean(hidden * hidden, axis=-1, keepdims=True) + epsilon)
        z = hidden * scale
        grad_z = grad * gain_ref[...]
        grad_hidden = scale * (grad_z - z * jnp.mean(grad_z * z, axis=-1, keepdims=True))
        value = base_ref[...].astype(f32) + grad_hidden
        out[...] = value
        low[...] = value.astype(bf16)

        @pl.when(pl.program_id(0) == 0)
        def _():
            gain_grad[...] = jnp.zeros_like(gain_grad)

        gain_grad[...] += jnp.sum(grad * z, axis=0, keepdims=True)

    shapes = [jax.ShapeDtypeStruct((rows, width), f32), jax.ShapeDtypeStruct((rows, width), bf16)]
    return pl.pallas_call(
        kernel,
        grid=(rows // 256,),
        in_specs=[by_rows(gain_row), by_rows(hidden), by_rows(base), *[by_rows(g) for g in arrays]],
        out_specs=[*[by_rows(t) for t in shapes], spec((1, width), lambda i: (0, 0))],
        out_shape=[*shapes, jax.ShapeDtypeStruct((1, width), f32)],
        compiler_params=pltpu.CompilerParams(vmem_limit_bytes=vmem_room),
        cost_estimate=cost(rows * width * 16, rows * width * 22),
        name="norm_back",
    )(gain_row, hidden, base, *arrays)


def after(value, *others):
    return lax.optimization_barrier((value, *others))[0]


def swap_cores(values):
    return lax.ppermute(values, "mc", swap)


def swap_x(values):
    return row_major(lax.ppermute(row_major(values), "mx", swap))


def swap_y(values):
    return row_major(lax.ppermute(row_major(values), "dy", swap))


def gather_part(local):
    return row_major(lax.all_gather(row_major(local), "dz", axis=0, tiled=True))


def spread(part, x_last):
    if x_last:
        high = swap_y(part)
        return (part, high), (swap_x(part), swap_x(high))
    beside = swap_x(part)
    return (part, swap_y(part)), (beside, swap_y(beside))


def pieces(value, count):
    made = []
    for _ in range(count):
        made.append(value.astype(bf16))
        value = value - made[-1].astype(f32)
    return made


class Group:
    def __init__(self, x_items, y_items):
        self.own = [(r, v) for r, v, _ in (*x_items, *y_items)]
        self.own_x, self.own_y = self.own[: len(x_items)], self.own[len(x_items) :]
        self.other_x, self.other_y = ([(r, v) for r, _, v in items] for items in (x_items, y_items))

    def first(self):
        self.sent = [weight_grad(self.other_x, None), weight_grad([*self.own_y, *self.other_y], 1)]
        return self.sent

    def send(self, *deps):
        to_x, to_y = (after(t, *deps) if deps else t for t in self.sent)
        self.from_x, self.from_y = swap_x(to_x), swap_y(to_y)

    def second(self, *deps):
        self.from_x, self.from_y = after(self.from_x, *deps), after(self.from_y, *deps)
        wide_y = self.from_y.shape[1] // 2
        self.sent = [
            weight_grad(self.own_x, 1, [(self.from_x, 1, 0)]),
            weight_grad(self.other_y, 0, [(self.from_y, 0, -wide_y)]),
        ]
        self.middle = self.sent
        self.late_y, self.late_x = swap_y(self.sent[0]), swap_x(self.sent[1])
        return self.sent

    def third(self, *deps, behind=()):
        wide_x = self.from_x.shape[1]
        late_y, late_x = after(self.late_y, *deps), after(self.late_x, *deps)
        summed = weight_grad(
            self.own, 0, [(self.from_x, 0, 0), (late_y, 0, 0), (self.from_y, 0, wide_x), (late_x, 0, wide_x)]
        )
        self.sent = [summed]
        summed = after(summed, *behind) if behind else summed
        self.low = lax.psum_scatter(row_major(summed), "dz", scatter_dimension=0, tiled=True)
        self.result = self.low.astype(f32)
        return self.sent


def on_device(
    tokens,
    encoder,
    cotangent,
    lengths,
    deal,
    attn_in,
    attn_out,
    ff_in,
    ff_out,
    gains,
    mom_attn_in,
    mom_attn_out,
    mom_ff_in,
    mom_ff_out,
    mom_gains,
    avg_attn_in,
    avg_attn_out,
    avg_ff_in,
    avg_ff_out,
    avg_gains,
):
    seq_count, block_rows = tokens.shape[0], tokens.shape[1]
    core = lax.axis_index("mc")
    dy = lax.axis_index("dy")
    chip = lax.axis_index(chips)
    own_rows = block_rows * seq_count
    slot_len = 2 * own_rows
    heads_cols = attn_in.shape[2]
    hidden = ff_in.shape[2]
    model_rows = attn_in.shape[1]

    def exchange(values):
        return lax.all_to_all(values, chips, split_axis=0, concat_axis=0, tiled=True)

    def to_chips(values):
        return exchange(values).reshape(own_rows, D)

    def from_chips(rows):
        return exchange(rows.reshape(seq_count, block_rows, D))

    seq_len = lengths[deal[chip]]
    row_ids = jnp.arange(own_rows, dtype=jnp.int32)
    lane = row_ids % block_rows
    pos_own = (row_ids // block_rows * 2 + core) * block_rows + lane
    pos_other = (row_ids // block_rows * 2 + 1 - core) * block_rows + lane
    pos = jnp.concatenate([pos_own, pos_other])
    places = (pos[:, None], pos[None, :])
    length = seq_len[None]
    valid_own = (pos_own < seq_len).astype(f32)[:, None]

    hc = heads_cols
    pairs = hc // (2 * DK)
    spare = -hidden % 256
    deep = hidden + spare
    widen = lambda t: jnp.pad(t.astype(bf16), ((0, 0), (0, spare)))
    out_t = jnp.swapaxes(attn_out.astype(bf16), 1, 2)
    low_in = attn_in.astype(bf16)
    pad = jnp.zeros((model_rows, 125), bf16)
    chunk_a = jnp.concatenate([*low_in[0:3], out_t[0], gains.astype(bf16).T, pad], axis=1)
    chunk_b = jnp.concatenate([*low_in[3:6], out_t[1]], axis=1)
    chunk_c = jnp.concatenate([widen(ff_in[0]), widen(ff_in[1]), widen(ff_out.T)], axis=1)

    part_a, part_b, part_c = (gather_part(t) for t in (chunk_a, chunk_b, chunk_c))
    got_a = spread(part_a, True)
    tok_own = to_chips(after(tokens, part_a))
    cot_own = to_chips(cotangent)

    gain_f = jnp.concatenate([g[:, 4 * hc : 4 * hc + 3] for g in got_a[0]]).astype(f32).T
    gain_rows = [gain_f[n : n + 1] for n in range(3)]
    w_qkv = [(*g, 3 * hc, 0) for g in got_a]
    w_q, w_k, w_v, w_ot = ([(*g, hc, n) for g in got_a] for n in range(4))

    def both(own):
        return own, swap_cores(own)

    def over_cores(values, weights):
        away = [swap_cores(t) for t in combine(values, weights, 1)]
        return combine(values, weights, 0), away

    x_own = reorder([after(tok_own, chunk_b, chunk_c)], model_rows, dy, True)
    norm_one = both(add_norm([x_own], gain_rows[0])[0])
    norm_one = after(norm_one[0], part_b), norm_one[1]
    qkv = [project(norm_one, [w_qkv[0]])[0]]
    self_qkv = [[(qkv[0], n * pairs, pairs) for n in range(3)]]
    self_out = [attend(*self_qkv[0], *places, length, True, 256)]
    qkv += project((after(norm_one[0], self_out[0][0]), norm_one[1]), [w_qkv[1]])
    self_qkv += [[(qkv[1], n * pairs, pairs) for n in range(3)]]
    high_b, beside_b = swap_y(part_b), swap_x(part_b)
    self_out += [attend(*self_qkv[1], *places, length, True, 256)]
    far_b = swap_y(after(beside_b, self_out[1][0], high_b))
    got_b = (part_b, high_b), (beside_b, far_b)
    w_cq, w_ck, w_cv, w_cot = ([(*g, hc, n) for g in got_b] for n in range(4))

    enc_own = to_chips(after(encoder, self_out[0][0]))
    part_c = after(part_c, self_out[1][0], far_b)
    high_c, beside_c = swap_y(part_c), swap_x(part_c)
    far_gu, far_d = swap_x(high_c[:, : 2 * deep]), swap_y(beside_c[:, 2 * deep :])
    w_g, w_u, w_dt = (
        [(part_c, high_c, deep, n), (beside_c, far, deep, n, place)]
        for n, far, place in ((0, far_gu, 0), (1, far_gu, 1), (2, far_d, 0))
    )

    self_mixed = [o[0] for o in self_out]
    hidden_one, norm_two = add_norm([x_own, *over_cores(self_mixed, w_ot)], gain_rows[1])
    norm_two = both(norm_two)
    e_own = reorder([enc_own], model_rows, dy, True)
    enc_rows = both(e_own)
    cross_kv = project(enc_rows, [*w_ck, *w_cv])
    cross_q = project(norm_two, w_cq)
    cross_qkv = [
        [(t, 0, pairs) for t in (cross_q[n], cross_kv[n], cross_kv[2 + n])] for n in range(2)
    ]
    cross_qkv[0][0] = (after(cross_q[0], cross_q[1], high_c, beside_c), 0, pairs)
    cross_out = [attend(*t, *places, length, False, 1024) for t in cross_qkv]
    cross_mixed = [o[0] for o in cross_out]
    hidden_two, norm_three = add_norm(
        [hidden_one, *over_cores(cross_mixed, w_cot)], gain_rows[2]
    )
    norm_three = both(norm_three)
    dy_own = reorder([cot_own], model_rows, dy, True, valid_own)
    grad_out = both(dy_own)
    inner, slope, value = zip(*[project(norm_three, list(w), "gelu") for w in zip(w_g, w_u)])

    scales = [t for pair in zip(slope, value) for t in pair]
    grad_gu = project(grad_out, w_dt, "scale", scales)
    grad_gate, grad_up = grad_gu[::2], grad_gu[1::2]
    group_c = Group([(norm_three, *grad_gate), (grad_out, *inner)], [(norm_three, *grad_up)])
    sent = group_c.first()
    group_c.send()
    parts = over_cores([after(grad_gate[0], *sent), grad_gate[1], *grad_up], [*w_g, *w_u])
    grad_two, low_two, gain_three = norm_back(hidden_two, gain_rows[2], parts, dy_own)
    grad_co = both(low_two)
    out_parts = over_cores([after(inner[0], low_two), inner[1]], w_dt)
    grad_ca = project((after(grad_co[0], out_parts[0][0]), grad_co[1]), w_cot)
    out_block = reorder([after(hidden_two, *grad_ca), *out_parts], model_rows, dy, False, valid_own)
    block_output = from_chips(out_block)
    cross_back = [attend_back(*cross_qkv[0], *places, cross_out[0][1], after(grad_ca[0], out_block), False, 1024)]
    grad_late = after(grad_ca[1], group_c.from_y, *cross_back[0])
    cross_back += [attend_back(*cross_qkv[1], *places, cross_out[1][1], grad_late, False, 1024)]
    grad_cq, grad_ck, grad_cv = zip(*cross_back)
    sent = group_c.second(*grad_cq)
    grad_cq = (after(grad_cq[0], *sent), grad_cq[1])
    group_b = Group(
        [(norm_two, *grad_cq), (grad_co, *[o[0] for o in cross_out])],
        [(enc_rows, *grad_ck), (enc_rows, *grad_cv)],
    )
    parts = over_cores(grad_cq, w_cq)
    sent = group_b.first()
    group_b.send()
    parts_enc = over_cores([after(grad_ck[0], *sent), grad_ck[1], *grad_cv], [*w_ck, *w_cv])
    grad_one, low_one, gain_two = norm_back(
        hidden_one, gain_rows[1], [parts[0], [after(parts[1][0], parts_enc[0][0]), parts[1][1]]], grad_two
    )
    grad_o = both(low_one)
    out_enc = reorder([parts_enc[0], [after(parts_enc[1][0], low_one), parts_enc[1][1]]], model_rows, dy, False)
    grad_encoder = from_chips(out_enc)
    grad_a = project((after(grad_o[0], out_enc, block_output), grad_o[1]), w_ot)
    self_back = [attend_back(*self_qkv[0], *places, self_out[0][1], grad_a[0], True, 256)]
    sent = group_c.third(*self_back[0])
    self_back.append(attend_back(*self_qkv[1], *places, self_out[1][1], after(grad_a[1], *sent), True, 256))
    grad_q, grad_k, grad_v = zip(*self_back)
    group_a = Group(
        [(norm_one, *grad_q), (grad_o, *[o[0] for o in self_out])],
        [(norm_one, *grad_k), (norm_one, *grad_v)],
    )
    sent = group_a.first()
    parts = over_cores(
        [after(grad_q[0], *sent), grad_q[1], *grad_k, *grad_v], [*w_q, *w_k, *w_v]
    )
    group_b.second(*parts[0])
    group_a.send(group_b.late_x, group_b.late_y)
    sent = group_b.third(behind=[group_c.low])
    _, low_tok, gain_one = norm_back(
        x_own, gain_rows[0], [[after(parts[0][0], *sent, group_c.low), parts[0][1]], parts[1]], grad_one
    )
    out_tok = reorder([after(low_tok, grad_encoder)], model_rows, dy, False)
    group_a.second(low_tok)
    group_a.third(behind=[group_b.low])
    dp_count = seq_count // 2
    gain_part = jnp.concatenate([gain_one, gain_two, gain_three])
    parts = [gain_part[:, n * D // 2 : (n + 1) * D // 2].reshape(3, dp_count // 2, model_rows) for n in range(2)]
    gain_part = jnp.stack([jnp.where(dy == 0, *parts), jnp.where(dy == 0, *parts[::-1])], axis=2)
    gain_part = jnp.swapaxes(gain_part.reshape(3, dp_count, model_rows), 0, 1).reshape(dp_count, -1)
    mx = lax.axis_index("mx")
    tops = jnp.stack([jnp.where(mx == n, self_out[0][2], self_out[1][2]) for n in range(2)])
    tops = jnp.broadcast_to(tops[None], (dp_count, *tops.shape)).reshape(seq_count, -1)
    small = jnp.concatenate([*pieces(jnp.repeat(gain_part, 2, axis=0), 2), *pieces(tops, 3)], axis=1)
    small = jnp.pad(small, ((0, 0), (0, D - small.shape[1])))[:, None]
    sent = jnp.concatenate([out_tok.reshape(seq_count, block_rows, D), small], axis=1)
    came = exchange(after(sent, *group_a.middle))
    grad_tokens, small = came[:, :block_rows], came[:, block_rows].astype(f32)
    group_a.third(out_tok, behind=[group_b.low])
    sum_a, sum_b, sum_c = group_a.result, group_b.result, group_c.result

    small = after(small, group_a.low)
    wide = 3 * model_rows
    red_gain = jnp.sum(small[:, :wide] + small[:, wide : 2 * wide], axis=0).reshape(3, model_rows)
    red_gain = red_gain + swap_cores(red_gain)
    tops = small[:, 2 * wide : 2 * wide + 3 * (hc // DK)].reshape(seq_count, 3, -1)
    head_peak = jnp.max(tops[:, 0] + tops[:, 1] + tops[:, 2], axis=0)

    cut = lambda t, n: t[:, n * hc : (n + 1) * hc]
    red_in = jnp.stack([cut(t, n) for t in (sum_a, sum_b) for n in (0, 2, 3)])
    red_out = jnp.stack([cut(sum_a, 1).T, cut(sum_b, 1).T])
    red_ff = jnp.stack([sum_c[:, n * deep : n * deep + hidden] for n in (0, 2)])
    red_in = row_major(red_in)
    red_out = with_layout_constraint(red_out, Layout(major_to_minor=(0, 1, 2)))
    red_ff = with_layout_constraint(red_ff, Layout(major_to_minor=(0, 2, 1)))
    red_down = with_layout_constraint(sum_c[:, deep : deep + hidden].T, Layout(major_to_minor=(0, 1)))
    clip_factors = clip_limit / jnp.maximum(head_peak, clip_limit)
    column = jnp.repeat(jnp.sqrt(clip_factors), DK)
    factor = jnp.where((jnp.arange(6) < 2)[:, None, None], column[None, None, :], 1.0)
    grad_scale = float(seq_count * slot_len) ** (-0.5)
    up_a = apply_update(attn_in, red_in, mom_attn_in, avg_attn_in, factor, grad_scale)
    up_b = apply_update(attn_out, red_out, mom_attn_out, avg_attn_out, 1.0, grad_scale)
    up_c = apply_update(ff_in, red_ff, mom_ff_in, avg_ff_in, 1.0, grad_scale)
    up_d = apply_update(ff_out, red_down, mom_ff_out, avg_ff_out, 1.0, grad_scale)
    up_e = apply_update(gains, red_gain, mom_gains, avg_gains, 1.0, grad_scale)
    return (
        block_output.astype(f32),
        grad_tokens.astype(f32),
        grad_encoder.astype(f32),
        *up_a,
        *up_b,
        *up_c,
        *up_d,
        *up_e,
        head_peak,
        clip_factors,
    )


def solution(mesh):
    dp, mp = mesh.shape["dp"], mesh.shape["mp"]
    fine = Mesh(mesh.devices.reshape(dp // 2, 2, mp // 2, 2), ("dz", "dy", "mx", "mc"))
    dp_axes, mp_axes = ("dz", "dy"), ("mx", "mc")
    rows = P(None, (*dp_axes, *mp_axes), None)
    wide = P(None, dp_axes, mp_axes)
    tall = P(None, mp_axes, dp_axes)
    down = P(mp_axes, dp_axes)
    gain = P(None, dp_axes)
    state = (wide, tall, wide, down, gain)
    in_specs = (rows, rows, rows, P(), P(), *state, *state, *state)
    out_specs = (
        rows,
        rows,
        rows,
        *[wide] * 4,
        *[tall] * 4,
        *[wide] * 4,
        *[down] * 4,
        *[gain] * 4,
        P(mp_axes),
        P(mp_axes),
    )
    return jax.shard_map(
        on_device, mesh=fine, in_specs=in_specs, out_specs=out_specs, check_vma=False
    )
```

```python
import functools

import jax
import jax.numpy as jnp
from jax import lax
from jax.experimental import pallas as pl
from jax.experimental.layout import Layout, with_layout_constraint
from jax.experimental.pallas import tpu as pltpu
from jax.sharding import Mesh, PartitionSpec as P

D = 1024
DK = 64

epsilon = 1e-06
clip_limit = 10.0
momentum_rate = 0.9
learn_rate = 0.01
average_rate = 0.5
neg_large = -1e30
vmem_room = 24 << 20
tanh_rate = 0.7978845608
tanh_cube = 0.044715
bf16 = jnp.bfloat16
f32 = jnp.float32
swap = ((0, 1), (1, 0))
chips = ("dz", "dy", "mx")


def dot(left, right, dims):
    return lax.dot_general(left, right, (dims, ((), ())), preferred_element_type=f32)


def head_lanes(block, head):
    lanes = lax.broadcasted_iota(jnp.int32, block.shape, 1)
    return jnp.where((lanes >= DK) == (head == 1), block, jnp.zeros_like(block))


def key_spans(rows, keys, start, size, causal):
    half = rows // 2
    reach = start % half + size
    return [(0, reach), (half, half + reach)] if causal and reach < half else [(0, keys)]


def total(parts):
    return functools.reduce(jnp.add, parts)


def attend_kernel(causal, size, q_ref, k_ref, v_ref, pq_ref, pk_ref, len_ref, o_ref, lse_ref, top_ref):
    rows, keys = q_ref.shape[0], k_ref.shape[0]
    tops = []
    for head in range(2):
        k, v = head_lanes(k_ref[...], head), head_lanes(v_ref[...], head)
        top = jnp.full((1, 1), neg_large, f32)
        for start in range(0, rows, size):
            r = slice(start, start + size)
            spans = key_spans(rows, keys, start, size, causal)
            q = q_ref[r, :]
            s = [dot(q, k[a:b], ((1,), (1,))) for a, b in spans]
            if causal:
                s = [jnp.where(pk_ref[:, a:b] <= pq_ref[r, :], t, neg_large) for t, (a, b) in zip(s, spans)]
            m = functools.reduce(jnp.maximum, [jnp.max(t, axis=1, keepdims=True) for t in s])
            if causal:
                real = jnp.where(pq_ref[r, :] < len_ref[0], m, neg_large)
                top = jnp.maximum(top, jnp.max(real, axis=0, keepdims=True))
            e = [jnp.exp(t - m) for t in s]
            mass = total([jnp.sum(t, axis=1, keepdims=True) for t in e])
            scale = 1.0 / mass
            mix = total([dot((t * scale).astype(bf16), v[a:b], ((1,), (0,))) for t, (a, b) in zip(e, spans)])
            if head == 0:
                o_ref[r, :] = mix.astype(bf16)
            else:
                o_ref[r, :] = (o_ref[r, :].astype(f32) + mix).astype(bf16)
            lse_ref[0, r, head : head + 1] = m + jnp.log(mass)
        tops.append(top)
    lanes = lax.broadcasted_iota(jnp.int32, (8, 128), 1)
    top_ref[0] = jnp.where(lanes == 0, tops[0], tops[1])


def attend_back_kernel(
    causal, size, q_ref, k_ref, v_ref, pq_ref, pk_ref, lse_ref, do_ref, dq_ref, dk_ref, dv_ref, dk_acc, dv_acc
):
    rows, keys = q_ref.shape[0], k_ref.shape[0]
    dk_acc[...] = jnp.zeros_like(dk_acc)
    dv_acc[...] = jnp.zeros_like(dv_acc)
    for head in range(2):
        k, v = head_lanes(k_ref[...], head), head_lanes(v_ref[...], head)
        own = slice(DK * head, DK * head + DK)
        for start in range(0, rows, size):
            r = slice(start, start + size)
            spans = key_spans(rows, keys, start, size, causal)
            q, do, lse = q_ref[r, :], do_ref[r, :], lse_ref[0, r, head : head + 1]
            soft, grad = [], []
            for a, b in spans:
                s = dot(q, k[a:b], ((1,), (1,)))
                if causal:
                    s = jnp.where(pk_ref[:, a:b] <= pq_ref[r, :], s, neg_large)
                soft.append(jnp.exp(s - lse))
                grad.append(dot(do, v[a:b], ((1,), (1,))))
            row_dot = total([jnp.sum(p * t, axis=1, keepdims=True) for p, t in zip(soft, grad)])
            q_t, do_t = q.T[own], do.T[own]
            parts = []
            for (a, b), p, t in zip(spans, soft, grad):
                ds = (p * (t - row_dot)).astype(bf16)
                parts.append(dot(ds, k[a:b], ((1,), (0,))))
                dv_acc[own, a:b] += dot(do_t, p.astype(bf16), ((1,), (0,)))
                dk_acc[own, a:b] += dot(q_t, ds, ((1,), (0,)))
            dq = total(parts)
            if head == 0:
                dq_ref[r, :] = dq.astype(bf16)
            else:
                dq_ref[r, :] = (dq_ref[r, :].astype(f32) + dq).astype(bf16)
    dk_ref[...] = dk_acc[...].T.astype(bf16)
    dv_ref[...] = dv_acc[...].T.astype(bf16)


def attend_cost(rows, keys, pairs, dots):
    return cost(0, 0)


def lane_pairs(count, first):
    return pl.BlockSpec((count, 2 * DK), lambda p: (0, first + p))


def attend(q, k, v, pos_col, pos_row, length, causal, size):
    rows, keys, pairs = q[0].shape[0], k[0].shape[0], q[2]
    mixed, lse, top = pl.pallas_call(
        functools.partial(attend_kernel, causal, size),
        grid=(pairs,),
        in_specs=[
            lane_pairs(rows, q[1]),
            lane_pairs(keys, k[1]),
            lane_pairs(keys, v[1]),
            pl.BlockSpec((rows, 1), lambda p: (0, 0)),
            pl.BlockSpec((1, keys), lambda p: (0, 0)),
            pl.BlockSpec(memory_space=pltpu.SMEM),
        ],
        out_specs=[
            lane_pairs(rows, 0),
            pl.BlockSpec((1, rows, 2), lambda p: (p, 0, 0)),
            pl.BlockSpec((1, 8, 128), lambda p: (p, 0, 0)),
        ],
        out_shape=[
            jax.ShapeDtypeStruct((rows, pairs * 2 * DK), bf16),
            jax.ShapeDtypeStruct((pairs, rows, 2), f32),
            jax.ShapeDtypeStruct((pairs, 8, 128), f32),
        ],
        compiler_params=pltpu.CompilerParams(vmem_limit_bytes=vmem_room),
        cost_estimate=attend_cost(rows, keys, pairs, 2),
        name="attend",
    )(q[0], k[0], v[0], pos_col, pos_row, length)
    return mixed, lse, top[:, 0, :2].reshape(-1)


def attend_back(q, k, v, pos_col, pos_row, lse, grad, causal, size):
    rows, keys, pairs = q[0].shape[0], k[0].shape[0], q[2]
    return pl.pallas_call(
        functools.partial(attend_back_kernel, causal, size),
        grid=(pairs,),
        in_specs=[
            lane_pairs(rows, q[1]),
            lane_pairs(keys, k[1]),
            lane_pairs(keys, v[1]),
            pl.BlockSpec((rows, 1), lambda p: (0, 0)),
            pl.BlockSpec((1, keys), lambda p: (0, 0)),
            pl.BlockSpec((1, rows, 2), lambda p: (p, 0, 0)),
            lane_pairs(rows, 0),
        ],
        out_specs=[lane_pairs(rows, 0), lane_pairs(keys, 0), lane_pairs(keys, 0)],
        out_shape=[jax.ShapeDtypeStruct((n, pairs * 2 * DK), bf16) for n in (rows, keys, keys)],
        scratch_shapes=[pltpu.VMEM((2 * DK, keys), f32)] * 2,
        compiler_params=pltpu.CompilerParams(vmem_limit_bytes=vmem_room),
        cost_estimate=attend_cost(rows, keys, pairs, 5),
        name="attend_back",
    )(q[0], k[0], v[0], pos_col, pos_row, lse, grad)


def apply_update(weight, grad_sum, moment, average, factor, grad_scale):
    grad_now = grad_sum * grad_scale
    moment_new = momentum_rate * moment + grad_now
    master_new = (weight - learn_rate * (grad_now + momentum_rate * moment_new)) * factor
    average_new = average_rate * average + (1.0 - average_rate) * master_new
    return (grad_now, moment_new, average_new, master_new)


def flat_columns(block):
    return jnp.swapaxes(block, 0, 1).reshape(block.shape[1], -1)


def row_major(values):
    return with_layout_constraint(values, Layout(major_to_minor=tuple(range(values.ndim))))


spec = pl.BlockSpec


def cost(flops, moved):
    return pl.CostEstimate(flops=1, bytes_accessed=1, transcendentals=0)


def reorder(parts, block, dy, to_own, keep=None):
    arrays = halves(parts)
    rows, width = arrays[0].shape[0], D
    steps = width // block // 2
    extra = [] if keep is None else [keep]
    if block % 128:
        value = total([(jnp.concatenate(p, axis=1) if isinstance(p, (list, tuple)) else p).astype(f32) for p in parts])
        value = value * (1.0 if keep is None else keep)
        axis = 2 if to_own else 1
        value = value.reshape((rows, steps, 2, block) if to_own else (rows, 2, steps, block))
        low, high = (lax.index_in_dim(value, n, axis, keepdims=False) for n in range(2))
        pair = jnp.where(dy == 0, low, high), jnp.where(dy == 0, high, low)
        return jnp.stack(pair, axis=3 - axis).reshape(rows, width).astype(bf16)

    def source(j, flag):
        if to_own:
            return j % steps * 2 + (j // steps + flag) % 2
        return j // 2 + (j % 2 + flag) % 2 * steps

    def kernel(flag_ref, *refs):
        out = refs[-1]
        whole = len(arrays) == 1
        value = refs[0] if whole else read_total(parts, refs[: len(arrays)])
        for j in range(2 * steps):
            spans = [slice(source(j, flag) * block, (source(j, flag) + 1) * block) for flag in range(2)]
            picked = jnp.where(flag_ref[0] == 0, value[:, spans[0]], value[:, spans[1]])
            if extra:
                picked = picked.astype(f32) * refs[len(arrays)][...]
            out[:, j * block : (j + 1) * block] = picked.astype(bf16)

    return pl.pallas_call(
        kernel,
        grid=(4,),
        in_specs=[
            spec(memory_space=pltpu.SMEM),
            *[by_rows(p, rows // 4) for p in [*arrays, *extra]],
        ],
        out_specs=spec((rows // 4, width), lambda i: (i, 0)),
        out_shape=jax.ShapeDtypeStruct((rows, width), bf16),
        compiler_params=pltpu.CompilerParams(vmem_limit_bytes=vmem_room),
        cost_estimate=cost(0, rows * width * 4),
        name="reorder",
    )(dy[None], *arrays, *extra)


def weight_specs(weights):
    specs, arrays = [], []
    for own, other, width, *places in weights:
        for array, place in zip((own, other), (places[0], places[-1])):
            specs.append(spec((array.shape[0], width), lambda i, place=place: (0, place)))
            arrays.append(array)
    return specs, arrays


def project(rows, weights, mode="plain", scales=()):
    own, other = rows
    half, size = own.shape[0], own.shape[0] // 2
    specs, arrays = weight_specs(weights)
    widths = [w[2] for w in weights]
    count = len(weights)
    out_widths = {"plain": widths, "gelu": widths[:1] * 3, "scale": [w for w in widths for _ in range(2)]}[mode]

    def kernel(own_ref, other_ref, *refs):
        here = pl.program_id(0) < 2
        x = jnp.where(here, own_ref[...], other_ref[...])
        split = x.shape[1] // 2
        made = []
        for j in range(count):
            low, high = refs[2 * j], refs[2 * j + 1]
            made.append(
                dot(x[:, :split], low[...], ((1,), (0,))) + dot(x[:, split:], high[...], ((1,), (0,)))
            )
        outs = refs[2 * count + len(scales) :]
        if mode == "plain":
            for out, value in zip(outs, made):
                out[...] = value.astype(bf16)
        elif mode == "gelu":
            gate, up = made
            square = gate * gate
            bend = jnp.tanh(tanh_rate * gate * (1.0 + tanh_cube * square))
            rise = 0.5 * (1.0 + bend)
            value = gate * rise
            slope = rise + 0.5 * gate * (1.0 - bend * bend) * tanh_rate * (1.0 + 3.0 * tanh_cube * square)
            outs[0][...] = (value * up).astype(bf16)
            outs[1][...] = (slope * up).astype(bf16)
            outs[2][...] = value.astype(bf16)
        else:
            for j, out in enumerate(outs):
                out[...] = (made[j // 2] * refs[2 * count + j][...].astype(f32)).astype(bf16)

    by_rows = lambda width: spec((size, width), lambda i: (i, 0))
    width_all = own.shape[1]
    return pl.pallas_call(
        kernel,
        grid=(4,),
        in_specs=[
            spec((size, width_all), lambda i: (jnp.minimum(i, 1), 0)),
            spec((size, width_all), lambda i: (jnp.maximum(i - 2, 0), 0)),
            *specs,
            *[by_rows(t.shape[1]) for t in scales],
        ],
        out_specs=[by_rows(w) for w in out_widths],
        out_shape=[jax.ShapeDtypeStruct((2 * half, w), bf16) for w in out_widths],
        compiler_params=pltpu.CompilerParams(vmem_limit_bytes=vmem_room),
        cost_estimate=cost(4 * half * width_all * sum(widths), half * width_all * 4 + width_all * sum(widths) * 2),
        name="project_" + mode,
    )(own, other, *arrays, *scales)


def combine(values, weights, which):
    specs, arrays = weight_specs(weights)
    half = values[0].shape[0] // 2
    size = half // 2
    count = len(values)
    depth = weights[0][0].shape[0]

    def kernel(*refs):
        for side in range(2):
            parts = [
                dot(refs[j][...], refs[count + 2 * j + side][...], ((1,), (1,))) for j in range(count)
            ]
            refs[side - 2][...] = total(parts)

    return pl.pallas_call(
        kernel,
        grid=(2,),
        in_specs=[spec((size, v.shape[1]), lambda i: (2 * which + i, 0)) for v in values] + specs,
        out_specs=[spec((size, depth), lambda i: (i, 0))] * 2,
        out_shape=[jax.ShapeDtypeStruct((half, depth), f32)] * 2,
        compiler_params=pltpu.CompilerParams(vmem_limit_bytes=vmem_room),
        cost_estimate=cost(0, 0),
        name="combine",
    )(*values, *arrays)


def weight_grad(items, part, arrived=()):
    sources = []
    for rows, _ in items:
        if not any(rows is t for t in sources):
            sources.append(rows)
    half, width = sources[0][0].shape
    size = width // 2
    steps, base = (2, 0) if part is None else (1, part)
    spans, last = [], 0
    for _, value in items:
        spans.append((last, last + value.shape[1]))
        last = spans[-1][1]
    first = len(sources) * 2

    def kernel(*refs):
        out = refs[-1]
        for (rows, _), value, (a, b) in zip(items, refs[first:], spans):
            place = [rows is t for t in sources].index(True)
            own, other = refs[2 * place], refs[2 * place + 1]
            made = dot(own[...], value[:half], ((0,), (0,))) + dot(other[...], value[half:], ((0,), (0,)))
            for (array, _, start), came in zip(arrived, refs[first + len(items) :]):
                if start <= a < start + array.shape[1]:
                    made = made + came[:, a - start : b - start].astype(f32)
            out[:, a:b] = made.astype(bf16)

    columns = spec((half, size), lambda i: (0, base + i))
    return pl.pallas_call(
        kernel,
        grid=(steps,),
        in_specs=[columns] * first
        + [spec(v.shape, lambda i: (0, 0)) for _, v in items]
        + [spec((size, a.shape[1]), lambda i, place=place: (place + i, 0)) for a, place, _ in arrived],
        out_specs=spec((size, last), lambda i: (i, 0)),
        out_shape=jax.ShapeDtypeStruct((steps * size, last), bf16),
        compiler_params=pltpu.CompilerParams(vmem_limit_bytes=vmem_room),
        cost_estimate=cost(4 * half * steps * size * last, half * width * 4 + half * 4 * last),
        name="weight_grad",
    )(*[t for pair in sources for t in pair], *[v for _, v in items], *[a for a, _, _ in arrived])


def halves(parts):
    return [t for p in parts for t in (p if isinstance(p, (list, tuple)) else [p])]


def read_total(parts, refs):
    refs, read = list(refs), []
    for p in parts:
        if isinstance(p, (list, tuple)):
            read.append(jnp.concatenate([refs.pop(0)[...] for _ in p], axis=1))
        else:
            read.append(refs.pop(0)[...])
    return total([r.astype(f32) for r in read])


def by_rows(array, size=256):
    if array.shape[0] == 1:
        return spec(array.shape, lambda i: (0, 0))
    return spec((size, array.shape[1]), lambda i: (i, 0))


def add_norm(parts, gain_row):
    arrays = halves(parts)
    rows, width = arrays[0].shape[0], D

    def kernel(gain_ref, *refs):
        hidden = read_total(parts, refs[: len(arrays)])
        scale = lax.rsqrt(jnp.mean(hidden * hidden, axis=-1, keepdims=True) + epsilon)
        refs[-1][...] = (hidden * scale * gain_ref[...]).astype(bf16)
        if len(parts) > 1:
            refs[-2][...] = hidden

    kinds = [f32, bf16] if len(parts) > 1 else [bf16]
    shapes = [jax.ShapeDtypeStruct((rows, width), k) for k in kinds]
    return pl.pallas_call(
        kernel,
        grid=(rows // 256,),
        in_specs=[by_rows(gain_row), *[by_rows(p) for p in arrays]],
        out_specs=[by_rows(t) for t in shapes],
        out_shape=shapes,
        compiler_params=pltpu.CompilerParams(vmem_limit_bytes=vmem_room),
        cost_estimate=cost(rows * width * 8, rows * width * 14),
        name="add_norm",
    )(gain_row, *arrays)


def norm_back(hidden, gain_row, grads, base):
    rows, width = hidden.shape
    arrays = halves(grads)

    def kernel(gain_ref, hidden_ref, base_ref, *refs):
        grad = read_total(grads, refs[: len(arrays)])
        out, low, gain_grad = refs[len(arrays) :]
        hidden = hidden_ref[...].astype(f32)
        scale = lax.rsqrt(jnp.mean(hidden * hidden, axis=-1, keepdims=True) + epsilon)
        z = hidden * scale
        grad_z = grad * gain_ref[...]
        grad_hidden = scale * (grad_z - z * jnp.mean(grad_z * z, axis=-1, keepdims=True))
        value = base_ref[...].astype(f32) + grad_hidden
        out[...] = value
        low[...] = value.astype(bf16)

        @pl.when(pl.program_id(0) == 0)
        def _():
            gain_grad[...] = jnp.zeros_like(gain_grad)

        gain_grad[...] += jnp.sum(grad * z, axis=0, keepdims=True)

    shapes = [jax.ShapeDtypeStruct((rows, width), f32), jax.ShapeDtypeStruct((rows, width), bf16)]
    return pl.pallas_call(
        kernel,
        grid=(rows // 256,),
        in_specs=[by_rows(gain_row), by_rows(hidden), by_rows(base), *[by_rows(g) for g in arrays]],
        out_specs=[*[by_rows(t) for t in shapes], spec((1, width), lambda i: (0, 0))],
        out_shape=[*shapes, jax.ShapeDtypeStruct((1, width), f32)],
        compiler_params=pltpu.CompilerParams(vmem_limit_bytes=vmem_room),
        cost_estimate=cost(rows * width * 16, rows * width * 22),
        name="norm_back",
    )(gain_row, hidden, base, *arrays)


def after(value, *others):
    return lax.optimization_barrier((value, *others))[0]


def swap_cores(values):
    return lax.ppermute(values, "mc", swap)


def swap_x(values):
    return row_major(lax.ppermute(row_major(values), "mx", swap))


def swap_y(values):
    return row_major(lax.ppermute(row_major(values), "dy", swap))


def gather_part(local):
    return row_major(lax.all_gather(row_major(local), "dz", axis=0, tiled=True))


def spread(part, x_last):
    if x_last:
        high = swap_y(part)
        return (part, high), (swap_x(part), swap_x(high))
    beside = swap_x(part)
    return (part, swap_y(part)), (beside, swap_y(beside))


def pieces(value, count):
    made = []
    for _ in range(count):
        made.append(value.astype(bf16))
        value = value - made[-1].astype(f32)
    return made


class Group:
    def __init__(self, x_items, y_items):
        self.own = [(r, v) for r, v, _ in (*x_items, *y_items)]
        self.own_x, self.own_y = self.own[: len(x_items)], self.own[len(x_items) :]
        self.other_x, self.other_y = ([(r, v) for r, _, v in items] for items in (x_items, y_items))

    def first(self):
        self.sent = [weight_grad(self.other_x, None), weight_grad([*self.own_y, *self.other_y], 1)]
        return self.sent

    def send(self, *deps):
        to_x, to_y = (after(t, *deps) if deps else t for t in self.sent)
        self.from_x, self.from_y = swap_x(to_x), swap_y(to_y)

    def second(self, *deps):
        self.from_x, self.from_y = after(self.from_x, *deps), after(self.from_y, *deps)
        wide_y = self.from_y.shape[1] // 2
        self.sent = [
            weight_grad(self.own_x, 1, [(self.from_x, 1, 0)]),
            weight_grad(self.other_y, 0, [(self.from_y, 0, -wide_y)]),
        ]
        self.middle = self.sent
        self.late_y, self.late_x = swap_y(self.sent[0]), swap_x(self.sent[1])
        return self.sent

    def third(self, *deps, behind=()):
        wide_x = self.from_x.shape[1]
        late_y, late_x = after(self.late_y, *deps), after(self.late_x, *deps)
        summed = weight_grad(
            self.own, 0, [(self.from_x, 0, 0), (late_y, 0, 0), (self.from_y, 0, wide_x), (late_x, 0, wide_x)]
        )
        self.sent = [summed]
        summed = after(summed, *behind) if behind else summed
        self.low = lax.psum_scatter(row_major(summed), "dz", scatter_dimension=0, tiled=True)
        self.result = self.low.astype(f32)
        return self.sent


def on_device(
    tokens,
    encoder,
    cotangent,
    lengths,
    deal,
    attn_in,
    attn_out,
    ff_in,
    ff_out,
    gains,
    mom_attn_in,
    mom_attn_out,
    mom_ff_in,
    mom_ff_out,
    mom_gains,
    avg_attn_in,
    avg_attn_out,
    avg_ff_in,
    avg_ff_out,
    avg_gains,
):
    seq_count, block_rows = tokens.shape[0], tokens.shape[1]
    core = lax.axis_index("mc")
    dy = lax.axis_index("dy")
    chip = lax.axis_index(chips)
    own_rows = block_rows * seq_count
    slot_len = 2 * own_rows
    heads_cols = attn_in.shape[2]
    hidden = ff_in.shape[2]
    model_rows = attn_in.shape[1]

    def exchange(values):
        return lax.all_to_all(values, chips, split_axis=0, concat_axis=0, tiled=True)

    def to_chips(values):
        return exchange(values).reshape(own_rows, D)

    def from_chips(rows):
        return exchange(rows.reshape(seq_count, block_rows, D))

    seq_len = lengths[deal[chip]]
    row_ids = jnp.arange(own_rows, dtype=jnp.int32)
    lane = row_ids % block_rows
    pos_own = (row_ids // block_rows * 2 + core) * block_rows + lane
    pos_other = (row_ids // block_rows * 2 + 1 - core) * block_rows + lane
    pos = jnp.concatenate([pos_own, pos_other])
    places = (pos[:, None], pos[None, :])
    length = seq_len[None]
    valid_own = (pos_own < seq_len).astype(f32)[:, None]

    hc = heads_cols
    pairs = hc // (2 * DK)
    spare = -hidden % 256
    deep = hidden + spare
    widen = lambda t: jnp.pad(t.astype(bf16), ((0, 0), (0, spare)))
    out_t = jnp.swapaxes(attn_out.astype(bf16), 1, 2)
    low_in = attn_in.astype(bf16)
    pad = jnp.zeros((model_rows, 125), bf16)
    chunk_a = jnp.concatenate([*low_in[0:3], out_t[0], gains.astype(bf16).T, pad], axis=1)
    chunk_b = jnp.concatenate([*low_in[3:6], out_t[1]], axis=1)
    chunk_c = jnp.concatenate([widen(ff_in[0]), widen(ff_in[1]), widen(ff_out.T)], axis=1)

    part_a, part_b, part_c = (gather_part(t) for t in (chunk_a, chunk_b, chunk_c))
    got_a = spread(part_a, True)
    tok_own = to_chips(after(tokens, part_a))
    cot_own = to_chips(cotangent)

    gain_f = jnp.concatenate([g[:, 4 * hc : 4 * hc + 3] for g in got_a[0]]).astype(f32).T
    gain_rows = [gain_f[n : n + 1] for n in range(3)]
    w_qkv = [(*g, 3 * hc, 0) for g in got_a]
    w_q, w_k, w_v, w_ot = ([(*g, hc, n) for g in got_a] for n in range(4))

    def both(own):
        return own, swap_cores(own)

    def over_cores(values, weights):
        away = [swap_cores(t) for t in combine(values, weights, 1)]
        return combine(values, weights, 0), away

    x_own = reorder([after(tok_own, chunk_b, chunk_c)], model_rows, dy, True)
    norm_one = both(add_norm([x_own], gain_rows[0])[0])
    norm_one = after(norm_one[0], part_b), norm_one[1]
    qkv = [project(norm_one, [w_qkv[0]])[0]]
    self_qkv = [[(qkv[0], n * pairs, pairs) for n in range(3)]]
    self_out = [attend(*self_qkv[0], *places, length, True, 256)]
    qkv += project((after(norm_one[0], self_out[0][0]), norm_one[1]), [w_qkv[1]])
    self_qkv += [[(qkv[1], n * pairs, pairs) for n in range(3)]]
    high_b, beside_b = swap_y(part_b), swap_x(part_b)
    self_out += [attend(*self_qkv[1], *places, length, True, 256)]
    far_b = swap_y(after(beside_b, self_out[1][0], high_b))
    got_b = (part_b, high_b), (beside_b, far_b)
    w_cq, w_ck, w_cv, w_cot = ([(*g, hc, n) for g in got_b] for n in range(4))

    enc_own = to_chips(after(encoder, self_out[0][0]))
    part_c = after(part_c, self_out[1][0], far_b)
    high_c, beside_c = swap_y(part_c), swap_x(part_c)
    far_gu, far_d = swap_x(high_c[:, : 2 * deep]), swap_y(beside_c[:, 2 * deep :])
    w_g, w_u, w_dt = (
        [(part_c, high_c, deep, n), (beside_c, far, deep, n, place)]
        for n, far, place in ((0, far_gu, 0), (1, far_gu, 1), (2, far_d, 0))
    )

    self_mixed = [o[0] for o in self_out]
    hidden_one, norm_two = add_norm([x_own, *over_cores(self_mixed, w_ot)], gain_rows[1])
    norm_two = both(norm_two)
    e_own = reorder([enc_own], model_rows, dy, True)
    enc_rows = both(e_own)
    cross_kv = project(enc_rows, [*w_ck, *w_cv])
    cross_q = project(norm_two, w_cq)
    cross_qkv = [
        [(t, 0, pairs) for t in (cross_q[n], cross_kv[n], cross_kv[2 + n])] for n in range(2)
    ]
    cross_qkv[0][0] = (after(cross_q[0], cross_q[1], high_c, beside_c), 0, pairs)
    cross_out = [attend(*t, *places, length, False, 1024) for t in cross_qkv]
    cross_mixed = [o[0] for o in cross_out]
    hidden_two, norm_three = add_norm(
        [hidden_one, *over_cores(cross_mixed, w_cot)], gain_rows[2]
    )
    norm_three = both(norm_three)
    dy_own = reorder([cot_own], model_rows, dy, True, valid_own)
    grad_out = both(dy_own)
    inner, slope, value = zip(*[project(norm_three, list(w), "gelu") for w in zip(w_g, w_u)])

    scales = [t for pair in zip(slope, value) for t in pair]
    grad_gu = project(grad_out, w_dt, "scale", scales)
    grad_gate, grad_up = grad_gu[::2], grad_gu[1::2]
    group_c = Group([(norm_three, *grad_gate), (grad_out, *inner)], [(norm_three, *grad_up)])
    sent = group_c.first()
    group_c.send()
    parts = over_cores([after(grad_gate[0], *sent), grad_gate[1], *grad_up], [*w_g, *w_u])
    grad_two, low_two, gain_three = norm_back(hidden_two, gain_rows[2], parts, dy_own)
    grad_co = both(low_two)
    out_parts = over_cores([after(inner[0], low_two), inner[1]], w_dt)
    grad_ca = project((after(grad_co[0], out_parts[0][0]), grad_co[1]), w_cot)
    out_block = reorder([after(hidden_two, *grad_ca), *out_parts], model_rows, dy, False, valid_own)
    block_output = from_chips(out_block)
    cross_back = [attend_back(*cross_qkv[0], *places, cross_out[0][1], after(grad_ca[0], out_block), False, 1024)]
    grad_late = after(grad_ca[1], group_c.from_y, *cross_back[0])
    cross_back += [attend_back(*cross_qkv[1], *places, cross_out[1][1], grad_late, False, 1024)]
    grad_cq, grad_ck, grad_cv = zip(*cross_back)
    sent = group_c.second(*grad_cq)
    grad_cq = (after(grad_cq[0], *sent), grad_cq[1])
    group_b = Group(
        [(norm_two, *grad_cq), (grad_co, *[o[0] for o in cross_out])],
        [(enc_rows, *grad_ck), (enc_rows, *grad_cv)],
    )
    parts = over_cores(grad_cq, w_cq)
    sent = group_b.first()
    group_b.send()
    parts_enc = over_cores([after(grad_ck[0], *sent), grad_ck[1], *grad_cv], [*w_ck, *w_cv])
    grad_one, low_one, gain_two = norm_back(
        hidden_one, gain_rows[1], [parts[0], [after(parts[1][0], parts_enc[0][0]), parts[1][1]]], grad_two
    )
    grad_o = both(low_one)
    out_enc = reorder([parts_enc[0], [after(parts_enc[1][0], low_one), parts_enc[1][1]]], model_rows, dy, False)
    grad_encoder = from_chips(out_enc)
    grad_a = project((after(grad_o[0], out_enc, block_output), grad_o[1]), w_ot)
    self_back = [attend_back(*self_qkv[0], *places, self_out[0][1], grad_a[0], True, 256)]
    sent = group_c.third(*self_back[0])
    self_back.append(attend_back(*self_qkv[1], *places, self_out[1][1], after(grad_a[1], *sent), True, 256))
    grad_q, grad_k, grad_v = zip(*self_back)
    group_a = Group(
        [(norm_one, *grad_q), (grad_o, *[o[0] for o in self_out])],
        [(norm_one, *grad_k), (norm_one, *grad_v)],
    )
    sent = group_a.first()
    parts = over_cores(
        [after(grad_q[0], *sent), grad_q[1], *grad_k, *grad_v], [*w_q, *w_k, *w_v]
    )
    group_b.second(*parts[0])
    group_a.send(group_b.late_x, group_b.late_y)
    sent = group_b.third(behind=[group_c.low])
    _, low_tok, gain_one = norm_back(
        x_own, gain_rows[0], [[after(parts[0][0], *sent), parts[0][1]], parts[1]], grad_one
    )
    out_tok = reorder([after(low_tok, grad_encoder)], model_rows, dy, False)
    group_a.second(low_tok, group_c.low)
    group_a.third(behind=[group_b.low])
    dp_count = seq_count // 2
    gain_part = jnp.concatenate([gain_one, gain_two, gain_three])
    parts = [gain_part[:, n * D // 2 : (n + 1) * D // 2].reshape(3, dp_count // 2, model_rows) for n in range(2)]
    gain_part = jnp.stack([jnp.where(dy == 0, *parts), jnp.where(dy == 0, *parts[::-1])], axis=2)
    gain_part = jnp.swapaxes(gain_part.reshape(3, dp_count, model_rows), 0, 1).reshape(dp_count, -1)
    mx = lax.axis_index("mx")
    tops = jnp.stack([jnp.where(mx == n, self_out[0][2], self_out[1][2]) for n in range(2)])
    tops = jnp.broadcast_to(tops[None], (dp_count, *tops.shape)).reshape(seq_count, -1)
    small = jnp.concatenate([*pieces(jnp.repeat(gain_part, 2, axis=0), 2), *pieces(tops, 3)], axis=1)
    small = jnp.pad(small, ((0, 0), (0, D - small.shape[1])))[:, None]
    sent = jnp.concatenate([out_tok.reshape(seq_count, block_rows, D), small], axis=1)
    came = exchange(after(sent, *group_a.middle))
    grad_tokens, small = came[:, :block_rows], came[:, block_rows].astype(f32)
    group_a.third(out_tok, behind=[group_b.low])
    sum_a, sum_b, sum_c = group_a.result, group_b.result, group_c.result

    small = after(small, group_a.low)
    wide = 3 * model_rows
    red_gain = jnp.sum(small[:, :wide] + small[:, wide : 2 * wide], axis=0).reshape(3, model_rows)
    red_gain = red_gain + swap_cores(red_gain)
    tops = small[:, 2 * wide : 2 * wide + 3 * (hc // DK)].reshape(seq_count, 3, -1)
    head_peak = jnp.max(tops[:, 0] + tops[:, 1] + tops[:, 2], axis=0)

    cut = lambda t, n: t[:, n * hc : (n + 1) * hc]
    red_in = jnp.stack([cut(t, n) for t in (sum_a, sum_b) for n in (0, 2, 3)])
    red_out = jnp.stack([cut(sum_a, 1).T, cut(sum_b, 1).T])
    red_ff = jnp.stack([sum_c[:, n * deep : n * deep + hidden] for n in (0, 2)])
    red_in = row_major(red_in)
    red_out = with_layout_constraint(red_out, Layout(major_to_minor=(0, 1, 2)))
    red_ff = with_layout_constraint(red_ff, Layout(major_to_minor=(0, 2, 1)))
    red_down = with_layout_constraint(sum_c[:, deep : deep + hidden].T, Layout(major_to_minor=(0, 1)))
    clip_factors = clip_limit / jnp.maximum(head_peak, clip_limit)
    column = jnp.repeat(jnp.sqrt(clip_factors), DK)
    factor = jnp.where((jnp.arange(6) < 2)[:, None, None], column[None, None, :], 1.0)
    grad_scale = float(seq_count * slot_len) ** (-0.5)
    up_a = apply_update(attn_in, red_in, mom_attn_in, avg_attn_in, factor, grad_scale)
    up_b = apply_update(attn_out, red_out, mom_attn_out, avg_attn_out, 1.0, grad_scale)
    up_c = apply_update(ff_in, red_ff, mom_ff_in, avg_ff_in, 1.0, grad_scale)
    up_d = apply_update(ff_out, red_down, mom_ff_out, avg_ff_out, 1.0, grad_scale)
    up_e = apply_update(gains, red_gain, mom_gains, avg_gains, 1.0, grad_scale)
    return (
        block_output.astype(f32),
        grad_tokens.astype(f32),
        grad_encoder.astype(f32),
        *up_a,
        *up_b,
        *up_c,
        *up_d,
        *up_e,
        head_peak,
        clip_factors,
    )


def solution(mesh):
    dp, mp = mesh.shape["dp"], mesh.shape["mp"]
    fine = Mesh(mesh.devices.reshape(dp // 2, 2, mp // 2, 2), ("dz", "dy", "mx", "mc"))
    dp_axes, mp_axes = ("dz", "dy"), ("mx", "mc")
    rows = P(None, (*dp_axes, *mp_axes), None)
    wide = P(None, dp_axes, mp_axes)
    tall = P(None, mp_axes, dp_axes)
    down = P(mp_axes, dp_axes)
    gain = P(None, dp_axes)
    state = (wide, tall, wide, down, gain)
    in_specs = (rows, rows, rows, P(), P(), *state, *state, *state)
    out_specs = (
        rows,
        rows,
        rows,
        *[wide] * 4,
        *[tall] * 4,
        *[wide] * 4,
        *[down] * 4,
        *[gain] * 4,
        P(mp_axes),
        P(mp_axes),
    )
    return jax.shard_map(
        on_device, mesh=fine, in_specs=in_specs, out_specs=out_specs, check_vma=False
    )
```
